32 devices in a mesh: lat: 4 (over x, core), lon: 8 (over z, y).
Axes of the slice: x: 2, y: 2, z: 4, core: 2. Of those that a mesh axis runs over, the one named last changes fastest.
Arguments:
- atmosphere_inputs: bfloat16 [9, 512, 1024], P(None, 'lat', 'lon'), may hold values from -6 to 6
- thermal_anomaly: float32 [64, 131072], P(None, ('lat', 'lon')), may hold values from -6 to 6
- mixing_rates: float32 [64, 131072], P(None, ('lat', 'lon')), may hold values from 0.1 to 10
- adjacency_table: int32 [6, 131072], P(None, ('lat', 'lon')), may hold values from 0 to 4351
- lateral_spread_factor: float32 [6, 131072], P(None, ('lat', 'lon')), may hold values from 0.02 to 0.15
- sent_vertices: int32 [256, 32], P(('lat', 'lon')), may hold values from 0 to 4095
- corner_parallel: int32 [4, 131072], P(None, ('lat', 'lon')), may hold values from 0 to 127, as said below
- corner_longitude: int32 [4, 131072], P(None, ('lat', 'lon')), may hold values from 0 to 1023, as said below
- corner_share: float32 [4, 131072], P(None, ('lat', 'lon')), as said below
- exchange_factor: float32 [9], replicated, may hold values from -3 to 3
- sensitivity_vector: float32 [64, 131072], P(None, ('lat', 'lon')), may hold values from -6 to 6
Outputs:
- updated_warmth: float32 [64, 131072], P(None, ('lat', 'lon'))
- temp_grad: float32 [64, 131072], P(None, ('lat', 'lon'))
- forcing_grad: float32 [9, 512, 1024], P(None, 'lat', 'lon')
The draws below stay inside these ranges and needn't reach their ends.
Inputs may be any that keep to these rules, and one draw needn't show every extreme that they name: `adjacency_table`: entries below 4096 are the partition's own nodes; entry 4096 + c * 32 + h is the h-th halo node received from the c-th partition of its group. `sent_vertices`: row p * 8 + c lists local nodes of partition p sent to the c-th partition of its group. `corner_parallel`: the four stencil points of a node are rows r, r + 1, r, r + 1 of its latitude band. `corner_longitude`: the four stencil points of a node are columns c, c, c + 1, c + 1 taken modulo 1024; for a partition of lon index b all of them lie in the 256 columns from b * 128 - 128 / 2 on, taken modulo 1024, and both ends of that window are named by some node of every partition. `corner_share`: products (1 - u)(1 - v), u (1 - v), (1 - u) v, u v of the node's row fraction u and column fraction v.
All inputs are finite; a program needn't handle non-finite values.
Results may differ from the reference program's by a relative error of at most 0.00055.
Values may be sent and summed in bfloat16 or wider, within the bound.
A program may use at most 128 MiB of HBM per device.

```python
import math
import jax
import jax.numpy as jnp
from jax import lax

FIELDS = 9
TILE = 128
DEPTH_LAYERS = 64
NEIGH = 6
NODES_DEV = 4096
HALO = 32
NLAT = 512
NLON = 1024
MESH_VERTICES = 131072
N_LAT = 4
N_LON = 8
DEVICES = 32


def stencil_base(key):
    key_col, key_row = jax.random.split(jax.random.fold_in(key, 7))
    node = jnp.arange(MESH_VERTICES).astype(jnp.int32)
    local = node % NODES_DEV
    owner = node // NODES_DEV
    offset = jax.random.randint(key_col, (MESH_VERTICES,), 0, 2 * TILE - 1).astype(jnp.int32)
    offset = jnp.where(local == 0, 0, jnp.where(local == 1, 2 * TILE - 2, offset))
    base_col = (owner % N_LON * TILE - TILE // 2 + offset) % NLON
    base_row = jax.random.randint(key_row, (MESH_VERTICES,), 0, TILE - 1).astype(jnp.int32)
    base_row = jnp.where(local == 0, 0, jnp.where(local == 1, TILE - 2, base_row))
    return (base_row.astype(jnp.int32), base_col.astype(jnp.int32))


def draw_corner_parallel(key, part):
    base_row, base_col = stencil_base(key)
    return jnp.stack([base_row, base_row + 1, base_row, base_row + 1], 0).astype(jnp.int32)


def draw_corner_longitude(key, part):
    base_row, base_col = stencil_base(key)
    next_col = (base_col + 1) % NLON
    return jnp.stack([base_col, base_col, next_col, next_col], 0).astype(jnp.int32)


def draw_corner_share(key, part):
    key_u, key_v = jax.random.split(jax.random.fold_in(key, 11))
    frac_u = jax.random.uniform(key_u, (MESH_VERTICES,), jnp.float32)
    frac_v = jax.random.uniform(key_v, (MESH_VERTICES,), jnp.float32)
    return jnp.stack([(1.0 - frac_u) * (1.0 - frac_v), frac_u * (1.0 - frac_v), (1.0 - frac_u) * frac_v, frac_u * frac_v], 0).astype(jnp.float32)


def set_ends(values, stream_key, least, top_value):
    longest = values.shape.index(max(values.shape))
    spots = []
    for shift in (0, 1):
        where = [jax.random.randint(jax.random.fold_in(stream_key, axis), (), 0, length) for axis, length in enumerate(values.shape)]
        where[longest] = (where[longest] + shift) % values.shape[longest]
        spots.append(tuple(where))
    return values.at[spots[0]].set(least).at[spots[1]].set(top_value)


def block_scale(own_key, dims, cuts, smallest, top_value):
    factor_of = 1.0
    for axis_at, parts in cuts:
        draws = jax.random.uniform(jax.random.fold_in(jax.random.fold_in(own_key, 6), axis_at), (parts,), jnp.float32, smallest / len(cuts), top_value / len(cuts))
        factor_of = factor_of * jnp.repeat(jnp.exp(draws), dims[axis_at] // parts).reshape((-1,) + (1,) * (len(dims) - 1 - axis_at))
    return factor_of


def centred(rng, dims, deviation, most, pieces=(), dtype=jnp.bfloat16):
    gain = block_scale(rng, dims, pieces, -0.22, 0.18) if pieces else 1.0
    array = jax.random.normal(rng, dims, jnp.float32) * deviation * gain
    return jnp.minimum(jnp.maximum(array, -most), most).astype(dtype)


def setup_inputs(seed: int = 0) -> dict:
    keys = jax.random.split(jax.random.key(seed), 12)
    return {
        "atmosphere_inputs": centred(keys[0], (FIELDS, NLAT, NLON), 1.0, 6.0, ((1, 4), (2, 8))),
        "thermal_anomaly": centred(keys[1], (DEPTH_LAYERS, MESH_VERTICES), 1.0, 6.0, ((1, 32),), jnp.float32),
        "mixing_rates": jnp.clip(jnp.exp(math.log(10.0) - 4.6051702 * jax.random.uniform(keys[2], (DEPTH_LAYERS, MESH_VERTICES), jnp.float32) ** block_scale(keys[2], (DEPTH_LAYERS, MESH_VERTICES), ((1, 32),), -0.2, 0.2)), 0.1, 10.0),
        "adjacency_table": set_ends(jax.random.randint(keys[3], (NEIGH, MESH_VERTICES), 0, NODES_DEV + N_LON * HALO), jax.random.fold_in(keys[3], 1), 0, (NODES_DEV + N_LON * HALO) - 1).astype(jnp.int32),
        "lateral_spread_factor": jnp.clip(0.02 + 0.13000001 * jax.random.uniform(keys[4], (NEIGH, MESH_VERTICES), jnp.float32) ** block_scale(keys[4], (NEIGH, MESH_VERTICES), ((1, 32),), -0.2, 0.2), 0.02, 0.15),
        "sent_vertices": set_ends(jax.random.randint(keys[5], (DEVICES * N_LON, HALO), 0, NODES_DEV), jax.random.fold_in(keys[5], 1), 0, NODES_DEV - 1).astype(jnp.int32),
        "corner_parallel": draw_corner_parallel(jax.random.fold_in(keys[11], 71), 0),
        "corner_longitude": draw_corner_longitude(jax.random.fold_in(keys[11], 71), 0),
        "corner_share": draw_corner_share(jax.random.fold_in(keys[11], 71), 0),
        "exchange_factor": centred(keys[9], (FIELDS,), 0.5, 3.0, (), jnp.float32),
        "sensitivity_vector": centred(keys[10], (DEPTH_LAYERS, MESH_VERTICES), 1.0, 6.0, ((1, 32),), jnp.float32),
    }


def column_solve(mixing_rates, source_vector):
    zero_row = jnp.zeros_like(mixing_rates[:1])
    prev_k = jnp.concatenate([zero_row, mixing_rates[:-1]], 0)
    above_k = jnp.concatenate([-mixing_rates[:-1], zero_row], 0)
    diagonal = 1.0 + prev_k + mixing_rates

    def sweep_down(carry, level_items):
        c_prev, d_prev = carry
        below_row, diag_row, above_row, rhs_row = level_items
        pivot = diag_row - below_row * c_prev
        c_next = above_row / pivot
        d_next = (rhs_row - below_row * d_prev) / pivot
        return ((c_next, d_next), (c_next, d_next))
    start = (jnp.zeros_like(mixing_rates[0]), jnp.zeros_like(mixing_rates[0]))
    _, (c_all, d_all) = lax.scan(sweep_down, start, (-prev_k, diagonal, above_k, source_vector))

    def sweep_up(x_next, level_items):
        c_row, d_row = level_items
        x_row = d_row - c_row * x_next
        return (x_row, x_row)
    _, solved = lax.scan(sweep_up, jnp.zeros_like(mixing_rates[0]), (c_all, d_all), reverse=True)
    return solved

def inner_portion(parallel_band, thermal_anomaly, extended_vertices, mixing_rates, adjacency_table, lateral_spread_factor, corner_position, corner_share, exchange_factor, sensitivity_vector):
    fields = parallel_band.shape[0]
    vertex_total = thermal_anomaly.shape[1]
    points = jnp.take(parallel_band, corner_position.reshape(-1), axis=1).astype(jnp.float32).reshape(fields, 4, vertex_total)
    driven_profile = lax.optimization_barrier(jnp.sum(points * corner_share[None], 1))
    breeze_drive = jnp.sqrt(driven_profile[0] * driven_profile[0] + driven_profile[1] * driven_profile[1] + 1.0)
    boundary_transfer = lax.optimization_barrier(jnp.sum(exchange_factor[:, None] * driven_profile, 0)) + 0.1 * breeze_drive * (driven_profile[2] - thermal_anomaly[0])
    gathered_entries = jnp.take(extended_vertices, adjacency_table, axis=1)
    source_vector = thermal_anomaly + lax.optimization_barrier(jnp.sum(lateral_spread_factor[None] * (gathered_entries - thermal_anomaly[:, None, :]), 1))
    source_vector = source_vector.at[0].add(boundary_transfer)
    updated_warmth = column_solve(mixing_rates, source_vector)
    adjoint = column_solve(mixing_rates, sensitivity_vector)
    surface = adjoint[0]
    spread = lateral_spread_factor[None] * adjoint[:, None, :]
    ext_grad = jnp.zeros_like(extended_vertices).at[:, adjacency_table].add(spread)
    temp_grad = adjoint * (1.0 - lax.optimization_barrier(jnp.sum(lateral_spread_factor, 0)))[None] + ext_grad[:, :vertex_total]
    temp_grad = temp_grad.at[0].add(-0.1 * surface * breeze_drive)
    excess_quantity = 0.1 * (driven_profile[2] - thermal_anomaly[0]) / breeze_drive
    node_grad = surface[None] * exchange_factor[:, None]
    node_grad = node_grad.at[0].add(surface * excess_quantity * driven_profile[0])
    node_grad = node_grad.at[1].add(surface * excess_quantity * driven_profile[1])
    node_grad = node_grad.at[2].add(surface * 0.1 * breeze_drive)
    entries_list = (node_grad[:, None, :] * corner_share[None]).reshape(fields, 4 * vertex_total)
    return (updated_warmth, temp_grad, ext_grad[:, vertex_total:], entries_list)

def reference(atmosphere_inputs, thermal_anomaly, mixing_rates, adjacency_table, lateral_spread_factor, sent_vertices, corner_parallel, corner_longitude, corner_share, exchange_factor, sensitivity_vector):

    def split_pieces(whole):
        return whole.reshape(whole.shape[0], DEVICES, NODES_DEV).transpose(1, 0, 2)
    corner_position = (corner_parallel * NLON + corner_longitude).astype(jnp.int32)
    thermal_portion = split_pieces(thermal_anomaly)
    sequences = sent_vertices.reshape(DEVICES, N_LON, HALO)
    departing_border = jax.vmap(lambda quantity_layer, matrix_lines: jnp.take(quantity_layer, matrix_lines, axis=1))(thermal_portion, sequences)
    received_border = departing_border.reshape(N_LAT, N_LON, DEPTH_LAYERS, N_LON, HALO).transpose(0, 3, 2, 1, 4).reshape(DEVICES, DEPTH_LAYERS, N_LON * HALO)
    extended_vertices = jnp.concatenate([thermal_portion, received_border], 2)
    bands = atmosphere_inputs.reshape(FIELDS, N_LAT, TILE, NLON).transpose(1, 0, 2, 3).reshape(N_LAT, FIELDS, TILE * NLON)
    processor_labels = jnp.arange(DEVICES).astype(jnp.int32)

    def single_processor(items):
        ident, temp_one, ext_one, kv_one, nbr_one, coef_one, idx_one, wgt_one, cot_one = items
        parallel_band = bands[ident // N_LON]
        return inner_portion(parallel_band, temp_one, ext_one, kv_one, nbr_one, coef_one, idx_one, wgt_one, exchange_factor, cot_one)
    updated_warmth, owned_derivative, border_derivative, entries_list = lax.map(single_processor, (processor_labels, thermal_portion, extended_vertices, split_pieces(mixing_rates), split_pieces(adjacency_table), split_pieces(lateral_spread_factor), split_pieces(corner_position), split_pieces(corner_share), split_pieces(sensitivity_vector)))
    back = border_derivative.reshape(N_LAT, N_LON, DEPTH_LAYERS, N_LON, HALO).transpose(0, 3, 2, 1, 4).reshape(DEVICES, DEPTH_LAYERS, N_LON, HALO)
    temp_grad = jax.vmap(lambda grad_one, matrix_lines, back_one: grad_one.at[:, matrix_lines].add(back_one))(owned_derivative, sequences, back)
    flat_index = split_pieces(corner_position).reshape(N_LAT, N_LON * 4 * NODES_DEV)
    band_values = entries_list.reshape(N_LAT, N_LON, FIELDS, 4 * NODES_DEV).transpose(0, 2, 1, 3).reshape(N_LAT, FIELDS, N_LON * 4 * NODES_DEV)
    band_grad = jax.vmap(lambda index_row, value_rows: jnp.zeros((FIELDS, TILE * NLON), jnp.float32).at[:, index_row].add(value_rows))(flat_index, band_values)
    forcing_grad = band_grad.reshape(N_LAT, FIELDS, TILE, NLON).transpose(1, 0, 2, 3).reshape(FIELDS, NLAT, NLON)

    def join(per_device):
        return per_device.transpose(1, 0, 2).reshape(DEPTH_LAYERS, MESH_VERTICES)
    return (join(updated_warmth), join(temp_grad), forcing_grad)
```

```python
import functools

import jax
import jax.numpy as jnp
from jax import lax
from jax.experimental import pallas as pl
from jax.experimental.pallas import tpu as pltpu
from jax.sharding import PartitionSpec as P

F32 = jnp.float32
BF16 = jnp.bfloat16
MEBI = 1024 * 1024
LANES = 128
SLOT_ROWS = 256
NODE_TILE = 256
FORCE_TILE = 512
LANE_CONTRACT = (((1,), (1,)), ((), ()))
MESH = pl.DeviceIdType.MESH


def whole(count):
    return [pl.BlockSpec(memory_space=pltpu.VMEM)] * count


def halves(value):
    high = value.astype(BF16)
    return high, (value - high.astype(F32)).astype(BF16)


def spread_levels(source_ref, dense_ref):
    layers = dense_ref.shape[0]
    for level in range(0, layers, 8):
        dense_ref[level : level + 8] = source_ref[level : level + 8, :].reshape(
            (8,) + dense_ref.shape[1:]
        )


def sweep_up(x_ref, gain_ref, zero):
    layers = x_ref.shape[0]

    def up(step, x_next):
        level = layers - 1 - step
        x_here = x_ref[level] + gain_ref[level] * x_next
        x_ref[level] = x_here
        return x_here

    lax.fori_loop(0, layers, up, zero, unroll=8)


def best_scale(values, count):
    trial = lax.broadcasted_iota(jnp.int32, (count, values[0].shape[1]), 0).astype(F32)
    trial = 1.0 + trial * (1.0 / count)
    inverse = 1.0 / trial
    miss = jnp.zeros_like(trial)
    for value in values:
        gap = (value * inverse).astype(BF16).astype(F32) * trial - value
        miss = miss + gap * gap
    least = jnp.min(miss, axis=0, keepdims=True)
    return jnp.max(jnp.where(miss == least, trial, 1.0), axis=0, keepdims=True)


def slot_weights(adj_ref, merged_ref, cols, first_row):
    row = lax.broadcasted_iota(jnp.int32, (SLOT_ROWS, NODE_TILE), 0).astype(F32).astype(BF16)
    local = (adj_ref[:, cols] - first_row).astype(F32).astype(BF16)
    share = merged_ref[:, cols].astype(BF16)
    weights = jnp.zeros((SLOT_ROWS, NODE_TILE), BF16)
    for k in range(adj_ref.shape[0]):
        weights = jnp.where(row == local[k : k + 1, :], share[k : k + 1, :], weights)
    return weights


def chosen_rows(sent_ref, part, nodes, first_node):
    halo = sent_ref.shape[1]
    padded = jnp.concatenate(
        [sent_ref[...].astype(F32), jnp.zeros((sent_ref.shape[0], LANES - halo), F32)], 1
    )
    column = padded.T[:halo, part : part + 1] - first_node
    node_at = lax.broadcasted_iota(jnp.int32, (halo, nodes), 1).astype(F32)
    return jnp.where(column == node_at, 1.0, 0.0).astype(BF16)


def exchange_kernel(
    mix_ref,
    sens_ref,
    thermal_ref,
    adj_ref,
    coef_ref,
    sent_ref,
    atm_ref,
    scaled_ref,
    xkeep_ref,
    surface_ref,
    gain_ref,
    scale_ref,
    carry_ref,
    merged_ref,
    node_scale_ref,
    received_ref,
    back_ref,
    other_ref,
    mix3_ref,
    x_ref,
    depart_buf,
    received_buf,
    hgrad_buf,
    back_buf,
    right_buf,
    left_buf,
    from_left_buf,
    from_right_buf,
    send_sem,
    recv_sem,
    gsend_sem,
    grecv_sem,
    rim_sem,
):
    layers, nodes = mix_ref.shape
    slots = adj_ref.shape[0]
    parts, each = sent_ref.shape
    halo = parts * each
    fields, tile_rows, tile_cols = atm_ref.shape
    mid = tile_rows // 2
    me = lax.axis_index("lon")
    ahead = lax.rem(me + 1, parts)
    behind = lax.rem(me + parts - 1, parts)

    barrier = pltpu.get_barrier_semaphore()
    for off in range(1, parts):
        pl.semaphore_signal(
            barrier, inc=1, device_id={"lon": lax.rem(me + off, parts)}, device_id_type=MESH
        )

    low_lane = lax.broadcasted_iota(jnp.int32, (mid, tile_cols), 1) < tile_cols // 2
    for f in range(fields):
        upper = atm_ref[f, :mid, :].astype(F32)
        lower = pltpu.roll(atm_ref[f, mid:, :].astype(F32), tile_cols // 2, 1)
        right_buf[f] = jnp.where(low_lane, lower, upper).astype(BF16)
        left_buf[f] = jnp.where(low_lane, upper, lower).astype(BF16)

    pl.semaphore_wait(barrier, parts - 1)

    def rim_copy(source, target, index, to):
        return pltpu.make_async_remote_copy(
            src_ref=source,
            dst_ref=target,
            send_sem=rim_sem.at[index],
            recv_sem=rim_sem.at[2 + index],
            device_id={"lon": to},
            device_id_type=MESH,
        )

    rims = [
        rim_copy(right_buf, from_left_buf, 0, ahead),
        rim_copy(left_buf, from_right_buf, 1, behind),
    ]
    for copy in rims:
        copy.start()

    depart = jnp.zeros((halo, 2 * layers), F32)
    tile = 1024

    def pick(step, total):
        cols = pl.ds(pl.multiple_of(step * tile, tile), tile)
        high, low = halves(thermal_ref[:, cols])
        ext = jnp.concatenate([high, low], 0)
        first = (step * tile).astype(F32)
        chosen = jnp.concatenate(
            [chosen_rows(sent_ref, c, tile, first) for c in range(parts)], 0
        )
        return total + lax.dot_general(
            chosen, ext, LANE_CONTRACT, preferred_element_type=F32
        )

    depart = lax.fori_loop(0, nodes // tile, pick, depart)
    depart_buf[...] = depart.astype(BF16)

    def rows_of(part):
        return pl.ds(pl.multiple_of(part * each, each), each)

    def halo_copies(source, target, sends, recvs):
        copies = []
        for off in range(1, parts):
            peer = lax.rem(me + off, parts)
            copies.append(
                pltpu.make_async_remote_copy(
                    src_ref=source.at[rows_of(peer)],
                    dst_ref=target.at[rows_of(me)],
                    send_sem=sends.at[off],
                    recv_sem=recvs.at[off],
                    device_id={"lon": peer},
                    device_id_type=MESH,
                )
            )
        return copies

    def own_copy(source, target, sem):
        return pltpu.make_async_copy(source.at[rows_of(me)], target.at[rows_of(me)], sem)

    there = halo_copies(depart_buf, received_buf, send_sem, recv_sem)
    for copy in there:
        copy.start()
    mine = own_copy(depart_buf, received_buf, send_sem.at[0])
    mine.start()

    for k in range(slots):
        same = coef_ref[k : k + 1, :]
        for m in range(slots):
            if m != k:
                equal = adj_ref[k : k + 1, :] == adj_ref[m : m + 1, :]
                same = same + jnp.where(equal, coef_ref[m : m + 1, :], 0.0)
        merged_ref[k : k + 1, :] = same

    def fit(step, carry):
        cols = pl.ds(pl.multiple_of(step * NODE_TILE, NODE_TILE), NODE_TILE)
        merged = [merged_ref[k : k + 1, cols] for k in range(slots)]
        scale = best_scale(merged, 64)
        node_scale_ref[:, cols] = scale
        merged_ref[:, cols] = merged_ref[:, cols] / scale
        return carry

    lax.fori_loop(0, nodes // NODE_TILE, fit, 0)

    zero = jnp.zeros(x_ref.shape[1:], F32)
    spread_levels(mix_ref, mix3_ref)
    spread_levels(sens_ref, x_ref)

    def down(level, state):
        mix_prev, gain_prev, d_prev = state
        mix = mix3_ref[level]
        scale = 1.0 / (1.0 + mix + mix_prev * (1.0 - gain_prev))
        gain = mix * scale
        carry = mix_prev * scale
        d_next = x_ref[level] * scale + carry * d_prev
        gain_ref[level] = gain
        scale_ref[level] = scale
        carry_ref[level] = carry
        x_ref[level] = d_next
        return mix, gain, d_next

    lax.fori_loop(0, layers, down, (zero, zero, zero), unroll=4)
    sweep_up(x_ref, gain_ref, zero)
    keep = 1.0 - jnp.sum(coef_ref[...], axis=0, keepdims=True)
    for level in range(0, layers, 16):
        flat = x_ref[level : level + 16].reshape(16, nodes)
        if level == 0:
            surface_ref[...] = flat[0:1]
        xkeep_ref[level : level + 16, :] = flat * keep
        high, low = halves(flat * node_scale_ref[...])
        scaled_ref[level : level + 16, :] = high
        scaled_ref[layers + level : layers + level + 16, :] = low

    for block in range(halo // SLOT_ROWS):

        def collect(step, total):
            cols = pl.ds(pl.multiple_of(step * NODE_TILE, NODE_TILE), NODE_TILE)
            weights = slot_weights(adj_ref, merged_ref, cols, nodes + block * SLOT_ROWS)
            return total + lax.dot_general(
                scaled_ref[:, cols], weights, LANE_CONTRACT, preferred_element_type=F32
            )

        total = lax.fori_loop(
            0, nodes // NODE_TILE, collect, jnp.zeros((2 * layers, SLOT_ROWS), F32)
        )
        high, low = halves(total[:layers] + total[layers:])
        both = jnp.concatenate([high.astype(F32), low.astype(F32)], 0)
        hgrad_buf[block * SLOT_ROWS : (block + 1) * SLOT_ROWS, :] = both.T.astype(BF16)

    home = halo_copies(hgrad_buf, back_buf, gsend_sem, grecv_sem)
    for copy in home:
        copy.start()
    mine_back = own_copy(hgrad_buf, back_buf, gsend_sem.at[0])
    mine_back.start()

    for copy in rims:
        copy.wait()
    for f in range(fields):
        right = from_right_buf[f].astype(F32)
        left = from_left_buf[f].astype(F32)
        other_ref[f, :mid, :] = jnp.where(low_lane, right, left).astype(BF16)
        other_ref[f, mid:, :] = pltpu.roll(
            jnp.where(low_lane, left, right), tile_cols // 2, 1
        ).astype(BF16)

    mine.wait()
    for copy in there:
        copy.wait()
    received_ref[...] = received_buf[...].astype(F32).T.astype(BF16)
    mine_back.wait()
    for copy in home:
        copy.wait()
    back_ref[...] = back_buf[...].astype(F32).T.astype(BF16)


def forcing_kernel(
    start_ref,
    factor_ref,
    atm_ref,
    other_ref,
    row_ref,
    col_ref,
    share_ref,
    surface_ref,
    thermal_ref,
    flux_ref,
    corr_ref,
    own_ref,
    up_ref,
    down_ref,
    window_ref,
    grad_ref,
):
    fields, tile_rows, window_cols = grad_ref.shape
    tile_cols = window_cols // 2
    mid = tile_rows // 2
    tile = row_ref.shape[1]

    @pl.when(pl.program_id(0) == 0)
    def _():
        grad_ref[...] = jnp.zeros_like(grad_ref)
        window_ref[:, :tile_cols] = atm_ref[...].reshape(fields * tile_rows, tile_cols)
        window_ref[:, tile_cols:] = other_ref[...].reshape(fields * tile_rows, tile_cols)

    share = share_ref[...]
    row_low = share[0:1] + share[2:3]
    row_high = share[1:2] + share[3:4]
    col_low = share[0:1] + share[1:2]
    col_high = share[2:3] + share[3:4]
    scale = best_scale([col_low, col_high], 64)
    col_low = col_low / scale
    col_high = col_high / scale
    base_row = row_ref[0:1, :]
    base_col = lax.rem(col_ref[0:1, :] + start_ref[0], window_cols)
    next_col = lax.rem(base_col + 1, window_cols)
    row_at = lax.broadcasted_iota(jnp.int32, (tile_rows, tile), 0)
    col_at = lax.broadcasted_iota(jnp.int32, (window_cols, tile), 0)
    rows = jnp.where(
        row_at == base_row, row_low, jnp.where(row_at == base_row + 1, row_high, 0.0)
    )
    cols = jnp.where(
        col_at == base_col, col_low, jnp.where(col_at == next_col, col_high, 0.0)
    )
    cols = cols.astype(BF16)
    rows = rows * scale
    mixed = jnp.dot(window_ref[...], cols, preferred_element_type=F32)
    forced = [
        jnp.sum(mixed[f * tile_rows : (f + 1) * tile_rows] * rows, axis=0, keepdims=True)
        for f in range(fields)
    ]
    wind = jnp.sqrt(forced[0] * forced[0] + forced[1] * forced[1] + 1.0)
    excess = forced[2] - thermal_ref[0:1, :]
    flux = 0.1 * wind * excess
    for f in range(fields):
        flux = flux + factor_ref[f] * forced[f]
    flux_ref[...] = flux
    surface = surface_ref[...]
    corr_ref[...] = -0.1 * surface * wind
    quotient = surface * (0.1 * excess / wind)
    dot = functools.partial(
        lax.dot_general,
        dimension_numbers=LANE_CONTRACT,
        preferred_element_type=F32,
    )
    lefts = []
    for f in range(fields):
        node_grad = surface * factor_ref[f]
        if f < 2:
            node_grad = node_grad + quotient * forced[f]
        if f == 2:
            node_grad = node_grad + 0.1 * surface * wind
        lefts.append(halves(node_grad * rows))
    left_hi = jnp.concatenate([high for high, _ in lefts], 0)
    left_lo = jnp.concatenate([low for _, low in lefts], 0)
    grad = dot(left_hi, cols) + dot(left_lo, cols)
    grad_ref[...] += grad.reshape(fields, tile_rows, window_cols)

    @pl.when(pl.program_id(0) == pl.num_programs(0) - 1)
    def _():
        low_lane = lax.broadcasted_iota(jnp.int32, (mid, tile_cols), 1) < tile_cols // 2
        for f in range(fields):
            own_ref[f] = grad_ref[f, :, :tile_cols]
            upper = grad_ref[f, :mid, tile_cols:]
            lower = pltpu.roll(grad_ref[f, mid:, tile_cols:], tile_cols // 2, 1)
            up_ref[f] = jnp.where(low_lane, upper, lower)
            down_ref[f] = jnp.where(low_lane, lower, upper)


def lateral_kernel(
    adj_ref,
    merged_ref,
    node_scale_ref,
    coef_ref,
    thermal_ref,
    received_ref,
    scaled_ref,
    xkeep_ref,
    back_ref,
    sent_ref,
    flux_ref,
    corr_ref,
    gain_ref,
    scale_ref,
    carry_ref,
    warm_ref,
    grad_ref,
    rhs_ref,
    x_ref,
):
    slots, nodes = adj_ref.shape
    layers = rhs_ref.shape[0]
    parts = sent_ref.shape[0]
    tiles = nodes // NODE_TILE
    keep = 1.0 - jnp.sum(coef_ref[...], axis=0, keepdims=True)
    rhs_ref[...] = thermal_ref[...] * keep

    def block(step, carry):
        here = pl.ds(pl.multiple_of(step * SLOT_ROWS, SLOT_ROWS), SLOT_ROWS)
        high, low = halves(thermal_ref[:, here])
        ext = jnp.concatenate([high, low], 0)
        total = jnp.zeros((2 * layers, SLOT_ROWS), F32)
        for tile in range(tiles):
            cols = pl.ds(tile * NODE_TILE, NODE_TILE)
            weights = slot_weights(adj_ref, merged_ref, cols, step * SLOT_ROWS)
            part = jnp.dot(ext, weights, preferred_element_type=F32)
            rhs_ref[:, cols] += (part[:layers] + part[layers:]) * node_scale_ref[:, cols]
            total += lax.dot_general(
                scaled_ref[:, cols], weights, LANE_CONTRACT, preferred_element_type=F32
            )
        grad_ref[:, here] = xkeep_ref[:, here] + (total[:layers] + total[layers:])
        return carry

    lax.fori_loop(0, nodes // SLOT_ROWS, block, 0)
    for first in range(0, received_ref.shape[1], SLOT_ROWS):
        ext = received_ref[:, first : first + SLOT_ROWS]

        def arrive(step, carry):
            cols = pl.ds(pl.multiple_of(step * NODE_TILE, NODE_TILE), NODE_TILE)
            weights = slot_weights(adj_ref, merged_ref, cols, nodes + first)
            part = jnp.dot(ext, weights, preferred_element_type=F32)
            rhs_ref[:, cols] += (part[:layers] + part[layers:]) * node_scale_ref[:, cols]
            return carry

        lax.fori_loop(0, tiles, arrive, 0)

    def give_back(step, carry):
        cols = pl.ds(pl.multiple_of(step * NODE_TILE, NODE_TILE), NODE_TILE)
        first = (step * NODE_TILE).astype(F32)
        chosen = jnp.concatenate(
            [chosen_rows(sent_ref, c, NODE_TILE, first) for c in range(parts)], 0
        )
        part = jnp.dot(back_ref[...], chosen, preferred_element_type=F32)
        grad_ref[:, cols] += part[:layers] + part[layers:]
        return carry

    lax.fori_loop(0, tiles, give_back, 0)
    grad_ref[0:1, :] += corr_ref[...]

    rhs_ref[0:1, :] += flux_ref[...]
    zero = jnp.zeros(x_ref.shape[1:], F32)
    spread_levels(rhs_ref, x_ref)

    def down(level, d_prev):
        d_next = x_ref[level] * scale_ref[level] + carry_ref[level] * d_prev
        x_ref[level] = d_next
        return d_next

    lax.fori_loop(0, layers, down, zero, unroll=8)
    sweep_up(x_ref, gain_ref, zero)
    for level in range(0, layers, 8):
        warm_ref[level : level + 8, :] = x_ref[level : level + 8].reshape(8, nodes)


def join_kernel(own_ref, below_ref, above_ref, out_ref):
    fields, tile_rows, tile_cols = own_ref.shape
    mid = tile_rows // 2
    low_lane = lax.broadcasted_iota(jnp.int32, (mid, tile_cols), 1) < tile_cols // 2
    for f in range(fields):
        below, above = below_ref[f], above_ref[f]
        out_ref[f, :mid, :] = own_ref[f, :mid, :] + jnp.where(low_lane, below, above)
        out_ref[f, mid:, :] = own_ref[f, mid:, :] + pltpu.roll(
            jnp.where(low_lane, above, below), tile_cols // 2, 1
        )


def cost(flops, moved):
    return pl.CostEstimate(flops=flops, bytes_accessed=moved, transcendentals=0)


def per_device(
    atmosphere_inputs,
    thermal_anomaly,
    mixing_rates,
    adjacency_table,
    lateral_spread_factor,
    sent_vertices,
    corner_parallel,
    corner_longitude,
    corner_share,
    exchange_factor,
    sensitivity_vector,
):
    layers, nodes = thermal_anomaly.shape
    fields, tile_rows, tile_cols = atmosphere_inputs.shape
    columns, each = sent_vertices.shape
    halo = columns * each
    slots = adjacency_table.shape[0]
    window_cols = 2 * tile_cols
    extended = nodes + halo
    upward = [(i, (i + 1) % columns) for i in range(columns)]
    downward = [((i + 1) % columns, i) for i in range(columns)]
    position = lax.axis_index("lon")
    start = ((columns - position) * tile_cols).astype(jnp.int32).reshape(1)

    dense = (layers, nodes // LANES, LANES)
    block = jax.ShapeDtypeStruct(dense, F32)
    rim = (fields, tile_rows // 2, tile_cols)
    (
        scaled,
        xkeep,
        surface,
        gain,
        scale,
        carry,
        merged,
        node_scale,
        received,
        back,
        other,
    ) = pl.pallas_call(
        exchange_kernel,
        out_shape=(
            jax.ShapeDtypeStruct((2 * layers, nodes), BF16),
            jax.ShapeDtypeStruct((layers, nodes), F32),
            jax.ShapeDtypeStruct((1, nodes), F32),
            block,
            block,
            block,
            jax.ShapeDtypeStruct((slots, nodes), F32),
            jax.ShapeDtypeStruct((1, nodes), F32),
            jax.ShapeDtypeStruct((2 * layers, halo), BF16),
            jax.ShapeDtypeStruct((2 * layers, halo), BF16),
            jax.ShapeDtypeStruct(atmosphere_inputs.shape, BF16),
        ),
        in_specs=whole(7),
        out_specs=tuple(whole(11)),
        scratch_shapes=[
            pltpu.VMEM(dense, F32),
            pltpu.VMEM(dense, F32),
            pltpu.VMEM((halo, 2 * layers), BF16),
            pltpu.VMEM((halo, 2 * layers), BF16),
            pltpu.VMEM((halo, 2 * layers), BF16),
            pltpu.VMEM((halo, 2 * layers), BF16),
            pltpu.VMEM(rim, BF16),
            pltpu.VMEM(rim, BF16),
            pltpu.VMEM(rim, BF16),
            pltpu.VMEM(rim, BF16),
            pltpu.SemaphoreType.DMA((columns,)),
            pltpu.SemaphoreType.DMA((columns,)),
            pltpu.SemaphoreType.DMA((columns,)),
            pltpu.SemaphoreType.DMA((columns,)),
            pltpu.SemaphoreType.DMA((4,)),
        ],
        compiler_params=pltpu.CompilerParams(
            vmem_limit_bytes=24 * MEBI, collective_id=0, has_side_effects=True
        ),
        cost_estimate=cost(layers * nodes * 20, layers * nodes * 24),
        name="exchange",
    )(
        mixing_rates,
        sensitivity_vector,
        thermal_anomaly,
        adjacency_table,
        lateral_spread_factor,
        sent_vertices,
        atmosphere_inputs,
    )

    line = pl.BlockSpec((1, FORCE_TILE), lambda i: (0, i))
    four = pl.BlockSpec((4, FORCE_TILE), lambda i: (0, i))

    def all_of(*shape):
        return pl.BlockSpec(shape, lambda i: (0,) * len(shape))

    flux, corr, own_forcing, up_rim, down_rim = pl.pallas_call(
        forcing_kernel,
        grid=(nodes // FORCE_TILE,),
        out_shape=(
            jax.ShapeDtypeStruct((1, nodes), F32),
            jax.ShapeDtypeStruct((1, nodes), F32),
            jax.ShapeDtypeStruct((fields, tile_rows, tile_cols), F32),
            jax.ShapeDtypeStruct(rim, F32),
            jax.ShapeDtypeStruct(rim, F32),
        ),
        in_specs=[
            pl.BlockSpec(memory_space=pltpu.SMEM),
            pl.BlockSpec(memory_space=pltpu.SMEM),
            all_of(fields, tile_rows, tile_cols),
            all_of(fields, tile_rows, tile_cols),
            four,
            four,
            four,
            line,
            pl.BlockSpec((8, FORCE_TILE), lambda i: (0, i)),
        ],
        out_specs=(
            line,
            line,
            all_of(fields, tile_rows, tile_cols),
            all_of(*rim),
            all_of(*rim),
        ),
        scratch_shapes=[
            pltpu.VMEM((fields * tile_rows, window_cols), BF16),
            pltpu.VMEM((fields, tile_rows, window_cols), F32),
        ],
        compiler_params=pltpu.CompilerParams(vmem_limit_bytes=32 * MEBI),
        cost_estimate=cost(8 * fields * tile_rows * window_cols * nodes, 4000000),
        name="forcing",
    )(
        start,
        exchange_factor,
        atmosphere_inputs,
        other,
        corner_parallel,
        corner_longitude,
        corner_share,
        surface,
        thermal_anomaly,
    )
    below = lax.ppermute(up_rim, "lon", upward)
    above = lax.ppermute(down_rim, "lon", downward)

    updated_warmth, temp_grad = pl.pallas_call(
        lateral_kernel,
        out_shape=(
            jax.ShapeDtypeStruct((layers, nodes), F32),
            jax.ShapeDtypeStruct((layers, nodes), F32),
        ),
        in_specs=whole(15),
        out_specs=tuple(whole(2)),
        scratch_shapes=[pltpu.VMEM((layers, nodes), F32), pltpu.VMEM(dense, F32)],
        compiler_params=pltpu.CompilerParams(vmem_limit_bytes=32 * MEBI),
        cost_estimate=cost(8 * layers * nodes * extended, 8000000),
        name="lateral",
    )(
        adjacency_table,
        merged,
        node_scale,
        lateral_spread_factor,
        thermal_anomaly,
        received,
        scaled,
        xkeep,
        back,
        sent_vertices,
        flux,
        corr,
        gain,
        scale,
        carry,
    )

    forcing_grad = pl.pallas_call(
        join_kernel,
        out_shape=jax.ShapeDtypeStruct((fields, tile_rows, tile_cols), F32),
        in_specs=whole(3),
        out_specs=pl.BlockSpec(memory_space=pltpu.VMEM),
        compiler_params=pltpu.CompilerParams(vmem_limit_bytes=8 * MEBI),
        cost_estimate=cost(fields * tile_rows * tile_cols, 2000000),
        name="join",
    )(own_forcing, below, above)
    return (updated_warmth, temp_grad, forcing_grad)


def solution(mesh):
    nodes = P(None, ("lat", "lon"))
    placed = (
        P(None, "lat", "lon"),
        nodes,
        nodes,
        nodes,
        nodes,
        P(("lat", "lon"), None),
        nodes,
        nodes,
        nodes,
        P(),
        nodes,
    )
    return jax.shard_map(
        per_device,
        mesh=mesh,
        in_specs=placed,
        out_specs=(nodes, nodes, P(None, "lat", "lon")),
        check_vma=False,
    )
```

```python
import functools

import jax
import jax.numpy as jnp
from jax import lax
from jax.experimental import pallas as pl
from jax.experimental.pallas import tpu as pltpu
from jax.sharding import PartitionSpec as P

F32 = jnp.float32
BF16 = jnp.bfloat16
MEBI = 1024 * 1024
LANES = 128
SLOT_ROWS = 256
NODE_TILE = 256
FORCE_TILE = 512
LANE_CONTRACT = (((1,), (1,)), ((), ()))
MESH = pl.DeviceIdType.MESH


def whole(count):
    return [pl.BlockSpec(memory_space=pltpu.VMEM)] * count


def halves(value):
    high = value.astype(BF16)
    return high, (value - high.astype(F32)).astype(BF16)


def spread_levels(source_ref, dense_ref):
    layers = dense_ref.shape[0]
    for level in range(0, layers, 8):
        dense_ref[level : level + 8] = source_ref[level : level + 8, :].reshape(
            (8,) + dense_ref.shape[1:]
        )


def sweep_up(x_ref, gain_ref, zero):
    layers = x_ref.shape[0]

    def up(step, x_next):
        level = layers - 1 - step
        x_here = x_ref[level] + gain_ref[level] * x_next
        x_ref[level] = x_here
        return x_here

    lax.fori_loop(0, layers, up, zero, unroll=8)


def best_scale(values, count):
    trial = lax.broadcasted_iota(jnp.int32, (count, values[0].shape[1]), 0).astype(F32)
    trial = 1.0 + trial * (1.0 / count)
    inverse = 1.0 / trial
    miss = jnp.zeros_like(trial)
    for value in values:
        gap = (value * inverse).astype(BF16).astype(F32) * trial - value
        miss = miss + gap * gap
    least = jnp.min(miss, axis=0, keepdims=True)
    return jnp.max(jnp.where(miss == least, trial, 1.0), axis=0, keepdims=True)


def slot_weights(adj_ref, merged_ref, cols, first_row):
    row = lax.broadcasted_iota(jnp.int32, (SLOT_ROWS, NODE_TILE), 0).astype(F32).astype(BF16)
    local = (adj_ref[:, cols] - first_row).astype(F32).astype(BF16)
    share = merged_ref[:, cols].astype(BF16)
    weights = jnp.zeros((SLOT_ROWS, NODE_TILE), BF16)
    for k in range(adj_ref.shape[0]):
        weights = jnp.where(row == local[k : k + 1, :], share[k : k + 1, :], weights)
    return weights


def slot_tables(adj_ref, coef_ref, merged_ref, rank_ref, low_ref, high_ref):
    slots, nodes = adj_ref.shape
    pad = 8 - slots
    at = lax.broadcasted_iota(jnp.int32, (8, nodes), 0)
    spare = lax.broadcasted_iota(jnp.int32, (pad, nodes), 0) - pad
    ids = jnp.concatenate([adj_ref[...], spare], 0)
    coef = jnp.concatenate([coef_ref[...], jnp.zeros((pad, nodes), F32)], 0)
    low = (ids & (SLOT_ROWS - 1)).astype(F32)
    high = (ids >> (SLOT_ROWS.bit_length() - 1)).astype(F32)
    ids = ids.astype(F32)
    merged = coef
    repeat = jnp.zeros((8, nodes), F32)
    for shift in range(1, 8):
        equal = ids == pltpu.roll(ids, shift, 0)
        merged = merged + jnp.where(equal, pltpu.roll(coef, shift, 0), 0.0)
        repeat = jnp.where(jnp.logical_and(equal, at >= shift), 1.0, repeat)
    rank = jnp.zeros((8, nodes), F32)
    for shift in range(1, slots):
        met = jnp.logical_and(low == pltpu.roll(low, shift, 0), at >= shift)
        rank = rank + jnp.where(met, 1.0 - pltpu.roll(repeat, shift, 0), 0.0)
    rank = jnp.where(jnp.logical_or(repeat > 0.0, at >= slots), -1.0, rank)
    place = jnp.zeros((8, nodes), F32)
    for shift in range(1, slots):
        second = jnp.logical_and(pltpu.roll(rank, shift, 0) == 1.0, at >= shift)
        place = place + jnp.where(second, 1.0, 0.0)
    merged_ref[...] = merged
    rank_ref[...] = rank
    low_ref[:8, :] = jnp.where(rank == 0.0, low, -1.0)
    high_ref[:8, :] = high
    for j in range(slots // 2):
        here = jnp.logical_and(rank == 1.0, place == float(j))
        low_ref[8 + j : 9 + j, :] = jnp.max(jnp.where(here, low, -1.0), axis=0, keepdims=True)
        high_ref[8 + j : 9 + j, :] = jnp.max(jnp.where(here, high, -1.0), axis=0, keepdims=True)


def chosen_rows(sent_ref, part, nodes, first_node):
    halo = sent_ref.shape[1]
    padded = jnp.concatenate(
        [sent_ref[...].astype(F32), jnp.zeros((sent_ref.shape[0], LANES - halo), F32)], 1
    )
    column = padded.T[:halo, part : part + 1] - first_node
    node_at = lax.broadcasted_iota(jnp.int32, (halo, nodes), 1).astype(F32)
    return jnp.where(column == node_at, 1.0, 0.0).astype(BF16)


def exchange_kernel(
    mix_ref,
    sens_ref,
    thermal_ref,
    adj_ref,
    coef_ref,
    sent_ref,
    atm_ref,
    scaled_ref,
    xkeep_ref,
    surface_ref,
    gain_ref,
    scale_ref,
    carry_ref,
    merged_ref,
    rank_ref,
    low_ref,
    high_ref,
    node_scale_ref,
    received_ref,
    back_ref,
    other_ref,
    mix3_ref,
    x_ref,
    depart_buf,
    received_buf,
    hgrad_buf,
    back_buf,
    right_buf,
    left_buf,
    from_left_buf,
    from_right_buf,
    send_sem,
    recv_sem,
    gsend_sem,
    grecv_sem,
    rim_sem,
):
    layers, nodes = mix_ref.shape
    slots = adj_ref.shape[0]
    parts, each = sent_ref.shape
    halo = parts * each
    fields, tile_rows, tile_cols = atm_ref.shape
    mid = tile_rows // 2
    me = lax.axis_index("lon")
    ahead = lax.rem(me + 1, parts)
    behind = lax.rem(me + parts - 1, parts)

    barrier = pltpu.get_barrier_semaphore()
    for off in range(1, parts):
        pl.semaphore_signal(
            barrier, inc=1, device_id={"lon": lax.rem(me + off, parts)}, device_id_type=MESH
        )

    low_lane = lax.broadcasted_iota(jnp.int32, (mid, tile_cols), 1) < tile_cols // 2
    for f in range(fields):
        upper = atm_ref[f, :mid, :].astype(F32)
        lower = pltpu.roll(atm_ref[f, mid:, :].astype(F32), tile_cols // 2, 1)
        right_buf[f] = jnp.where(low_lane, lower, upper).astype(BF16)
        left_buf[f] = jnp.where(low_lane, upper, lower).astype(BF16)

    pl.semaphore_wait(barrier, parts - 1)

    def rim_copy(source, target, index, to):
        return pltpu.make_async_remote_copy(
            src_ref=source,
            dst_ref=target,
            send_sem=rim_sem.at[index],
            recv_sem=rim_sem.at[2 + index],
            device_id={"lon": to},
            device_id_type=MESH,
        )

    rims = [
        rim_copy(right_buf, from_left_buf, 0, ahead),
        rim_copy(left_buf, from_right_buf, 1, behind),
    ]
    for copy in rims:
        copy.start()

    depart = jnp.zeros((halo, 2 * layers), F32)
    tile = 1024

    def pick(step, total):
        cols = pl.ds(pl.multiple_of(step * tile, tile), tile)
        high, low = halves(thermal_ref[:, cols])
        ext = jnp.concatenate([high, low], 0)
        first = (step * tile).astype(F32)
        chosen = jnp.concatenate(
            [chosen_rows(sent_ref, c, tile, first) for c in range(parts)], 0
        )
        return total + lax.dot_general(
            chosen, ext, LANE_CONTRACT, preferred_element_type=F32
        )

    depart = lax.fori_loop(0, nodes // tile, pick, depart)
    depart_buf[...] = depart.astype(BF16)

    def rows_of(part):
        return pl.ds(pl.multiple_of(part * each, each), each)

    def halo_copies(source, target, sends, recvs):
        copies = []
        for off in range(1, parts):
            peer = lax.rem(me + off, parts)
            copies.append(
                pltpu.make_async_remote_copy(
                    src_ref=source.at[rows_of(peer)],
                    dst_ref=target.at[rows_of(me)],
                    send_sem=sends.at[off],
                    recv_sem=recvs.at[off],
                    device_id={"lon": peer},
                    device_id_type=MESH,
                )
            )
        return copies

    def own_copy(source, target, sem):
        return pltpu.make_async_copy(source.at[rows_of(me)], target.at[rows_of(me)], sem)

    there = halo_copies(depart_buf, received_buf, send_sem, recv_sem)
    for copy in there:
        copy.start()
    mine = own_copy(depart_buf, received_buf, send_sem.at[0])
    mine.start()

    slot_tables(adj_ref, coef_ref, merged_ref, rank_ref, low_ref, high_ref)

    def fit(step, carry):
        cols = pl.ds(pl.multiple_of(step * NODE_TILE, NODE_TILE), NODE_TILE)
        merged = [merged_ref[k : k + 1, cols] for k in range(slots)]
        scale = best_scale(merged, 64)
        node_scale_ref[:, cols] = scale
        merged_ref[:, cols] = merged_ref[:, cols] / scale
        return carry

    lax.fori_loop(0, nodes // NODE_TILE, fit, 0)

    zero = jnp.zeros(x_ref.shape[1:], F32)
    spread_levels(mix_ref, mix3_ref)
    spread_levels(sens_ref, x_ref)

    def down(level, state):
        mix_prev, gain_prev, d_prev = state
        mix = mix3_ref[level]
        scale = 1.0 / (1.0 + mix + mix_prev * (1.0 - gain_prev))
        gain = mix * scale
        carry = mix_prev * scale
        d_next = x_ref[level] * scale + carry * d_prev
        gain_ref[level] = gain
        scale_ref[level] = scale
        carry_ref[level] = carry
        x_ref[level] = d_next
        return mix, gain, d_next

    lax.fori_loop(0, layers, down, (zero, zero, zero), unroll=4)
    sweep_up(x_ref, gain_ref, zero)
    keep = 1.0 - jnp.sum(coef_ref[...], axis=0, keepdims=True)
    for level in range(0, layers, 16):
        flat = x_ref[level : level + 16].reshape(16, nodes)
        if level == 0:
            surface_ref[...] = flat[0:1]
        xkeep_ref[level : level + 16, :] = flat * keep
        high, low = halves(flat * node_scale_ref[...])
        scaled_ref[level : level + 16, :] = high
        scaled_ref[layers + level : layers + level + 16, :] = low

    for block in range(halo // SLOT_ROWS):

        def collect(step, total):
            cols = pl.ds(pl.multiple_of(step * NODE_TILE, NODE_TILE), NODE_TILE)
            weights = slot_weights(adj_ref, merged_ref, cols, nodes + block * SLOT_ROWS)
            return total + lax.dot_general(
                scaled_ref[:, cols], weights, LANE_CONTRACT, preferred_element_type=F32
            )

        total = lax.fori_loop(
            0, nodes // NODE_TILE, collect, jnp.zeros((2 * layers, SLOT_ROWS), F32)
        )
        high, low = halves(total[:layers] + total[layers:])
        both = jnp.concatenate([high.astype(F32), low.astype(F32)], 0)
        hgrad_buf[block * SLOT_ROWS : (block + 1) * SLOT_ROWS, :] = both.T.astype(BF16)

    home = halo_copies(hgrad_buf, back_buf, gsend_sem, grecv_sem)
    for copy in home:
        copy.start()
    mine_back = own_copy(hgrad_buf, back_buf, gsend_sem.at[0])
    mine_back.start()

    for copy in rims:
        copy.wait()
    for f in range(fields):
        right = from_right_buf[f].astype(F32)
        left = from_left_buf[f].astype(F32)
        other_ref[f, :mid, :] = jnp.where(low_lane, right, left).astype(BF16)
        other_ref[f, mid:, :] = pltpu.roll(
            jnp.where(low_lane, left, right), tile_cols // 2, 1
        ).astype(BF16)

    mine.wait()
    for copy in there:
        copy.wait()
    received_ref[...] = received_buf[...].astype(F32).T.astype(BF16)
    mine_back.wait()
    for copy in home:
        copy.wait()
    back_ref[...] = back_buf[...].astype(F32).T.astype(BF16)


def forcing_kernel(
    start_ref,
    factor_ref,
    atm_ref,
    other_ref,
    row_ref,
    col_ref,
    share_ref,
    surface_ref,
    thermal_ref,
    flux_ref,
    corr_ref,
    own_ref,
    up_ref,
    down_ref,
    window_ref,
    grad_ref,
):
    fields, tile_rows, window_cols = grad_ref.shape
    tile_cols = window_cols // 2
    mid = tile_rows // 2
    tile = row_ref.shape[1]

    @pl.when(pl.program_id(0) == 0)
    def _():
        grad_ref[...] = jnp.zeros_like(grad_ref)
        window_ref[:, :tile_cols] = atm_ref[...].reshape(fields * tile_rows, tile_cols)
        window_ref[:, tile_cols:] = other_ref[...].reshape(fields * tile_rows, tile_cols)

    share = share_ref[...]
    row_low = share[0:1] + share[2:3]
    row_high = share[1:2] + share[3:4]
    col_low = share[0:1] + share[1:2]
    col_high = share[2:3] + share[3:4]
    scale = best_scale([col_low, col_high], 64)
    col_low = col_low / scale
    col_high = col_high / scale
    base_row = row_ref[0:1, :]
    base_col = lax.rem(col_ref[0:1, :] + start_ref[0], window_cols)
    next_col = lax.rem(base_col + 1, window_cols)
    row_at = lax.broadcasted_iota(jnp.int32, (tile_rows, tile), 0)
    col_at = lax.broadcasted_iota(jnp.int32, (window_cols, tile), 0)
    rows = jnp.where(
        row_at == base_row, row_low, jnp.where(row_at == base_row + 1, row_high, 0.0)
    )
    cols = jnp.where(
        col_at == base_col, col_low, jnp.where(col_at == next_col, col_high, 0.0)
    )
    cols = cols.astype(BF16)
    rows = rows * scale
    mixed = jnp.dot(window_ref[...], cols, preferred_element_type=F32)
    forced = [
        jnp.sum(mixed[f * tile_rows : (f + 1) * tile_rows] * rows, axis=0, keepdims=True)
        for f in range(fields)
    ]
    wind = jnp.sqrt(forced[0] * forced[0] + forced[1] * forced[1] + 1.0)
    excess = forced[2] - thermal_ref[0:1, :]
    flux = 0.1 * wind * excess
    for f in range(fields):
        flux = flux + factor_ref[f] * forced[f]
    flux_ref[...] = flux
    surface = surface_ref[...]
    corr_ref[...] = -0.1 * surface * wind
    quotient = surface * (0.1 * excess / wind)
    dot = functools.partial(
        lax.dot_general,
        dimension_numbers=LANE_CONTRACT,
        preferred_element_type=F32,
    )
    lefts = []
    for f in range(fields):
        node_grad = surface * factor_ref[f]
        if f < 2:
            node_grad = node_grad + quotient * forced[f]
        if f == 2:
            node_grad = node_grad + 0.1 * surface * wind
        lefts.append(halves(node_grad * rows))
    left_hi = jnp.concatenate([high for high, _ in lefts], 0)
    left_lo = jnp.concatenate([low for _, low in lefts], 0)
    grad = dot(left_hi, cols) + dot(left_lo, cols)
    grad_ref[...] += grad.reshape(fields, tile_rows, window_cols)

    @pl.when(pl.program_id(0) == pl.num_programs(0) - 1)
    def _():
        low_lane = lax.broadcasted_iota(jnp.int32, (mid, tile_cols), 1) < tile_cols // 2
        for f in range(fields):
            own_ref[f] = grad_ref[f, :, :tile_cols]
            upper = grad_ref[f, :mid, tile_cols:]
            lower = pltpu.roll(grad_ref[f, mid:, tile_cols:], tile_cols // 2, 1)
            up_ref[f] = jnp.where(low_lane, upper, lower)
            down_ref[f] = jnp.where(low_lane, lower, upper)


def write_keys(cols, tables, keys_ref):
    merged_ref, rank_ref, low_ref, high_ref = tables
    rank = rank_ref[:, cols]
    merged = merged_ref[:, cols]
    low = low_ref[:, cols].astype(BF16)
    high = high_ref[:, cols].astype(BF16)
    share = merged.astype(BF16)
    pairs = low.shape[0] - 8
    place = jnp.zeros((1, NODE_TILE), F32)
    seconds = [jnp.zeros((1, NODE_TILE), F32)] * pairs
    for k in range(1, 2 * pairs):
        here = rank[k : k + 1] == 1.0
        for j in range(pairs):
            mine = jnp.logical_and(here, place == float(j))
            seconds[j] = jnp.where(mine, merged[k : k + 1], seconds[j])
        place = place + jnp.where(here, 1.0, 0.0)
    seconds = [second.astype(BF16) for second in seconds]
    for first in range(0, SLOT_ROWS, 16):
        row = lax.broadcasted_iota(jnp.int32, (16, NODE_TILE), 0).astype(F32).astype(BF16)
        row = row + float(first)
        none = jnp.full((16, NODE_TILE), -1.0, BF16)
        zero = jnp.zeros((16, NODE_TILE), BF16)
        key, val = none, zero
        for k in range(2 * pairs):
            mine = row == low[k : k + 1]
            key = jnp.where(mine, high[k : k + 1], key)
            val = jnp.where(mine, share[k : k + 1], val)
        keys_ref[0, first : first + 16, :] = key
        keys_ref[1, first : first + 16, :] = val
        key, val = none, zero
        for j in range(pairs):
            mine = row == low[8 + j : 9 + j]
            key = jnp.where(mine, high[8 + j : 9 + j], key)
            val = jnp.where(mine, seconds[j], val)
        keys_ref[2, first : first + 16, :] = key
        keys_ref[3, first : first + 16, :] = val


def block_weights(keys_ref, blocks):
    pieces = [[] for _ in blocks]
    for first in range(0, SLOT_ROWS, 16):
        key0, val0, key1, val1 = (keys_ref[i, first : first + 16, :] for i in range(4))
        for block, into in zip(blocks, pieces):
            weights = jnp.where(key0 == float(block), val0, jnp.zeros_like(val0))
            into.append(jnp.where(key1 == float(block), val1, weights))
    return [jnp.concatenate(into, 0) for into in pieces]


def lateral_kernel(
    adj_ref,
    merged_ref,
    rank_ref,
    low_ref,
    high_ref,
    node_scale_ref,
    coef_ref,
    thermal_ref,
    received_ref,
    scaled_ref,
    xkeep_ref,
    back_ref,
    sent_ref,
    flux_ref,
    corr_ref,
    gain_ref,
    scale_ref,
    carry_ref,
    warm_ref,
    grad_ref,
    rhs_ref,
    x_ref,
    ext_ref,
    even_ref,
    odd_ref,
    even_sum_ref,
    odd_sum_ref,
    even_turned_ref,
    odd_turned_ref,
    deep_ref,
):
    slots, nodes = adj_ref.shape
    layers = rhs_ref.shape[0]
    parts = sent_ref.shape[0]
    tiles = nodes // NODE_TILE
    tables = merged_ref, rank_ref, low_ref, high_ref

    for tile in range(tiles):
        most = jnp.max(rank_ref[:, tile * NODE_TILE : (tile + 1) * NODE_TILE])
        deep_ref[tile] = most.astype(jnp.int32)
    high, low = halves(thermal_ref[...])
    ext_ref[:layers, :nodes] = high
    ext_ref[layers:, :nodes] = low
    ext_ref[:, nodes:] = received_ref[...]
    grad_ref[...] = xkeep_ref[...]

    def node_cols(tile):
        return pl.ds(pl.multiple_of(tile * NODE_TILE, NODE_TILE), NODE_TILE)

    def use(tile, keys_ref, sum_ref, turned_ref):
        cols = node_cols(tile)
        scaled = scaled_ref[:, cols]
        write_keys(cols, tables, keys_ref)
        blocks = ext_ref.shape[1] // SLOT_ROWS
        for start in range(0, blocks, 2):
            now = range(start, min(start + 2, blocks))
            for block, weights in zip(now, block_weights(keys_ref, now)):
                here = slice(block * SLOT_ROWS, (block + 1) * SLOT_ROWS)
                part = jnp.dot(ext_ref[:, here], weights, preferred_element_type=F32)
                if block == 0:
                    sum_ref[...] = part
                else:
                    sum_ref[...] += part
                if block * SLOT_ROWS < nodes:
                    turned_ref[:, here] = weights.T
                    part = jnp.dot(scaled, turned_ref[:, here], preferred_element_type=F32)
                    grad_ref[:, here] += part[:layers] + part[layers:]
        keep = 1.0 - jnp.sum(coef_ref[:, cols], axis=0, keepdims=True)
        rhs_ref[:, cols] = (
            thermal_ref[:, cols] * keep
            + (sum_ref[:layers, :] + sum_ref[layers:, :]) * node_scale_ref[:, cols]
        )

    def mend(tile):
        @pl.when(deep_ref[tile] > 1)
        def _():
            cols = node_cols(tile)
            adj = jnp.where(rank_ref[:slots, cols] > 1.0, adj_ref[:, cols], -SLOT_ROWS)
            share = merged_ref[:slots, cols].astype(BF16)
            row = lax.broadcasted_iota(jnp.int32, (SLOT_ROWS, NODE_TILE), 0)
            row = row.astype(F32).astype(BF16)

            def weights_of(block):
                local = (adj - block * SLOT_ROWS).astype(F32).astype(BF16)
                weights = jnp.zeros((SLOT_ROWS, NODE_TILE), BF16)
                for k in range(2, slots):
                    weights = jnp.where(row == local[k : k + 1], share[k : k + 1], weights)
                return weights

            def forward(block, weights):
                here = pl.ds(pl.multiple_of(block * SLOT_ROWS, SLOT_ROWS), SLOT_ROWS)
                part = jnp.dot(ext_ref[:, here], weights, preferred_element_type=F32)
                rhs_ref[:, cols] += (part[:layers] + part[layers:]) * node_scale_ref[:, cols]

            def own(block, carry):
                weights = weights_of(block)
                forward(block, weights)
                here = pl.ds(pl.multiple_of(block * SLOT_ROWS, SLOT_ROWS), SLOT_ROWS)
                part = lax.dot_general(
                    scaled_ref[:, cols], weights, LANE_CONTRACT, preferred_element_type=F32
                )
                grad_ref[:, here] += part[:layers] + part[layers:]
                return carry

            def arrived(block, carry):
                forward(block, weights_of(block))
                return carry

            lax.fori_loop(0, nodes // SLOT_ROWS, own, 0)
            lax.fori_loop(nodes // SLOT_ROWS, ext_ref.shape[1] // SLOT_ROWS, arrived, 0)

    def pair(step, carry):
        use(2 * step, even_ref, even_sum_ref, even_turned_ref)
        use(2 * step + 1, odd_ref, odd_sum_ref, odd_turned_ref)
        mend(2 * step)
        mend(2 * step + 1)
        return carry

    lax.fori_loop(0, tiles // 2, pair, 0)

    def give_back(step, carry):
        cols = pl.ds(pl.multiple_of(step * NODE_TILE, NODE_TILE), NODE_TILE)
        first = (step * NODE_TILE).astype(F32)
        chosen = jnp.concatenate(
            [chosen_rows(sent_ref, c, NODE_TILE, first) for c in range(parts)], 0
        )
        part = jnp.dot(back_ref[...], chosen, preferred_element_type=F32)
        grad_ref[:, cols] += part[:layers] + part[layers:]
        return carry

    lax.fori_loop(0, tiles, give_back, 0)
    grad_ref[0:1, :] += corr_ref[...]

    rhs_ref[0:1, :] += flux_ref[...]
    zero = jnp.zeros(x_ref.shape[1:], F32)
    spread_levels(rhs_ref, x_ref)

    def down(level, d_prev):
        d_next = x_ref[level] * scale_ref[level] + carry_ref[level] * d_prev
        x_ref[level] = d_next
        return d_next

    lax.fori_loop(0, layers, down, zero, unroll=8)
    sweep_up(x_ref, gain_ref, zero)
    for level in range(0, layers, 8):
        warm_ref[level : level + 8, :] = x_ref[level : level + 8].reshape(8, nodes)


def join_kernel(own_ref, below_ref, above_ref, out_ref):
    fields, tile_rows, tile_cols = own_ref.shape
    mid = tile_rows // 2
    low_lane = lax.broadcasted_iota(jnp.int32, (mid, tile_cols), 1) < tile_cols // 2
    for f in range(fields):
        below, above = below_ref[f], above_ref[f]
        out_ref[f, :mid, :] = own_ref[f, :mid, :] + jnp.where(low_lane, below, above)
        out_ref[f, mid:, :] = own_ref[f, mid:, :] + pltpu.roll(
            jnp.where(low_lane, above, below), tile_cols // 2, 1
        )


def cost(flops, moved):
    return pl.CostEstimate(flops=flops, bytes_accessed=moved, transcendentals=0)


def per_device(
    atmosphere_inputs,
    thermal_anomaly,
    mixing_rates,
    adjacency_table,
    lateral_spread_factor,
    sent_vertices,
    corner_parallel,
    corner_longitude,
    corner_share,
    exchange_factor,
    sensitivity_vector,
):
    layers, nodes = thermal_anomaly.shape
    fields, tile_rows, tile_cols = atmosphere_inputs.shape
    columns, each = sent_vertices.shape
    halo = columns * each
    slots = adjacency_table.shape[0]
    window_cols = 2 * tile_cols
    extended = nodes + halo
    upward = [(i, (i + 1) % columns) for i in range(columns)]
    downward = [((i + 1) % columns, i) for i in range(columns)]
    position = lax.axis_index("lon")
    start = ((columns - position) * tile_cols).astype(jnp.int32).reshape(1)

    dense = (layers, nodes // LANES, LANES)
    block = jax.ShapeDtypeStruct(dense, F32)
    rim = (fields, tile_rows // 2, tile_cols)
    (
        scaled,
        xkeep,
        surface,
        gain,
        scale,
        carry,
        merged,
        rank,
        low,
        high,
        node_scale,
        received,
        back,
        other,
    ) = pl.pallas_call(
        exchange_kernel,
        out_shape=(
            jax.ShapeDtypeStruct((2 * layers, nodes), BF16),
            jax.ShapeDtypeStruct((layers, nodes), F32),
            jax.ShapeDtypeStruct((1, nodes), F32),
            block,
            block,
            block,
            jax.ShapeDtypeStruct((8, nodes), F32),
            jax.ShapeDtypeStruct((8, nodes), F32),
            jax.ShapeDtypeStruct((8 + slots // 2, nodes), F32),
            jax.ShapeDtypeStruct((8 + slots // 2, nodes), F32),
            jax.ShapeDtypeStruct((1, nodes), F32),
            jax.ShapeDtypeStruct((2 * layers, halo), BF16),
            jax.ShapeDtypeStruct((2 * layers, halo), BF16),
            jax.ShapeDtypeStruct(atmosphere_inputs.shape, BF16),
        ),
        in_specs=whole(7),
        out_specs=tuple(whole(14)),
        scratch_shapes=[
            pltpu.VMEM(dense, F32),
            pltpu.VMEM(dense, F32),
            pltpu.VMEM((halo, 2 * layers), BF16),
            pltpu.VMEM((halo, 2 * layers), BF16),
            pltpu.VMEM((halo, 2 * layers), BF16),
            pltpu.VMEM((halo, 2 * layers), BF16),
            pltpu.VMEM(rim, BF16),
            pltpu.VMEM(rim, BF16),
            pltpu.VMEM(rim, BF16),
            pltpu.VMEM(rim, BF16),
            pltpu.SemaphoreType.DMA((columns,)),
            pltpu.SemaphoreType.DMA((columns,)),
            pltpu.SemaphoreType.DMA((columns,)),
            pltpu.SemaphoreType.DMA((columns,)),
            pltpu.SemaphoreType.DMA((4,)),
        ],
        compiler_params=pltpu.CompilerParams(
            vmem_limit_bytes=24 * MEBI, collective_id=0, has_side_effects=True
        ),
        cost_estimate=cost(layers * nodes * 20, layers * nodes * 24),
        name="exchange",
    )(
        mixing_rates,
        sensitivity_vector,
        thermal_anomaly,
        adjacency_table,
        lateral_spread_factor,
        sent_vertices,
        atmosphere_inputs,
    )

    line = pl.BlockSpec((1, FORCE_TILE), lambda i: (0, i))
    four = pl.BlockSpec((4, FORCE_TILE), lambda i: (0, i))

    def all_of(*shape):
        return pl.BlockSpec(shape, lambda i: (0,) * len(shape))

    flux, corr, own_forcing, up_rim, down_rim = pl.pallas_call(
        forcing_kernel,
        grid=(nodes // FORCE_TILE,),
        out_shape=(
            jax.ShapeDtypeStruct((1, nodes), F32),
            jax.ShapeDtypeStruct((1, nodes), F32),
            jax.ShapeDtypeStruct((fields, tile_rows, tile_cols), F32),
            jax.ShapeDtypeStruct(rim, F32),
            jax.ShapeDtypeStruct(rim, F32),
        ),
        in_specs=[
            pl.BlockSpec(memory_space=pltpu.SMEM),
            pl.BlockSpec(memory_space=pltpu.SMEM),
            all_of(fields, tile_rows, tile_cols),
            all_of(fields, tile_rows, tile_cols),
            four,
            four,
            four,
            line,
            pl.BlockSpec((8, FORCE_TILE), lambda i: (0, i)),
        ],
        out_specs=(
            line,
            line,
            all_of(fields, tile_rows, tile_cols),
            all_of(*rim),
            all_of(*rim),
        ),
        scratch_shapes=[
            pltpu.VMEM((fields * tile_rows, window_cols), BF16),
            pltpu.VMEM((fields, tile_rows, window_cols), F32),
        ],
        compiler_params=pltpu.CompilerParams(vmem_limit_bytes=32 * MEBI),
        cost_estimate=cost(8 * fields * tile_rows * window_cols * nodes, 4000000),
        name="forcing",
    )(
        start,
        exchange_factor,
        atmosphere_inputs,
        other,
        corner_parallel,
        corner_longitude,
        corner_share,
        surface,
        thermal_anomaly,
    )
    below = lax.ppermute(up_rim, "lon", upward)
    above = lax.ppermute(down_rim, "lon", downward)

    updated_warmth, temp_grad = pl.pallas_call(
        lateral_kernel,
        out_shape=(
            jax.ShapeDtypeStruct((layers, nodes), F32),
            jax.ShapeDtypeStruct((layers, nodes), F32),
        ),
        in_specs=whole(18),
        out_specs=tuple(whole(2)),
        scratch_shapes=[
            pltpu.VMEM((layers, nodes), F32),
            pltpu.VMEM(dense, F32),
            pltpu.VMEM((2 * layers, extended), BF16),
            pltpu.VMEM((4, SLOT_ROWS, NODE_TILE), BF16),
            pltpu.VMEM((4, SLOT_ROWS, NODE_TILE), BF16),
            pltpu.VMEM((2 * layers, NODE_TILE), F32),
            pltpu.VMEM((2 * layers, NODE_TILE), F32),
            pltpu.VMEM((NODE_TILE, nodes), BF16),
            pltpu.VMEM((NODE_TILE, nodes), BF16),
            pltpu.SMEM((nodes // NODE_TILE,), jnp.int32),
        ],
        compiler_params=pltpu.CompilerParams(vmem_limit_bytes=32 * MEBI),
        cost_estimate=cost(8 * layers * nodes * extended, 8000000),
        name="lateral",
    )(
        adjacency_table,
        merged,
        rank,
        low,
        high,
        node_scale,
        lateral_spread_factor,
        thermal_anomaly,
        received,
        scaled,
        xkeep,
        back,
        sent_vertices,
        flux,
        corr,
        gain,
        scale,
        carry,
    )

    forcing_grad = pl.pallas_call(
        join_kernel,
        out_shape=jax.ShapeDtypeStruct((fields, tile_rows, tile_cols), F32),
        in_specs=whole(3),
        out_specs=pl.BlockSpec(memory_space=pltpu.VMEM),
        compiler_params=pltpu.CompilerParams(vmem_limit_bytes=8 * MEBI),
        cost_estimate=cost(fields * tile_rows * tile_cols, 2000000),
        name="join",
    )(own_forcing, below, above)
    return (updated_warmth, temp_grad, forcing_grad)


def solution(mesh):
    nodes = P(None, ("lat", "lon"))
    placed = (
        P(None, "lat", "lon"),
        nodes,
        nodes,
        nodes,
        nodes,
        P(("lat", "lon"), None),
        nodes,
        nodes,
        nodes,
        P(),
        nodes,
    )
    return jax.shard_map(
        per_device,
        mesh=mesh,
        in_specs=placed,
        out_specs=(nodes, nodes, P(None, "lat", "lon")),
        check_vma=False,
    )
```

```python
import functools

import jax
import jax.numpy as jnp
from jax import lax
from jax.experimental import pallas as pl
from jax.experimental.pallas import tpu as pltpu
from jax.sharding import PartitionSpec as P

F32 = jnp.float32
BF16 = jnp.bfloat16
MEBI = 1024 * 1024
LANES = 128
SLOT_ROWS = 256
NODE_TILE = 256
FORCE_TILE = 512
LANE_CONTRACT = (((1,), (1,)), ((), ()))
MESH = pl.DeviceIdType.MESH


def whole(count):
    return [pl.BlockSpec(memory_space=pltpu.VMEM)] * count


def halves(value):
    high = value.astype(BF16)
    return high, (value - high.astype(F32)).astype(BF16)


def spread_levels(source_ref, dense_ref):
    layers = dense_ref.shape[0]
    for level in range(0, layers, 8):
        dense_ref[level : level + 8] = source_ref[level : level + 8, :].reshape(
            (8,) + dense_ref.shape[1:]
        )


def sweep_up(x_ref, gain_ref, zero):
    layers = x_ref.shape[0]

    def up(step, x_next):
        level = layers - 1 - step
        x_here = x_ref[level] + gain_ref[level] * x_next
        x_ref[level] = x_here
        return x_here

    lax.fori_loop(0, layers, up, zero, unroll=8)


def best_scale(values, count):
    trial = lax.broadcasted_iota(jnp.int32, (count, values[0].shape[1]), 0).astype(F32)
    trial = 1.0 + trial * (1.0 / count)
    inverse = 1.0 / trial
    miss = jnp.zeros_like(trial)
    for value in values:
        gap = (value * inverse).astype(BF16).astype(F32) * trial - value
        miss = miss + gap * gap
    least = jnp.min(miss, axis=0, keepdims=True)
    return jnp.max(jnp.where(miss == least, trial, 1.0), axis=0, keepdims=True)


def slot_weights(adj_ref, merged_ref, cols, first_row):
    row = lax.broadcasted_iota(jnp.int32, (SLOT_ROWS, NODE_TILE), 0).astype(F32).astype(BF16)
    local = (adj_ref[:, cols] - first_row).astype(F32).astype(BF16)
    share = merged_ref[:, cols].astype(BF16)
    weights = jnp.zeros((SLOT_ROWS, NODE_TILE), BF16)
    for k in range(adj_ref.shape[0]):
        weights = jnp.where(row == local[k : k + 1, :], share[k : k + 1, :], weights)
    return weights


def slot_tables(adj_ref, coef_ref, merged_ref, rank_ref, low_ref, high_ref):
    slots, nodes = adj_ref.shape
    pad = 8 - slots
    at = lax.broadcasted_iota(jnp.int32, (8, nodes), 0)
    spare = lax.broadcasted_iota(jnp.int32, (pad, nodes), 0) - pad
    ids = jnp.concatenate([adj_ref[...], spare], 0)
    coef = jnp.concatenate([coef_ref[...], jnp.zeros((pad, nodes), F32)], 0)
    low = (ids & (SLOT_ROWS - 1)).astype(F32)
    high = (ids >> (SLOT_ROWS.bit_length() - 1)).astype(F32)
    ids = ids.astype(F32)
    merged = coef
    repeat = jnp.zeros((8, nodes), F32)
    for shift in range(1, 8):
        equal = ids == pltpu.roll(ids, shift, 0)
        merged = merged + jnp.where(equal, pltpu.roll(coef, shift, 0), 0.0)
        repeat = jnp.where(jnp.logical_and(equal, at >= shift), 1.0, repeat)
    rank = jnp.zeros((8, nodes), F32)
    for shift in range(1, slots):
        met = jnp.logical_and(low == pltpu.roll(low, shift, 0), at >= shift)
        rank = rank + jnp.where(met, 1.0 - pltpu.roll(repeat, shift, 0), 0.0)
    rank = jnp.where(jnp.logical_or(repeat > 0.0, at >= slots), -1.0, rank)
    place = jnp.zeros((8, nodes), F32)
    for shift in range(1, slots):
        second = jnp.logical_and(pltpu.roll(rank, shift, 0) == 1.0, at >= shift)
        place = place + jnp.where(second, 1.0, 0.0)
    merged_ref[...] = merged
    rank_ref[...] = rank
    low_ref[:8, :] = jnp.where(rank == 0.0, low, -1.0)
    high_ref[:8, :] = high
    for j in range(slots // 2):
        here = jnp.logical_and(rank == 1.0, place == float(j))
        low_ref[8 + j : 9 + j, :] = jnp.max(jnp.where(here, low, -1.0), axis=0, keepdims=True)
        high_ref[8 + j : 9 + j, :] = jnp.max(jnp.where(here, high, -1.0), axis=0, keepdims=True)


def chosen_rows(sent_ref, part, nodes, first_node):
    halo = sent_ref.shape[1]
    padded = jnp.concatenate(
        [sent_ref[...].astype(F32), jnp.zeros((sent_ref.shape[0], LANES - halo), F32)], 1
    )
    column = padded.T[:halo, part : part + 1] - first_node
    node_at = lax.broadcasted_iota(jnp.int32, (halo, nodes), 1).astype(F32)
    return jnp.where(column == node_at, 1.0, 0.0).astype(BF16)


def exchange_kernel(
    mix_hbm,
    sens_hbm,
    thermal_hbm,
    adj_hbm,
    coef_hbm,
    sent_hbm,
    atm_hbm,
    scaled_ref,
    xkeep_ref,
    surface_ref,
    gain_ref,
    scale_ref,
    carry_ref,
    merged_ref,
    rank_ref,
    low_ref,
    high_ref,
    node_scale_ref,
    received_ref,
    back_ref,
    other_ref,
    mix3_ref,
    x_ref,
    depart_buf,
    received_buf,
    hgrad_buf,
    back_buf,
    right_buf,
    left_buf,
    from_left_buf,
    from_right_buf,
    send_sem,
    recv_sem,
    gsend_sem,
    grecv_sem,
    rim_sem,
    mix_ref,
    sens_ref,
    thermal_ref,
    adj_ref,
    coef_ref,
    sent_ref,
    atm_ref,
    load_sem,
):
    load = {}
    sources = (
        ("atm", atm_hbm, atm_ref),
        ("sent", sent_hbm, sent_ref),
        ("thermal", thermal_hbm, thermal_ref),
        ("adj", adj_hbm, adj_ref),
        ("coef", coef_hbm, coef_ref),
        ("mix", mix_hbm, mix_ref),
        ("sens", sens_hbm, sens_ref),
    )
    for index, (name, source, target) in enumerate(sources):
        load[name] = pltpu.make_async_copy(source, target, load_sem.at[index])
        load[name].start()
    layers, nodes = mix_ref.shape
    slots = adj_ref.shape[0]
    parts, each = sent_ref.shape
    halo = parts * each
    fields, tile_rows, tile_cols = atm_ref.shape
    mid = tile_rows // 2
    me = lax.axis_index("lon")
    ahead = lax.rem(me + 1, parts)
    behind = lax.rem(me + parts - 1, parts)

    barrier = pltpu.get_barrier_semaphore()
    for off in range(1, parts):
        pl.semaphore_signal(
            barrier, inc=1, device_id={"lon": lax.rem(me + off, parts)}, device_id_type=MESH
        )

    load["atm"].wait()
    low_lane = lax.broadcasted_iota(jnp.int32, (mid, tile_cols), 1) < tile_cols // 2
    for f in range(fields):
        upper = atm_ref[f, :mid, :].astype(F32)
        lower = pltpu.roll(atm_ref[f, mid:, :].astype(F32), tile_cols // 2, 1)
        right_buf[f] = jnp.where(low_lane, lower, upper).astype(BF16)
        left_buf[f] = jnp.where(low_lane, upper, lower).astype(BF16)

    pl.semaphore_wait(barrier, parts - 1)

    def rim_copy(source, target, index, to):
        return pltpu.make_async_remote_copy(
            src_ref=source,
            dst_ref=target,
            send_sem=rim_sem.at[index],
            recv_sem=rim_sem.at[2 + index],
            device_id={"lon": to},
            device_id_type=MESH,
        )

    rims = [
        rim_copy(right_buf, from_left_buf, 0, ahead),
        rim_copy(left_buf, from_right_buf, 1, behind),
    ]
    for copy in rims:
        copy.start()

    load["sent"].wait()
    load["thermal"].wait()
    depart = jnp.zeros((halo, 2 * layers), F32)
    tile = 1024

    def pick(step, total):
        cols = pl.ds(pl.multiple_of(step * tile, tile), tile)
        high, low = halves(thermal_ref[:, cols])
        ext = jnp.concatenate([high, low], 0)
        first = (step * tile).astype(F32)
        chosen = jnp.concatenate(
            [chosen_rows(sent_ref, c, tile, first) for c in range(parts)], 0
        )
        return total + lax.dot_general(
            chosen, ext, LANE_CONTRACT, preferred_element_type=F32
        )

    depart = lax.fori_loop(0, nodes // tile, pick, depart)
    depart_buf[...] = depart.astype(BF16)

    def rows_of(part):
        return pl.ds(pl.multiple_of(part * each, each), each)

    def halo_copies(source, target, sends, recvs):
        copies = []
        for off in range(1, parts):
            peer = lax.rem(me + off, parts)
            copies.append(
                pltpu.make_async_remote_copy(
                    src_ref=source.at[rows_of(peer)],
                    dst_ref=target.at[rows_of(me)],
                    send_sem=sends.at[off],
                    recv_sem=recvs.at[off],
                    device_id={"lon": peer},
                    device_id_type=MESH,
                )
            )
        return copies

    def own_copy(source, target, sem):
        return pltpu.make_async_copy(source.at[rows_of(me)], target.at[rows_of(me)], sem)

    there = halo_copies(depart_buf, received_buf, send_sem, recv_sem)
    for copy in there:
        copy.start()
    mine = own_copy(depart_buf, received_buf, send_sem.at[0])
    mine.start()

    load["adj"].wait()
    load["coef"].wait()
    slot_tables(adj_ref, coef_ref, merged_ref, rank_ref, low_ref, high_ref)

    def fit(step, carry):
        cols = pl.ds(pl.multiple_of(step * NODE_TILE, NODE_TILE), NODE_TILE)
        merged = [merged_ref[k : k + 1, cols] for k in range(slots)]
        scale = best_scale(merged, 64)
        node_scale_ref[:, cols] = scale
        merged_ref[:, cols] = merged_ref[:, cols] / scale
        return carry

    lax.fori_loop(0, nodes // NODE_TILE, fit, 0)

    zero = jnp.zeros(x_ref.shape[1:], F32)
    load["mix"].wait()
    load["sens"].wait()
    spread_levels(mix_ref, mix3_ref)
    spread_levels(sens_ref, x_ref)

    def down(level, state):
        mix_prev, gain_prev, d_prev = state
        mix = mix3_ref[level]
        scale = 1.0 / (1.0 + mix + mix_prev * (1.0 - gain_prev))
        gain = mix * scale
        carry = mix_prev * scale
        d_next = x_ref[level] * scale + carry * d_prev
        gain_ref[level] = gain
        scale_ref[level] = scale
        carry_ref[level] = carry
        x_ref[level] = d_next
        return mix, gain, d_next

    lax.fori_loop(0, layers, down, (zero, zero, zero), unroll=4)
    sweep_up(x_ref, gain_ref, zero)
    keep = 1.0 - jnp.sum(coef_ref[...], axis=0, keepdims=True)
    for level in range(0, layers, 16):
        flat = x_ref[level : level + 16].reshape(16, nodes)
        if level == 0:
            surface_ref[...] = flat[0:1]
        xkeep_ref[level : level + 16, :] = flat * keep
        high, low = halves(flat * node_scale_ref[...])
        scaled_ref[level : level + 16, :] = high
        scaled_ref[layers + level : layers + level + 16, :] = low

    for block in range(halo // SLOT_ROWS):

        def collect(step, total):
            cols = pl.ds(pl.multiple_of(step * NODE_TILE, NODE_TILE), NODE_TILE)
            weights = slot_weights(adj_ref, merged_ref, cols, nodes + block * SLOT_ROWS)
            return total + lax.dot_general(
                scaled_ref[:, cols], weights, LANE_CONTRACT, preferred_element_type=F32
            )

        total = lax.fori_loop(
            0, nodes // NODE_TILE, collect, jnp.zeros((2 * layers, SLOT_ROWS), F32)
        )
        high, low = halves(total[:layers] + total[layers:])
        both = jnp.concatenate([high.astype(F32), low.astype(F32)], 0)
        hgrad_buf[block * SLOT_ROWS : (block + 1) * SLOT_ROWS, :] = both.T.astype(BF16)

    home = halo_copies(hgrad_buf, back_buf, gsend_sem, grecv_sem)
    for copy in home:
        copy.start()
    mine_back = own_copy(hgrad_buf, back_buf, gsend_sem.at[0])
    mine_back.start()

    for copy in rims:
        copy.wait()
    for f in range(fields):
        right = from_right_buf[f].astype(F32)
        left = from_left_buf[f].astype(F32)
        other_ref[f, :mid, :] = jnp.where(low_lane, right, left).astype(BF16)
        other_ref[f, mid:, :] = pltpu.roll(
            jnp.where(low_lane, left, right), tile_cols // 2, 1
        ).astype(BF16)

    mine.wait()
    for copy in there:
        copy.wait()
    received_ref[...] = received_buf[...].astype(F32).T.astype(BF16)
    mine_back.wait()
    for copy in home:
        copy.wait()
    back_ref[...] = back_buf[...].astype(F32).T.astype(BF16)


def forcing_kernel(
    start_ref,
    factor_ref,
    atm_ref,
    other_ref,
    row_ref,
    col_ref,
    share_ref,
    surface_ref,
    thermal_ref,
    flux_ref,
    corr_ref,
    own_ref,
    up_ref,
    down_ref,
    window_ref,
    grad_ref,
):
    fields, tile_rows, window_cols = grad_ref.shape
    tile_cols = window_cols // 2
    mid = tile_rows // 2
    tile = row_ref.shape[1]

    @pl.when(pl.program_id(0) == 0)
    def _():
        grad_ref[...] = jnp.zeros_like(grad_ref)
        window_ref[:, :tile_cols] = atm_ref[...].reshape(fields * tile_rows, tile_cols)
        window_ref[:, tile_cols:] = other_ref[...].reshape(fields * tile_rows, tile_cols)

    share = share_ref[...]
    row_low = share[0:1] + share[2:3]
    row_high = share[1:2] + share[3:4]
    col_low = share[0:1] + share[1:2]
    col_high = share[2:3] + share[3:4]
    scale = best_scale([col_low, col_high], 64)
    col_low = col_low / scale
    col_high = col_high / scale
    base_row = row_ref[0:1, :]
    base_col = lax.rem(col_ref[0:1, :] + start_ref[0], window_cols)
    next_col = lax.rem(base_col + 1, window_cols)
    row_at = lax.broadcasted_iota(jnp.int32, (tile_rows, tile), 0)
    col_at = lax.broadcasted_iota(jnp.int32, (window_cols, tile), 0)
    rows = jnp.where(
        row_at == base_row, row_low, jnp.where(row_at == base_row + 1, row_high, 0.0)
    )
    cols = jnp.where(
        col_at == base_col, col_low, jnp.where(col_at == next_col, col_high, 0.0)
    )
    cols = cols.astype(BF16)
    rows = rows * scale
    mixed = jnp.dot(window_ref[...], cols, preferred_element_type=F32)
    forced = [
        jnp.sum(mixed[f * tile_rows : (f + 1) * tile_rows] * rows, axis=0, keepdims=True)
        for f in range(fields)
    ]
    wind = jnp.sqrt(forced[0] * forced[0] + forced[1] * forced[1] + 1.0)
    excess = forced[2] - thermal_ref[0:1, :]
    flux = 0.1 * wind * excess
    for f in range(fields):
        flux = flux + factor_ref[f] * forced[f]
    flux_ref[...] = flux
    surface = surface_ref[...]
    corr_ref[...] = -0.1 * surface * wind
    quotient = surface * (0.1 * excess / wind)
    dot = functools.partial(
        lax.dot_general,
        dimension_numbers=LANE_CONTRACT,
        preferred_element_type=F32,
    )
    lefts = []
    for f in range(fields):
        node_grad = surface * factor_ref[f]
        if f < 2:
            node_grad = node_grad + quotient * forced[f]
        if f == 2:
            node_grad = node_grad + 0.1 * surface * wind
        lefts.append(halves(node_grad * rows))
    left_hi = jnp.concatenate([high for high, _ in lefts], 0)
    left_lo = jnp.concatenate([low for _, low in lefts], 0)
    grad = dot(left_hi, cols) + dot(left_lo, cols)
    grad_ref[...] += grad.reshape(fields, tile_rows, window_cols)

    @pl.when(pl.program_id(0) == pl.num_programs(0) - 1)
    def _():
        low_lane = lax.broadcasted_iota(jnp.int32, (mid, tile_cols), 1) < tile_cols // 2
        for f in range(fields):
            own_ref[f] = grad_ref[f, :, :tile_cols]
            upper = grad_ref[f, :mid, tile_cols:]
            lower = pltpu.roll(grad_ref[f, mid:, tile_cols:], tile_cols // 2, 1)
            up_ref[f] = jnp.where(low_lane, upper, lower)
            down_ref[f] = jnp.where(low_lane, lower, upper)


def key_writer(cols, tables, keys_ref):
    merged_ref, rank_ref, low_ref, high_ref = tables
    rank = rank_ref[:, cols]
    merged = merged_ref[:, cols]
    low = low_ref[:, cols].astype(BF16)
    high = high_ref[:, cols].astype(BF16)
    share = merged.astype(BF16)
    pairs = low.shape[0] - 8
    place = jnp.zeros((1, NODE_TILE), F32)
    seconds = [jnp.zeros((1, NODE_TILE), F32)] * pairs
    for k in range(1, 2 * pairs):
        here = rank[k : k + 1] == 1.0
        for j in range(pairs):
            mine = jnp.logical_and(here, place == float(j))
            seconds[j] = jnp.where(mine, merged[k : k + 1], seconds[j])
        place = place + jnp.where(here, 1.0, 0.0)
    seconds = [second.astype(BF16) for second in seconds]

    def write(first):
        row = lax.broadcasted_iota(jnp.int32, (16, NODE_TILE), 0).astype(F32).astype(BF16)
        row = row + float(first)
        none = jnp.full((16, NODE_TILE), -1.0, BF16)
        zero = jnp.zeros((16, NODE_TILE), BF16)
        key, val = none, zero
        for k in range(2 * pairs):
            mine = row == low[k : k + 1]
            key = jnp.where(mine, high[k : k + 1], key)
            val = jnp.where(mine, share[k : k + 1], val)
        keys_ref[0, first : first + 16, :] = key
        keys_ref[1, first : first + 16, :] = val
        key, val = none, zero
        for j in range(pairs):
            mine = row == low[8 + j : 9 + j]
            key = jnp.where(mine, high[8 + j : 9 + j], key)
            val = jnp.where(mine, seconds[j], val)
        keys_ref[2, first : first + 16, :] = key
        keys_ref[3, first : first + 16, :] = val

    return write


def block_weights(keys_ref, blocks):
    pieces = [[] for _ in blocks]
    for first in range(0, SLOT_ROWS, 16):
        key0, val0, key1, val1 = (keys_ref[i, first : first + 16, :] for i in range(4))
        for block, into in zip(blocks, pieces):
            weights = jnp.where(key0 == float(block), val0, jnp.zeros_like(val0))
            into.append(jnp.where(key1 == float(block), val1, weights))
    return [jnp.concatenate(into, 0) for into in pieces]


def lateral_kernel(
    adj_ref,
    merged_ref,
    rank_ref,
    low_ref,
    high_ref,
    node_scale_ref,
    coef_ref,
    thermal_ref,
    received_ref,
    scaled_ref,
    xkeep_ref,
    back_ref,
    sent_ref,
    flux_ref,
    corr_ref,
    gain_ref,
    scale_ref,
    carry_ref,
    warm_ref,
    grad_ref,
    rhs_ref,
    x_ref,
    ext_ref,
    even_ref,
    odd_ref,
    even_sum_ref,
    odd_sum_ref,
    even_turned_ref,
    odd_turned_ref,
    deep_ref,
):
    slots, nodes = adj_ref.shape
    layers = rhs_ref.shape[0]
    parts = sent_ref.shape[0]
    tiles = nodes // NODE_TILE
    tables = merged_ref, rank_ref, low_ref, high_ref

    def node_cols(tile):
        start = tile * NODE_TILE
        if not isinstance(tile, int):
            start = pl.multiple_of(start, NODE_TILE)
        return pl.ds(start, NODE_TILE)

    def deep_block(tile, bound):
        cols = node_cols(tile)
        high = (adj_ref[:, cols] >> (SLOT_ROWS.bit_length() - 1)).astype(F32)
        deep = jnp.logical_and(rank_ref[:slots, cols] > 1.0, high < bound)
        return jnp.max(jnp.where(deep, high, -1.0)).astype(jnp.int32)

    for tile in range(tiles):
        deep_ref[tile] = deep_block(tile, float(ext_ref.shape[1]))
    high, low = halves(thermal_ref[...])
    ext_ref[:layers, :nodes] = high
    ext_ref[layers:, :nodes] = low
    ext_ref[:, nodes:] = received_ref[...]
    grad_ref[...] = xkeep_ref[...]

    def use(tile, keys_ref, next_keys_ref, sum_ref, turned_ref):
        write = key_writer(node_cols(jnp.minimum(tile + 1, tiles - 1)), tables, next_keys_ref)
        cols = node_cols(tile)
        scaled = scaled_ref[:, cols]
        groups = SLOT_ROWS // 16
        done = 0
        blocks = ext_ref.shape[1] // SLOT_ROWS
        for start in range(0, blocks, 2):
            now = range(start, min(start + 2, blocks))
            for block, weights in zip(now, block_weights(keys_ref, now)):
                here = slice(block * SLOT_ROWS, (block + 1) * SLOT_ROWS)
                part = jnp.dot(ext_ref[:, here], weights, preferred_element_type=F32)
                if block == 0:
                    sum_ref[...] = part
                else:
                    sum_ref[...] += part
                if block * SLOT_ROWS < nodes:
                    turned_ref[:, here] = weights.T
                    part = jnp.dot(scaled, turned_ref[:, here], preferred_element_type=F32)
                    grad_ref[:, here] += part[:layers] + part[layers:]
            until = min(groups, -(-groups * now[-1] // (blocks - 2)))
            for group in range(done, until):
                write(group * 16)
            done = until
        keep = 1.0 - jnp.sum(coef_ref[:, cols], axis=0, keepdims=True)
        rhs_ref[:, cols] = (
            thermal_ref[:, cols] * keep
            + (sum_ref[:layers, :] + sum_ref[layers:, :]) * node_scale_ref[:, cols]
        )

    def mend(tile):
        def one_block(block):
            cols = node_cols(tile)
            here = pl.ds(pl.multiple_of(block * SLOT_ROWS, SLOT_ROWS), SLOT_ROWS)
            local = jnp.where(
                rank_ref[:slots, cols] > 1.0, adj_ref[:, cols] - block * SLOT_ROWS, -1
            )
            local = local.astype(F32).astype(BF16)
            share = merged_ref[:slots, cols].astype(BF16)
            row = lax.broadcasted_iota(jnp.int32, (SLOT_ROWS, NODE_TILE), 0)
            row = row.astype(F32).astype(BF16)
            weights = jnp.zeros((SLOT_ROWS, NODE_TILE), BF16)
            for k in range(2, slots):
                weights = jnp.where(row == local[k : k + 1], share[k : k + 1], weights)
            part = jnp.dot(ext_ref[:, here], weights, preferred_element_type=F32)
            rhs_ref[:, cols] += (part[:layers] + part[layers:]) * node_scale_ref[:, cols]

            @pl.when(block * SLOT_ROWS < nodes)
            def _():
                part = lax.dot_general(
                    scaled_ref[:, cols], weights, LANE_CONTRACT, preferred_element_type=F32
                )
                grad_ref[:, here] += part[:layers] + part[layers:]

            return deep_block(tile, block.astype(F32))

        lax.while_loop(lambda block: block >= 0, one_block, deep_ref[tile])

    write = key_writer(node_cols(0), tables, even_ref)
    for group in range(SLOT_ROWS // 16):
        write(group * 16)

    def pair(step, carry):
        use(2 * step, even_ref, odd_ref, even_sum_ref, even_turned_ref)
        use(2 * step + 1, odd_ref, even_ref, odd_sum_ref, odd_turned_ref)
        mend(2 * step)
        mend(2 * step + 1)
        return carry

    lax.fori_loop(0, tiles // 2, pair, 0)

    def give_back(step, carry):
        cols = pl.ds(pl.multiple_of(step * NODE_TILE, NODE_TILE), NODE_TILE)
        first = (step * NODE_TILE).astype(F32)
        chosen = jnp.concatenate(
            [chosen_rows(sent_ref, c, NODE_TILE, first) for c in range(parts)], 0
        )
        part = jnp.dot(back_ref[...], chosen, preferred_element_type=F32)
        grad_ref[:, cols] += part[:layers] + part[layers:]
        return carry

    lax.fori_loop(0, tiles, give_back, 0)
    grad_ref[0:1, :] += corr_ref[...]

    rhs_ref[0:1, :] += flux_ref[...]
    zero = jnp.zeros(x_ref.shape[1:], F32)
    spread_levels(rhs_ref, x_ref)

    def down(level, d_prev):
        d_next = x_ref[level] * scale_ref[level] + carry_ref[level] * d_prev
        x_ref[level] = d_next
        return d_next

    lax.fori_loop(0, layers, down, zero, unroll=8)
    sweep_up(x_ref, gain_ref, zero)
    for level in range(0, layers, 8):
        warm_ref[level : level + 8, :] = x_ref[level : level + 8].reshape(8, nodes)


def join_kernel(own_ref, below_ref, above_ref, out_ref):
    fields, tile_rows, tile_cols = own_ref.shape
    mid = tile_rows // 2
    low_lane = lax.broadcasted_iota(jnp.int32, (mid, tile_cols), 1) < tile_cols // 2
    for f in range(fields):
        below, above = below_ref[f], above_ref[f]
        out_ref[f, :mid, :] = own_ref[f, :mid, :] + jnp.where(low_lane, below, above)
        out_ref[f, mid:, :] = own_ref[f, mid:, :] + pltpu.roll(
            jnp.where(low_lane, above, below), tile_cols // 2, 1
        )


def cost(flops, moved):
    return pl.CostEstimate(flops=flops, bytes_accessed=moved, transcendentals=0)


def per_device(
    atmosphere_inputs,
    thermal_anomaly,
    mixing_rates,
    adjacency_table,
    lateral_spread_factor,
    sent_vertices,
    corner_parallel,
    corner_longitude,
    corner_share,
    exchange_factor,
    sensitivity_vector,
):
    layers, nodes = thermal_anomaly.shape
    fields, tile_rows, tile_cols = atmosphere_inputs.shape
    columns, each = sent_vertices.shape
    halo = columns * each
    slots = adjacency_table.shape[0]
    window_cols = 2 * tile_cols
    extended = nodes + halo
    upward = [(i, (i + 1) % columns) for i in range(columns)]
    downward = [((i + 1) % columns, i) for i in range(columns)]
    position = lax.axis_index("lon")
    start = ((columns - position) * tile_cols).astype(jnp.int32).reshape(1)

    dense = (layers, nodes // LANES, LANES)
    block = jax.ShapeDtypeStruct(dense, F32)
    rim = (fields, tile_rows // 2, tile_cols)
    (
        scaled,
        xkeep,
        surface,
        gain,
        scale,
        carry,
        merged,
        rank,
        low,
        high,
        node_scale,
        received,
        back,
        other,
    ) = pl.pallas_call(
        exchange_kernel,
        out_shape=(
            jax.ShapeDtypeStruct((2 * layers, nodes), BF16),
            jax.ShapeDtypeStruct((layers, nodes), F32),
            jax.ShapeDtypeStruct((1, nodes), F32),
            block,
            block,
            block,
            jax.ShapeDtypeStruct((8, nodes), F32),
            jax.ShapeDtypeStruct((8, nodes), F32),
            jax.ShapeDtypeStruct((8 + slots // 2, nodes), F32),
            jax.ShapeDtypeStruct((8 + slots // 2, nodes), F32),
            jax.ShapeDtypeStruct((1, nodes), F32),
            jax.ShapeDtypeStruct((2 * layers, halo), BF16),
            jax.ShapeDtypeStruct((2 * layers, halo), BF16),
            jax.ShapeDtypeStruct(atmosphere_inputs.shape, BF16),
        ),
        in_specs=[pl.BlockSpec(memory_space=pltpu.HBM)] * 7,
        out_specs=tuple(whole(14)),
        scratch_shapes=[
            pltpu.VMEM(dense, F32),
            pltpu.VMEM(dense, F32),
            pltpu.VMEM((halo, 2 * layers), BF16),
            pltpu.VMEM((halo, 2 * layers), BF16),
            pltpu.VMEM((halo, 2 * layers), BF16),
            pltpu.VMEM((halo, 2 * layers), BF16),
            pltpu.VMEM(rim, BF16),
            pltpu.VMEM(rim, BF16),
            pltpu.VMEM(rim, BF16),
            pltpu.VMEM(rim, BF16),
            pltpu.SemaphoreType.DMA((columns,)),
            pltpu.SemaphoreType.DMA((columns,)),
            pltpu.SemaphoreType.DMA((columns,)),
            pltpu.SemaphoreType.DMA((columns,)),
            pltpu.SemaphoreType.DMA((4,)),
            pltpu.VMEM((layers, nodes), F32),
            pltpu.VMEM((layers, nodes), F32),
            pltpu.VMEM((layers, nodes), F32),
            pltpu.VMEM((slots, nodes), jnp.int32),
            pltpu.VMEM((slots, nodes), F32),
            pltpu.VMEM(sent_vertices.shape, jnp.int32),
            pltpu.VMEM(atmosphere_inputs.shape, BF16),
            pltpu.SemaphoreType.DMA((7,)),
        ],
        compiler_params=pltpu.CompilerParams(
            vmem_limit_bytes=47 * MEBI, collective_id=0, has_side_effects=True
        ),
        cost_estimate=cost(layers * nodes * 20, layers * nodes * 24),
        name="exchange",
    )(
        mixing_rates,
        sensitivity_vector,
        thermal_anomaly,
        adjacency_table,
        lateral_spread_factor,
        sent_vertices,
        atmosphere_inputs,
    )

    line = pl.BlockSpec((1, FORCE_TILE), lambda i: (0, i))
    four = pl.BlockSpec((4, FORCE_TILE), lambda i: (0, i))

    def all_of(*shape):
        return pl.BlockSpec(shape, lambda i: (0,) * len(shape))

    flux, corr, own_forcing, up_rim, down_rim = pl.pallas_call(
        forcing_kernel,
        grid=(nodes // FORCE_TILE,),
        out_shape=(
            jax.ShapeDtypeStruct((1, nodes), F32),
            jax.ShapeDtypeStruct((1, nodes), F32),
            jax.ShapeDtypeStruct((fields, tile_rows, tile_cols), F32),
            jax.ShapeDtypeStruct(rim, F32),
            jax.ShapeDtypeStruct(rim, F32),
        ),
        in_specs=[
            pl.BlockSpec(memory_space=pltpu.SMEM),
            pl.BlockSpec(memory_space=pltpu.SMEM),
            all_of(fields, tile_rows, tile_cols),
            all_of(fields, tile_rows, tile_cols),
            four,
            four,
            four,
            line,
            pl.BlockSpec((8, FORCE_TILE), lambda i: (0, i)),
        ],
        out_specs=(
            line,
            line,
            all_of(fields, tile_rows, tile_cols),
            all_of(*rim),
            all_of(*rim),
        ),
        scratch_shapes=[
            pltpu.VMEM((fields * tile_rows, window_cols), BF16),
            pltpu.VMEM((fields, tile_rows, window_cols), F32),
        ],
        compiler_params=pltpu.CompilerParams(vmem_limit_bytes=20 * MEBI),
        cost_estimate=cost(8 * fields * tile_rows * window_cols * nodes, 4000000),
        name="forcing",
    )(
        start,
        exchange_factor,
        atmosphere_inputs,
        other,
        corner_parallel,
        corner_longitude,
        corner_share,
        surface,
        thermal_anomaly,
    )
    below = lax.ppermute(up_rim, "lon", upward)
    above = lax.ppermute(down_rim, "lon", downward)

    updated_warmth, temp_grad = pl.pallas_call(
        lateral_kernel,
        out_shape=(
            jax.ShapeDtypeStruct((layers, nodes), F32),
            jax.ShapeDtypeStruct((layers, nodes), F32),
        ),
        in_specs=whole(18),
        out_specs=tuple(whole(2)),
        scratch_shapes=[
            pltpu.VMEM((layers, nodes), F32),
            pltpu.VMEM(dense, F32),
            pltpu.VMEM((2 * layers, extended), BF16),
            pltpu.VMEM((4, SLOT_ROWS, NODE_TILE), BF16),
            pltpu.VMEM((4, SLOT_ROWS, NODE_TILE), BF16),
            pltpu.VMEM((2 * layers, NODE_TILE), F32),
            pltpu.VMEM((2 * layers, NODE_TILE), F32),
            pltpu.VMEM((NODE_TILE, nodes), BF16),
            pltpu.VMEM((NODE_TILE, nodes), BF16),
            pltpu.SMEM((nodes // NODE_TILE,), jnp.int32),
        ],
        compiler_params=pltpu.CompilerParams(vmem_limit_bytes=32 * MEBI),
        cost_estimate=cost(8 * layers * nodes * extended, 8000000),
        name="lateral",
    )(
        adjacency_table,
        merged,
        rank,
        low,
        high,
        node_scale,
        lateral_spread_factor,
        thermal_anomaly,
        received,
        scaled,
        xkeep,
        back,
        sent_vertices,
        flux,
        corr,
        gain,
        scale,
        carry,
    )

    forcing_grad = pl.pallas_call(
        join_kernel,
        out_shape=jax.ShapeDtypeStruct((fields, tile_rows, tile_cols), F32),
        in_specs=whole(3),
        out_specs=pl.BlockSpec(memory_space=pltpu.VMEM),
        compiler_params=pltpu.CompilerParams(vmem_limit_bytes=8 * MEBI),
        cost_estimate=cost(fields * tile_rows * tile_cols, 2000000),
        name="join",
    )(own_forcing, below, above)
    return (updated_warmth, temp_grad, forcing_grad)


def solution(mesh):
    nodes = P(None, ("lat", "lon"))
    placed = (
        P(None, "lat", "lon"),
        nodes,
        nodes,
        nodes,
        nodes,
        P(("lat", "lon"), None),
        nodes,
        nodes,
        nodes,
        P(),
        nodes,
    )
    return jax.shard_map(
        per_device,
        mesh=mesh,
        in_specs=placed,
        out_specs=(nodes, nodes, P(None, "lat", "lon")),
        check_vma=False,
    )
```

```python
import functools

import jax
import jax.numpy as jnp
from jax import lax
from jax.experimental import pallas as pl
from jax.experimental.pallas import tpu as pltpu
from jax.sharding import PartitionSpec as P

F32 = jnp.float32
BF16 = jnp.bfloat16
MEBI = 1024 * 1024
LANES = 128
SLOT_ROWS = 256
NODE_TILE = 256
FORCE_TILE = 512
LANE_CONTRACT = (((1,), (1,)), ((), ()))
MESH = pl.DeviceIdType.MESH


def whole(count):
    return [pl.BlockSpec(memory_space=pltpu.VMEM)] * count


def halves(value):
    high = value.astype(BF16)
    return high, (value - high.astype(F32)).astype(BF16)


def spread_levels(source_ref, dense_ref):
    layers = dense_ref.shape[0]
    for level in range(0, layers, 8):
        dense_ref[level : level + 8] = source_ref[level : level + 8, :].reshape(
            (8,) + dense_ref.shape[1:]
        )


def sweep_up(x_ref, gain_ref, zero):
    layers = x_ref.shape[0]

    def up(step, x_next):
        level = layers - 1 - step
        x_here = x_ref[level] + gain_ref[level] * x_next
        x_ref[level] = x_here
        return x_here

    lax.fori_loop(0, layers, up, zero, unroll=8)


def best_scale(values, count):
    trial = lax.broadcasted_iota(jnp.int32, (count, values[0].shape[1]), 0).astype(F32)
    trial = 1.0 + trial * (1.0 / count)
    inverse = 1.0 / trial
    miss = jnp.zeros_like(trial)
    for value in values:
        gap = (value * inverse).astype(BF16).astype(F32) * trial - value
        miss = miss + gap * gap
    least = jnp.min(miss, axis=0, keepdims=True)
    return jnp.max(jnp.where(miss == least, trial, 1.0), axis=0, keepdims=True)


def slot_weights(adj_ref, merged_ref, cols, first_row):
    row = lax.broadcasted_iota(jnp.int32, (SLOT_ROWS, NODE_TILE), 0).astype(F32).astype(BF16)
    local = (adj_ref[:, cols] - first_row).astype(F32).astype(BF16)
    share = merged_ref[:, cols].astype(BF16)
    weights = jnp.zeros((SLOT_ROWS, NODE_TILE), BF16)
    for k in range(adj_ref.shape[0]):
        weights = jnp.where(row == local[k : k + 1, :], share[k : k + 1, :], weights)
    return weights


def slot_ids(adj_ref):
    slots, nodes = adj_ref.shape
    at = lax.broadcasted_iota(jnp.int32, (8, nodes), 0)
    spare = lax.broadcasted_iota(jnp.int32, (8 - slots, nodes), 0) - (8 - slots)
    return jnp.concatenate([adj_ref[...], spare], 0), at


def merge_slots(adj_ref, coef_ref, merged_ref):
    slots, nodes = adj_ref.shape
    ids, _ = slot_ids(adj_ref)
    coef = jnp.concatenate([coef_ref[...], jnp.zeros((8 - slots, nodes), F32)], 0)
    merged = coef
    for shift in range(1, 8):
        equal = ids == pltpu.roll(ids, shift, 0)
        merged = merged + jnp.where(equal, pltpu.roll(coef, shift, 0), 0.0)
    merged_ref[...] = merged


def rank_slots(adj_ref, rank_ref, low_ref, high_ref):
    slots, nodes = adj_ref.shape
    ids, at = slot_ids(adj_ref)
    low = (ids & (SLOT_ROWS - 1)).astype(F32)
    high = (ids >> (SLOT_ROWS.bit_length() - 1)).astype(F32)
    repeat = jnp.zeros((8, nodes), F32)
    for shift in range(1, slots):
        equal = ids == pltpu.roll(ids, shift, 0)
        repeat = jnp.where(jnp.logical_and(equal, at >= shift), 1.0, repeat)
    rank = jnp.zeros((8, nodes), F32)
    for shift in range(1, slots):
        met = jnp.logical_and(low == pltpu.roll(low, shift, 0), at >= shift)
        rank = rank + jnp.where(met, 1.0 - pltpu.roll(repeat, shift, 0), 0.0)
    rank = jnp.where(jnp.logical_or(repeat > 0.0, at >= slots), -1.0, rank)
    place = jnp.zeros((8, nodes), F32)
    for shift in range(1, slots):
        second = jnp.logical_and(pltpu.roll(rank, shift, 0) == 1.0, at >= shift)
        place = place + jnp.where(second, 1.0, 0.0)
    rank_ref[...] = rank
    low_ref[:8, :] = jnp.where(rank == 0.0, low, -1.0)
    high_ref[:8, :] = high
    for j in range(slots // 2):
        here = jnp.logical_and(rank == 1.0, place == float(j))
        low_ref[8 + j : 9 + j, :] = jnp.max(jnp.where(here, low, -1.0), axis=0, keepdims=True)
        high_ref[8 + j : 9 + j, :] = jnp.max(jnp.where(here, high, -1.0), axis=0, keepdims=True)


def sent_column(sent_ref, column_ref):
    parts, each = sent_ref.shape
    padded = jnp.concatenate(
        [sent_ref[...].astype(F32), jnp.zeros((parts, LANES - each), F32)], 1
    ).T
    for part in range(parts):
        column_ref[part * each : (part + 1) * each, :] = jnp.broadcast_to(
            padded[:each, part : part + 1], (each, LANES)
        )


def chosen_rows(column_ref, first_node):
    local = (column_ref[...] - first_node).astype(BF16)
    lane = lax.broadcasted_iota(jnp.int32, local.shape, 1).astype(F32)
    zero = jnp.zeros(local.shape, BF16)
    one = jnp.ones(local.shape, BF16)
    pieces = [
        jnp.where(local == (lane + float(start)).astype(BF16), one, zero)
        for start in range(0, NODE_TILE, LANES)
    ]
    return jnp.concatenate(pieces, 1)


def exchange_kernel(
    mix_hbm,
    sens_hbm,
    thermal_hbm,
    adj_hbm,
    coef_hbm,
    sent_hbm,
    atm_hbm,
    scaled_ref,
    xkeep_ref,
    surface_ref,
    gain_ref,
    scale_ref,
    carry_ref,
    merged_ref,
    rank_ref,
    low_ref,
    high_ref,
    node_scale_ref,
    received_ref,
    back_ref,
    other_ref,
    keep_ref,
    adj_out_ref,
    column_ref,
    mix3_ref,
    x_ref,
    depart_buf,
    received_buf,
    hgrad_buf,
    back_buf,
    right_buf,
    left_buf,
    from_left_buf,
    from_right_buf,
    send_sem,
    recv_sem,
    gsend_sem,
    grecv_sem,
    rim_sem,
    mix_ref,
    sens_ref,
    thermal_ref,
    adj_ref,
    coef_ref,
    sent_ref,
    atm_ref,
    load_sem,
):
    load = {}
    sources = (
        ("atm", atm_hbm, atm_ref),
        ("sent", sent_hbm, sent_ref),
        ("thermal", thermal_hbm, thermal_ref),
        ("adj", adj_hbm, adj_ref),
        ("coef", coef_hbm, coef_ref),
        ("mix", mix_hbm, mix_ref),
        ("sens", sens_hbm, sens_ref),
    )
    for index, (name, source, target) in enumerate(sources):
        load[name] = pltpu.make_async_copy(source, target, load_sem.at[index])
        load[name].start()
    layers, nodes = mix_ref.shape
    slots = adj_ref.shape[0]
    parts, each = sent_ref.shape
    halo = parts * each
    fields, tile_rows, tile_cols = atm_ref.shape
    mid = tile_rows // 2
    me = lax.axis_index("lon")
    ahead = lax.rem(me + 1, parts)
    behind = lax.rem(me + parts - 1, parts)

    barrier = pltpu.get_barrier_semaphore()
    for off in range(1, parts):
        pl.semaphore_signal(
            barrier, inc=1, device_id={"lon": lax.rem(me + off, parts)}, device_id_type=MESH
        )

    load["atm"].wait()
    low_lane = lax.broadcasted_iota(jnp.int32, (mid, tile_cols), 1) < tile_cols // 2
    for f in range(fields):
        upper = atm_ref[f, :mid, :].astype(F32)
        lower = pltpu.roll(atm_ref[f, mid:, :].astype(F32), tile_cols // 2, 1)
        right_buf[f] = jnp.where(low_lane, lower, upper).astype(BF16)
        left_buf[f] = jnp.where(low_lane, upper, lower).astype(BF16)

    pl.semaphore_wait(barrier, parts - 1)

    def rim_copy(source, target, index, to):
        return pltpu.make_async_remote_copy(
            src_ref=source,
            dst_ref=target,
            send_sem=rim_sem.at[index],
            recv_sem=rim_sem.at[2 + index],
            device_id={"lon": to},
            device_id_type=MESH,
        )

    rims = [
        rim_copy(right_buf, from_left_buf, 0, ahead),
        rim_copy(left_buf, from_right_buf, 1, behind),
    ]
    for copy in rims:
        copy.start()

    load["sent"].wait()
    load["thermal"].wait()
    sent_column(sent_ref, column_ref)
    depart = jnp.zeros((halo, 2 * layers), F32)
    tile = 1024

    def pick(step, total):
        cols = pl.ds(pl.multiple_of(step * tile, tile), tile)
        high, low = halves(thermal_ref[:, cols])
        ext = jnp.concatenate([high, low], 0)
        first = (step * tile).astype(F32)
        chosen = jnp.concatenate(
            [chosen_rows(column_ref, first + float(at)) for at in range(0, tile, NODE_TILE)], 1
        )
        return total + lax.dot_general(
            chosen, ext, LANE_CONTRACT, preferred_element_type=F32
        )

    depart = lax.fori_loop(0, nodes // tile, pick, depart)
    depart_buf[...] = depart.astype(BF16)

    def rows_of(part):
        return pl.ds(pl.multiple_of(part * each, each), each)

    def halo_copies(source, target, sends, recvs):
        copies = []
        for off in range(1, parts):
            peer = lax.rem(me + off, parts)
            copies.append(
                pltpu.make_async_remote_copy(
                    src_ref=source.at[rows_of(peer)],
                    dst_ref=target.at[rows_of(me)],
                    send_sem=sends.at[off],
                    recv_sem=recvs.at[off],
                    device_id={"lon": peer},
                    device_id_type=MESH,
                )
            )
        return copies

    def own_copy(source, target, sem):
        return pltpu.make_async_copy(source.at[rows_of(me)], target.at[rows_of(me)], sem)

    there = halo_copies(depart_buf, received_buf, send_sem, recv_sem)
    for copy in there:
        copy.start()
    mine = own_copy(depart_buf, received_buf, send_sem.at[0])
    mine.start()

    load["adj"].wait()
    load["coef"].wait()
    merge_slots(adj_ref, coef_ref, merged_ref)

    def fit(step, carry):
        cols = pl.ds(pl.multiple_of(step * NODE_TILE, NODE_TILE), NODE_TILE)
        merged = [merged_ref[k : k + 1, cols] for k in range(slots)]
        scale = best_scale(merged, 32)
        node_scale_ref[:, cols] = scale
        merged_ref[:, cols] = merged_ref[:, cols] / scale
        return carry

    lax.fori_loop(0, nodes // NODE_TILE, fit, 0)

    zero = jnp.zeros(x_ref.shape[1:], F32)
    load["mix"].wait()
    load["sens"].wait()
    spread_levels(mix_ref, mix3_ref)
    spread_levels(sens_ref, x_ref)

    def down(level, state):
        mix_prev, gain_prev, d_prev = state
        mix = mix3_ref[level]
        scale = 1.0 / (1.0 + mix + mix_prev * (1.0 - gain_prev))
        gain = mix * scale
        carry = mix_prev * scale
        d_next = x_ref[level] * scale + carry * d_prev
        gain_ref[level] = gain
        scale_ref[level] = scale
        carry_ref[level] = carry
        x_ref[level] = d_next
        return mix, gain, d_next

    lax.fori_loop(0, layers, down, (zero, zero, zero), unroll=4)
    sweep_up(x_ref, gain_ref, zero)
    keep = 1.0 - jnp.sum(coef_ref[...], axis=0, keepdims=True)
    keep_ref[...] = keep
    for level in range(0, layers, 16):
        flat = x_ref[level : level + 16].reshape(16, nodes)
        if level == 0:
            surface_ref[...] = flat[0:1]
        xkeep_ref[level : level + 16, :] = flat * keep
        high, low = halves(flat * node_scale_ref[...])
        scaled_ref[level : level + 16, :] = high
        scaled_ref[layers + level : layers + level + 16, :] = low

    for block in range(halo // SLOT_ROWS):

        def collect(step, total):
            cols = pl.ds(pl.multiple_of(step * NODE_TILE, NODE_TILE), NODE_TILE)
            weights = slot_weights(adj_ref, merged_ref, cols, nodes + block * SLOT_ROWS)
            return total + lax.dot_general(
                scaled_ref[:, cols], weights, LANE_CONTRACT, preferred_element_type=F32
            )

        total = lax.fori_loop(
            0, nodes // NODE_TILE, collect, jnp.zeros((2 * layers, SLOT_ROWS), F32)
        )
        high, low = halves(total[:layers] + total[layers:])
        both = jnp.concatenate([high.astype(F32), low.astype(F32)], 0)
        hgrad_buf[block * SLOT_ROWS : (block + 1) * SLOT_ROWS, :] = both.T.astype(BF16)

    home = halo_copies(hgrad_buf, back_buf, gsend_sem, grecv_sem)
    for copy in home:
        copy.start()
    mine_back = own_copy(hgrad_buf, back_buf, gsend_sem.at[0])
    mine_back.start()
    rank_slots(adj_ref, rank_ref, low_ref, high_ref)
    adj_out_ref[...] = adj_ref[...]

    for copy in rims:
        copy.wait()
    for f in range(fields):
        right = from_right_buf[f].astype(F32)
        left = from_left_buf[f].astype(F32)
        other_ref[f, :mid, :] = jnp.where(low_lane, right, left).astype(BF16)
        other_ref[f, mid:, :] = pltpu.roll(
            jnp.where(low_lane, left, right), tile_cols // 2, 1
        ).astype(BF16)

    mine.wait()
    for copy in there:
        copy.wait()
    received_ref[...] = received_buf[...].astype(F32).T.astype(BF16)
    mine_back.wait()
    for copy in home:
        copy.wait()
    back_ref[...] = back_buf[...].astype(F32).T.astype(BF16)


def forcing_kernel(
    start_ref,
    factor_ref,
    atm_ref,
    other_ref,
    row_ref,
    col_ref,
    share_ref,
    surface_ref,
    thermal_ref,
    flux_ref,
    corr_ref,
    own_ref,
    up_ref,
    down_ref,
    window_ref,
    grad_ref,
):
    fields, tile_rows, window_cols = grad_ref.shape
    tile_cols = window_cols // 2
    mid = tile_rows // 2
    tile = row_ref.shape[1]

    @pl.when(pl.program_id(0) == 0)
    def _():
        grad_ref[...] = jnp.zeros_like(grad_ref)
        window_ref[:, :tile_cols] = atm_ref[...].reshape(fields * tile_rows, tile_cols)
        window_ref[:, tile_cols:] = other_ref[...].reshape(fields * tile_rows, tile_cols)

    share = share_ref[...]
    row_low = share[0:1] + share[2:3]
    row_high = share[1:2] + share[3:4]
    col_low = share[0:1] + share[1:2]
    col_high = share[2:3] + share[3:4]
    scale = best_scale([col_low, col_high], 64)
    col_low = col_low / scale
    col_high = col_high / scale
    base_row = row_ref[0:1, :]
    base_col = lax.rem(col_ref[0:1, :] + start_ref[0], window_cols)
    next_col = lax.rem(base_col + 1, window_cols)
    row_at = lax.broadcasted_iota(jnp.int32, (tile_rows, tile), 0)
    col_at = lax.broadcasted_iota(jnp.int32, (window_cols, tile), 0)
    rows = jnp.where(
        row_at == base_row, row_low, jnp.where(row_at == base_row + 1, row_high, 0.0)
    )
    cols = jnp.where(
        col_at == base_col, col_low, jnp.where(col_at == next_col, col_high, 0.0)
    )
    cols = cols.astype(BF16)
    rows = rows * scale
    mixed = jnp.dot(window_ref[...], cols, preferred_element_type=F32)
    forced = [
        jnp.sum(mixed[f * tile_rows : (f + 1) * tile_rows] * rows, axis=0, keepdims=True)
        for f in range(fields)
    ]
    wind = jnp.sqrt(forced[0] * forced[0] + forced[1] * forced[1] + 1.0)
    excess = forced[2] - thermal_ref[0:1, :]
    flux = 0.1 * wind * excess
    for f in range(fields):
        flux = flux + factor_ref[f] * forced[f]
    flux_ref[...] = flux
    surface = surface_ref[...]
    corr_ref[...] = -0.1 * surface * wind
    quotient = surface * (0.1 * excess / wind)
    dot = functools.partial(
        lax.dot_general,
        dimension_numbers=LANE_CONTRACT,
        preferred_element_type=F32,
    )
    row_is = row_at.astype(F32).astype(BF16)
    base_is = base_row.astype(F32).astype(BF16)
    at_low = row_is == base_is
    at_high = row_is == base_is + 1.0
    none = jnp.zeros(row_is.shape, BF16)
    ends = [row_low * scale, row_high * scale]
    lefts = []
    for f in range(fields):
        node_grad = surface * factor_ref[f]
        if f < 2:
            node_grad = node_grad + quotient * forced[f]
        if f == 2:
            node_grad = node_grad + 0.1 * surface * wind
        below, above = (halves(node_grad * end) for end in ends)
        lefts.append(
            [
                jnp.where(at_low, low_end, jnp.where(at_high, high_end, none))
                for low_end, high_end in zip(below, above)
            ]
        )
    left_hi = jnp.concatenate([high for high, _ in lefts], 0)
    left_lo = jnp.concatenate([low for _, low in lefts], 0)
    grad = dot(left_hi, cols) + dot(left_lo, cols)
    grad_ref[...] += grad.reshape(fields, tile_rows, window_cols)

    @pl.when(pl.program_id(0) == pl.num_programs(0) - 1)
    def _():
        low_lane = lax.broadcasted_iota(jnp.int32, (mid, tile_cols), 1) < tile_cols // 2
        for f in range(fields):
            own_ref[f] = grad_ref[f, :, :tile_cols]
            upper = grad_ref[f, :mid, tile_cols:]
            lower = pltpu.roll(grad_ref[f, mid:, tile_cols:], tile_cols // 2, 1)
            up_ref[f] = jnp.where(low_lane, upper, lower)
            down_ref[f] = jnp.where(low_lane, lower, upper)


def key_writer(cols, tables, keys_ref):
    merged_ref, rank_ref, low_ref, high_ref = tables
    rank = rank_ref[:, cols]
    merged = merged_ref[:, cols]
    low = low_ref[:, cols].astype(BF16)
    high = high_ref[:, cols].astype(BF16)
    share = merged.astype(BF16)
    pairs = low.shape[0] - 8
    place = jnp.zeros((1, NODE_TILE), F32)
    seconds = [jnp.zeros((1, NODE_TILE), F32)] * pairs
    for k in range(1, 2 * pairs):
        here = rank[k : k + 1] == 1.0
        for j in range(pairs):
            mine = jnp.logical_and(here, place == float(j))
            seconds[j] = jnp.where(mine, merged[k : k + 1], seconds[j])
        place = place + jnp.where(here, 1.0, 0.0)
    seconds = [second.astype(BF16) for second in seconds]

    def write(first):
        row = lax.broadcasted_iota(jnp.int32, (16, NODE_TILE), 0).astype(F32).astype(BF16)
        row = row + float(first)
        none = jnp.full((16, NODE_TILE), -1.0, BF16)
        zero = jnp.zeros((16, NODE_TILE), BF16)
        key, val = none, zero
        for k in range(2 * pairs):
            mine = row == low[k : k + 1]
            key = jnp.where(mine, high[k : k + 1], key)
            val = jnp.where(mine, share[k : k + 1], val)
        keys_ref[0, first : first + 16, :] = key
        keys_ref[1, first : first + 16, :] = val
        key, val = none, zero
        for j in range(pairs):
            mine = row == low[8 + j : 9 + j]
            key = jnp.where(mine, high[8 + j : 9 + j], key)
            val = jnp.where(mine, seconds[j], val)
        keys_ref[2, first : first + 16, :] = key
        keys_ref[3, first : first + 16, :] = val

    return write


def block_weights(keys_ref, blocks):
    pieces = [[] for _ in blocks]
    for first in range(0, SLOT_ROWS, 16):
        key0, val0, key1, val1 = (keys_ref[i, first : first + 16, :] for i in range(4))
        for block, into in zip(blocks, pieces):
            weights = jnp.where(key0 == float(block), val0, jnp.zeros_like(val0))
            into.append(jnp.where(key1 == float(block), val1, weights))
    return [jnp.concatenate(into, 0) for into in pieces]


def lateral_kernel(
    adj_ref,
    merged_ref,
    rank_ref,
    low_ref,
    high_ref,
    node_scale_ref,
    keep_ref,
    thermal_ref,
    received_ref,
    scaled_ref,
    xkeep_ref,
    back_ref,
    column_ref,
    flux_ref,
    corr_ref,
    gain_ref,
    scale_ref,
    carry_ref,
    warm_ref,
    grad_ref,
    rhs_ref,
    x_ref,
    ext_ref,
    even_ref,
    odd_ref,
    even_sum_ref,
    odd_sum_ref,
    even_turned_ref,
    odd_turned_ref,
    deep_ref,
):
    slots, nodes = adj_ref.shape
    layers = rhs_ref.shape[0]
    tiles = nodes // NODE_TILE
    tables = merged_ref, rank_ref, low_ref, high_ref

    def node_cols(tile):
        start = tile * NODE_TILE
        if not isinstance(tile, int):
            start = pl.multiple_of(start, NODE_TILE)
        return pl.ds(start, NODE_TILE)

    def deep_block(tile, bound):
        cols = node_cols(tile)
        high = (adj_ref[:, cols] >> (SLOT_ROWS.bit_length() - 1)).astype(F32)
        deep = jnp.logical_and(rank_ref[:slots, cols] > 1.0, high < bound)
        return jnp.max(jnp.where(deep, high, -1.0)).astype(jnp.int32)

    for tile in range(tiles):
        deep_ref[tile] = deep_block(tile, float(ext_ref.shape[1]))
    high, low = halves(thermal_ref[...])
    ext_ref[:layers, :nodes] = high
    ext_ref[layers:, :nodes] = low
    ext_ref[:, nodes:] = received_ref[...]
    grad_ref[...] = xkeep_ref[...]

    def use(tile, keys_ref, next_keys_ref, sum_ref, turned_ref):
        write = key_writer(node_cols(jnp.minimum(tile + 1, tiles - 1)), tables, next_keys_ref)
        cols = node_cols(tile)
        scaled = scaled_ref[:, cols]
        groups = SLOT_ROWS // 16
        done = 0
        blocks = ext_ref.shape[1] // SLOT_ROWS
        for start in range(0, blocks, 2):
            now = range(start, min(start + 2, blocks))
            for block, weights in zip(now, block_weights(keys_ref, now)):
                here = slice(block * SLOT_ROWS, (block + 1) * SLOT_ROWS)
                part = jnp.dot(ext_ref[:, here], weights, preferred_element_type=F32)
                if block == 0:
                    sum_ref[...] = part
                else:
                    sum_ref[...] += part
                if block * SLOT_ROWS < nodes:
                    turned_ref[:, here] = weights.T
                    part = jnp.dot(scaled, turned_ref[:, here], preferred_element_type=F32)
                    grad_ref[:, here] += part[:layers] + part[layers:]
            until = min(groups, -(-groups * now[-1] // (blocks - 2)))
            for group in range(done, until):
                write(group * 16)
            done = until
        rhs_ref[:, cols] = (
            thermal_ref[:, cols] * keep_ref[:, cols]
            + (sum_ref[:layers, :] + sum_ref[layers:, :]) * node_scale_ref[:, cols]
        )

    def mend(tile):
        def one_block(block):
            cols = node_cols(tile)
            here = pl.ds(pl.multiple_of(block * SLOT_ROWS, SLOT_ROWS), SLOT_ROWS)
            local = jnp.where(
                rank_ref[:slots, cols] > 1.0, adj_ref[:, cols] - block * SLOT_ROWS, -1
            )
            local = local.astype(F32).astype(BF16)
            share = merged_ref[:slots, cols].astype(BF16)
            row = lax.broadcasted_iota(jnp.int32, (SLOT_ROWS, NODE_TILE), 0)
            row = row.astype(F32).astype(BF16)
            weights = jnp.zeros((SLOT_ROWS, NODE_TILE), BF16)
            for k in range(2, slots):
                weights = jnp.where(row == local[k : k + 1], share[k : k + 1], weights)
            part = jnp.dot(ext_ref[:, here], weights, preferred_element_type=F32)
            rhs_ref[:, cols] += (part[:layers] + part[layers:]) * node_scale_ref[:, cols]

            @pl.when(block * SLOT_ROWS < nodes)
            def _():
                part = lax.dot_general(
                    scaled_ref[:, cols], weights, LANE_CONTRACT, preferred_element_type=F32
                )
                grad_ref[:, here] += part[:layers] + part[layers:]

            return deep_block(tile, block.astype(F32))

        lax.while_loop(lambda block: block >= 0, one_block, deep_ref[tile])

    write = key_writer(node_cols(0), tables, even_ref)
    for group in range(SLOT_ROWS // 16):
        write(group * 16)

    def pair(step, carry):
        use(2 * step, even_ref, odd_ref, even_sum_ref, even_turned_ref)
        use(2 * step + 1, odd_ref, even_ref, odd_sum_ref, odd_turned_ref)
        mend(2 * step)
        mend(2 * step + 1)
        return carry

    lax.fori_loop(0, tiles // 2, pair, 0)

    width = 4 * NODE_TILE

    def give_back(step, carry):
        cols = pl.ds(pl.multiple_of(step * width, width), width)
        first = (step * width).astype(F32)
        chosen = jnp.concatenate(
            [chosen_rows(column_ref, first + float(at)) for at in range(0, width, NODE_TILE)], 1
        )
        part = jnp.dot(back_ref[...], chosen, preferred_element_type=F32)
        grad_ref[:, cols] += part[:layers] + part[layers:]
        return carry

    lax.fori_loop(0, nodes // width, give_back, 0)
    grad_ref[0:1, :] += corr_ref[...]

    rhs_ref[0:1, :] += flux_ref[...]
    zero = jnp.zeros(x_ref.shape[1:], F32)
    spread_levels(rhs_ref, x_ref)

    def down(level, d_prev):
        d_next = x_ref[level] * scale_ref[level] + carry_ref[level] * d_prev
        x_ref[level] = d_next
        return d_next

    lax.fori_loop(0, layers, down, zero, unroll=8)
    sweep_up(x_ref, gain_ref, zero)
    for level in range(0, layers, 8):
        warm_ref[level : level + 8, :] = x_ref[level : level + 8].reshape(8, nodes)


def join_kernel(own_ref, below_ref, above_ref, out_ref):
    fields, tile_rows, tile_cols = own_ref.shape
    mid = tile_rows // 2
    low_lane = lax.broadcasted_iota(jnp.int32, (mid, tile_cols), 1) < tile_cols // 2
    for f in range(fields):
        below, above = below_ref[f], above_ref[f]
        out_ref[f, :mid, :] = own_ref[f, :mid, :] + jnp.where(low_lane, below, above)
        out_ref[f, mid:, :] = own_ref[f, mid:, :] + pltpu.roll(
            jnp.where(low_lane, above, below), tile_cols // 2, 1
        )


def cost(flops, moved):
    return pl.CostEstimate(flops=flops, bytes_accessed=moved, transcendentals=0)


def per_device(
    atmosphere_inputs,
    thermal_anomaly,
    mixing_rates,
    adjacency_table,
    lateral_spread_factor,
    sent_vertices,
    corner_parallel,
    corner_longitude,
    corner_share,
    exchange_factor,
    sensitivity_vector,
):
    layers, nodes = thermal_anomaly.shape
    fields, tile_rows, tile_cols = atmosphere_inputs.shape
    columns, each = sent_vertices.shape
    halo = columns * each
    slots = adjacency_table.shape[0]
    window_cols = 2 * tile_cols
    extended = nodes + halo
    upward = [(i, (i + 1) % columns) for i in range(columns)]
    downward = [((i + 1) % columns, i) for i in range(columns)]
    position = lax.axis_index("lon")
    start = ((columns - position) * tile_cols).astype(jnp.int32).reshape(1)

    dense = (layers, nodes // LANES, LANES)
    block = jax.ShapeDtypeStruct(dense, F32)
    rim = (fields, tile_rows // 2, tile_cols)
    (
        scaled,
        xkeep,
        surface,
        gain,
        scale,
        carry,
        merged,
        rank,
        low,
        high,
        node_scale,
        received,
        back,
        other,
        keep,
        adjacency,
        column,
    ) = pl.pallas_call(
        exchange_kernel,
        out_shape=(
            jax.ShapeDtypeStruct((2 * layers, nodes), BF16),
            jax.ShapeDtypeStruct((layers, nodes), F32),
            jax.ShapeDtypeStruct((1, nodes), F32),
            block,
            block,
            block,
            jax.ShapeDtypeStruct((8, nodes), F32),
            jax.ShapeDtypeStruct((8, nodes), F32),
            jax.ShapeDtypeStruct((8 + slots // 2, nodes), F32),
            jax.ShapeDtypeStruct((8 + slots // 2, nodes), F32),
            jax.ShapeDtypeStruct((1, nodes), F32),
            jax.ShapeDtypeStruct((2 * layers, halo), BF16),
            jax.ShapeDtypeStruct((2 * layers, halo), BF16),
            jax.ShapeDtypeStruct(atmosphere_inputs.shape, BF16),
            jax.ShapeDtypeStruct((1, nodes), F32),
            jax.ShapeDtypeStruct((slots, nodes), jnp.int32),
            jax.ShapeDtypeStruct((halo, LANES), F32),
        ),
        in_specs=[pl.BlockSpec(memory_space=pltpu.HBM)] * 7,
        out_specs=tuple(whole(17)),
        scratch_shapes=[
            pltpu.VMEM(dense, F32),
            pltpu.VMEM(dense, F32),
            pltpu.VMEM((halo, 2 * layers), BF16),
            pltpu.VMEM((halo, 2 * layers), BF16),
            pltpu.VMEM((halo, 2 * layers), BF16),
            pltpu.VMEM((halo, 2 * layers), BF16),
            pltpu.VMEM(rim, BF16),
            pltpu.VMEM(rim, BF16),
            pltpu.VMEM(rim, BF16),
            pltpu.VMEM(rim, BF16),
            pltpu.SemaphoreType.DMA((columns,)),
            pltpu.SemaphoreType.DMA((columns,)),
            pltpu.SemaphoreType.DMA((columns,)),
            pltpu.SemaphoreType.DMA((columns,)),
            pltpu.SemaphoreType.DMA((4,)),
            pltpu.VMEM((layers, nodes), F32),
            pltpu.VMEM((layers, nodes), F32),
            pltpu.VMEM((layers, nodes), F32),
            pltpu.VMEM((slots, nodes), jnp.int32),
            pltpu.VMEM((slots, nodes), F32),
            pltpu.VMEM(sent_vertices.shape, jnp.int32),
            pltpu.VMEM(atmosphere_inputs.shape, BF16),
            pltpu.SemaphoreType.DMA((7,)),
        ],
        compiler_params=pltpu.CompilerParams(
            vmem_limit_bytes=47 * MEBI, collective_id=0, has_side_effects=True
        ),
        cost_estimate=cost(layers * nodes * 20, layers * nodes * 24),
        name="exchange",
    )(
        mixing_rates,
        sensitivity_vector,
        thermal_anomaly,
        adjacency_table,
        lateral_spread_factor,
        sent_vertices,
        atmosphere_inputs,
    )

    line = pl.BlockSpec((1, FORCE_TILE), lambda i: (0, i))
    four = pl.BlockSpec((4, FORCE_TILE), lambda i: (0, i))

    def all_of(*shape):
        return pl.BlockSpec(shape, lambda i: (0,) * len(shape))

    flux, corr, own_forcing, up_rim, down_rim = pl.pallas_call(
        forcing_kernel,
        grid=(nodes // FORCE_TILE,),
        out_shape=(
            jax.ShapeDtypeStruct((1, nodes), F32),
            jax.ShapeDtypeStruct((1, nodes), F32),
            jax.ShapeDtypeStruct((fields, tile_rows, tile_cols), F32),
            jax.ShapeDtypeStruct(rim, F32),
            jax.ShapeDtypeStruct(rim, F32),
        ),
        in_specs=[
            pl.BlockSpec(memory_space=pltpu.SMEM),
            pl.BlockSpec(memory_space=pltpu.SMEM),
            all_of(fields, tile_rows, tile_cols),
            all_of(fields, tile_rows, tile_cols),
            four,
            four,
            four,
            line,
            pl.BlockSpec((8, FORCE_TILE), lambda i: (0, i)),
        ],
        out_specs=(
            line,
            line,
            all_of(fields, tile_rows, tile_cols),
            all_of(*rim),
            all_of(*rim),
        ),
        scratch_shapes=[
            pltpu.VMEM((fields * tile_rows, window_cols), BF16),
            pltpu.VMEM((fields, tile_rows, window_cols), F32),
        ],
        compiler_params=pltpu.CompilerParams(vmem_limit_bytes=20 * MEBI),
        cost_estimate=cost(8 * fields * tile_rows * window_cols * nodes, 4000000),
        name="forcing",
    )(
        start,
        exchange_factor,
        atmosphere_inputs,
        other,
        corner_parallel,
        corner_longitude,
        corner_share,
        surface,
        thermal_anomaly,
    )
    below = lax.ppermute(up_rim, "lon", upward)
    above = lax.ppermute(down_rim, "lon", downward)

    updated_warmth, temp_grad = pl.pallas_call(
        lateral_kernel,
        out_shape=(
            jax.ShapeDtypeStruct((layers, nodes), F32),
            jax.ShapeDtypeStruct((layers, nodes), F32),
        ),
        in_specs=whole(18),
        out_specs=tuple(whole(2)),
        scratch_shapes=[
            pltpu.VMEM((layers, nodes), F32),
            pltpu.VMEM(dense, F32),
            pltpu.VMEM((2 * layers, extended), BF16),
            pltpu.VMEM((4, SLOT_ROWS, NODE_TILE), BF16),
            pltpu.VMEM((4, SLOT_ROWS, NODE_TILE), BF16),
            pltpu.VMEM((2 * layers, NODE_TILE), F32),
            pltpu.VMEM((2 * layers, NODE_TILE), F32),
            pltpu.VMEM((NODE_TILE, nodes), BF16),
            pltpu.VMEM((NODE_TILE, nodes), BF16),
            pltpu.SMEM((nodes // NODE_TILE,), jnp.int32),
        ],
        compiler_params=pltpu.CompilerParams(vmem_limit_bytes=32 * MEBI),
        cost_estimate=cost(8 * layers * nodes * extended, 8000000),
        name="lateral",
    )(
        adjacency,
        merged,
        rank,
        low,
        high,
        node_scale,
        keep,
        thermal_anomaly,
        received,
        scaled,
        xkeep,
        back,
        column,
        flux,
        corr,
        gain,
        scale,
        carry,
    )

    forcing_grad = pl.pallas_call(
        join_kernel,
        out_shape=jax.ShapeDtypeStruct((fields, tile_rows, tile_cols), F32),
        in_specs=whole(3),
        out_specs=pl.BlockSpec(memory_space=pltpu.VMEM),
        compiler_params=pltpu.CompilerParams(vmem_limit_bytes=8 * MEBI),
        cost_estimate=cost(fields * tile_rows * tile_cols, 2000000),
        name="join",
    )(own_forcing, below, above)
    return (updated_warmth, temp_grad, forcing_grad)


def solution(mesh):
    nodes = P(None, ("lat", "lon"))
    placed = (
        P(None, "lat", "lon"),
        nodes,
        nodes,
        nodes,
        nodes,
        P(("lat", "lon"), None),
        nodes,
        nodes,
        nodes,
        P(),
        nodes,
    )
    return jax.shard_map(
        per_device,
        mesh=mesh,
        in_specs=placed,
        out_specs=(nodes, nodes, P(None, "lat", "lon")),
        check_vma=False,
    )
```

```python
import functools

import jax
import jax.numpy as jnp
from jax import lax
from jax.experimental import pallas as pl
from jax.experimental.pallas import tpu as pltpu
from jax.sharding import PartitionSpec as P

F32 = jnp.float32
BF16 = jnp.bfloat16
MEBI = 1024 * 1024
LANES = 128
SLOT_ROWS = 256
NODE_TILE = 256
FORCE_TILE = 512
EARLY_PAIRS = 3
LANE_CONTRACT = (((1,), (1,)), ((), ()))
MESH = pl.DeviceIdType.MESH


def whole(count):
    return [pl.BlockSpec(memory_space=pltpu.VMEM)] * count


def halves(value):
    high = value.astype(BF16)
    return high, (value - high.astype(F32)).astype(BF16)


def spread_levels(source_ref, dense_ref):
    layers = dense_ref.shape[0]
    for level in range(0, layers, 8):
        dense_ref[level : level + 8] = source_ref[level : level + 8, :].reshape(
            (8,) + dense_ref.shape[1:]
        )


def sweep_up(x_ref, gain_ref, zero):
    layers = x_ref.shape[0]

    def up(step, x_next):
        level = layers - 1 - step
        x_here = x_ref[level] + gain_ref[level] * x_next
        x_ref[level] = x_here
        return x_here

    lax.fori_loop(0, layers, up, zero, unroll=8)


def best_scale(values, count):
    trial = lax.broadcasted_iota(jnp.int32, (count, values[0].shape[1]), 0).astype(F32)
    trial = 1.0 + trial * (1.0 / count)
    inverse = 1.0 / trial
    miss = jnp.zeros_like(trial)
    for value in values:
        gap = (value * inverse).astype(BF16).astype(F32) * trial - value
        miss = miss + gap * gap
    least = jnp.min(miss, axis=0, keepdims=True)
    return jnp.max(jnp.where(miss == least, trial, 1.0), axis=0, keepdims=True)


def slot_weights(adj_ref, merged_ref, cols, first_row, rank_ref=None):
    row = lax.broadcasted_iota(jnp.int32, (SLOT_ROWS, NODE_TILE), 0).astype(F32).astype(BF16)
    local = adj_ref[:, cols] - first_row
    if rank_ref is not None:
        rank = rank_ref[: adj_ref.shape[0], cols]
        local = jnp.where(jnp.logical_and(rank >= 0.0, rank <= 1.0), local, -1)
    local = local.astype(F32).astype(BF16)
    share = merged_ref[:, cols].astype(BF16)
    weights = jnp.zeros((SLOT_ROWS, NODE_TILE), BF16)
    for k in range(adj_ref.shape[0]):
        weights = jnp.where(row == local[k : k + 1, :], share[k : k + 1, :], weights)
    return weights


def slot_ids(adj_ref):
    slots, nodes = adj_ref.shape
    at = lax.broadcasted_iota(jnp.int32, (8, nodes), 0)
    spare = lax.broadcasted_iota(jnp.int32, (8 - slots, nodes), 0) - (8 - slots)
    return jnp.concatenate([adj_ref[...], spare], 0), at


def merge_slots(adj_ref, coef_ref, merged_ref):
    slots, nodes = adj_ref.shape
    ids, _ = slot_ids(adj_ref)
    coef = jnp.concatenate([coef_ref[...], jnp.zeros((8 - slots, nodes), F32)], 0)
    merged = coef
    for shift in range(1, 8):
        equal = ids == pltpu.roll(ids, shift, 0)
        merged = merged + jnp.where(equal, pltpu.roll(coef, shift, 0), 0.0)
    merged_ref[...] = merged


def rank_slots(adj_ref, rank_ref, low_ref, high_ref):
    slots, nodes = adj_ref.shape
    ids, at = slot_ids(adj_ref)
    low = (ids & (SLOT_ROWS - 1)).astype(F32)
    high = (ids >> (SLOT_ROWS.bit_length() - 1)).astype(F32)
    repeat = jnp.zeros((8, nodes), F32)
    for shift in range(1, slots):
        equal = ids == pltpu.roll(ids, shift, 0)
        repeat = jnp.where(jnp.logical_and(equal, at >= shift), 1.0, repeat)
    rank = jnp.zeros((8, nodes), F32)
    for shift in range(1, slots):
        met = jnp.logical_and(low == pltpu.roll(low, shift, 0), at >= shift)
        rank = rank + jnp.where(met, 1.0 - pltpu.roll(repeat, shift, 0), 0.0)
    rank = jnp.where(jnp.logical_or(repeat > 0.0, at >= slots), -1.0, rank)
    place = jnp.zeros((8, nodes), F32)
    for shift in range(1, slots):
        second = jnp.logical_and(pltpu.roll(rank, shift, 0) == 1.0, at >= shift)
        place = place + jnp.where(second, 1.0, 0.0)
    rank_ref[...] = rank
    low_ref[:8, :] = jnp.where(rank == 0.0, low, -1.0)
    high_ref[:8, :] = high
    for j in range(slots // 2):
        here = jnp.logical_and(rank == 1.0, place == float(j))
        low_ref[8 + j : 9 + j, :] = jnp.max(jnp.where(here, low, -1.0), axis=0, keepdims=True)
        high_ref[8 + j : 9 + j, :] = jnp.max(jnp.where(here, high, -1.0), axis=0, keepdims=True)


def sent_column(sent_ref, column_ref):
    parts, each = sent_ref.shape
    padded = jnp.concatenate(
        [sent_ref[...].astype(F32), jnp.zeros((parts, LANES - each), F32)], 1
    ).T
    for part in range(parts):
        column_ref[part * each : (part + 1) * each, :] = jnp.broadcast_to(
            padded[:each, part : part + 1], (each, LANES)
        )


def chosen_rows(column_ref, first_node):
    local = (column_ref[...] - first_node).astype(BF16)
    lane = lax.broadcasted_iota(jnp.int32, local.shape, 1).astype(F32)
    zero = jnp.zeros(local.shape, BF16)
    one = jnp.ones(local.shape, BF16)
    pieces = [
        jnp.where(local == (lane + float(start)).astype(BF16), one, zero)
        for start in range(0, NODE_TILE, LANES)
    ]
    return jnp.concatenate(pieces, 1)


def key_writer(cols, tables, keys_ref):
    merged_ref, rank_ref, low_ref, high_ref = tables
    rank = rank_ref[:, cols]
    merged = merged_ref[:, cols]
    low = low_ref[:, cols].astype(BF16)
    high = high_ref[:, cols].astype(BF16)
    share = merged.astype(BF16)
    pairs = low.shape[0] - 8
    place = jnp.zeros((1, NODE_TILE), F32)
    seconds = [jnp.zeros((1, NODE_TILE), F32)] * pairs
    for k in range(1, 2 * pairs):
        here = rank[k : k + 1] == 1.0
        for j in range(pairs):
            mine = jnp.logical_and(here, place == float(j))
            seconds[j] = jnp.where(mine, merged[k : k + 1], seconds[j])
        place = place + jnp.where(here, 1.0, 0.0)
    seconds = [second.astype(BF16) for second in seconds]

    def write(first):
        row = lax.broadcasted_iota(jnp.int32, (16, NODE_TILE), 0).astype(F32).astype(BF16)
        row = row + float(first)
        none = jnp.full((16, NODE_TILE), -1.0, BF16)
        zero = jnp.zeros((16, NODE_TILE), BF16)
        key, val = none, zero
        for k in range(2 * pairs):
            mine = row == low[k : k + 1]
            key = jnp.where(mine, high[k : k + 1], key)
            val = jnp.where(mine, share[k : k + 1], val)
        keys_ref[0, first : first + 16, :] = key
        keys_ref[1, first : first + 16, :] = val
        key, val = none, zero
        for j in range(pairs):
            mine = row == low[8 + j : 9 + j]
            key = jnp.where(mine, high[8 + j : 9 + j], key)
            val = jnp.where(mine, seconds[j], val)
        keys_ref[2, first : first + 16, :] = key
        keys_ref[3, first : first + 16, :] = val

    return write


def block_weights(keys_ref, blocks):
    key0, val0, key1, val1 = (keys_ref[i] for i in range(4))
    found = []
    for block in blocks:
        weights = jnp.where(key0 == float(block), val0, jnp.zeros_like(val0))
        found.append(jnp.where(key1 == float(block), val1, weights))
    return found


def node_cols(tile):
    start = tile * NODE_TILE
    if not isinstance(start, int):
        start = pl.multiple_of(start, NODE_TILE)
    return pl.ds(start, NODE_TILE)


def apply_tiles(first, end, rows, tables, fields, scratch):
    ext_ref, scaled_ref, thermal_ref, keep_ref, node_scale_ref, rhs_ref, grad_ref = fields
    even_ref, odd_ref, even_sum_ref, odd_sum_ref, even_turned_ref, odd_turned_ref = scratch
    layers, nodes = thermal_ref.shape
    tiles = nodes // NODE_TILE

    def use(tile, keys_ref, next_keys_ref, sum_ref, turned_ref):
        write = key_writer(node_cols(jnp.minimum(tile + 1, tiles - 1)), tables, next_keys_ref)
        cols = node_cols(tile)
        scaled = scaled_ref[:, cols]
        groups = SLOT_ROWS // 16
        done = 0
        blocks = rows // SLOT_ROWS
        for start in range(0, blocks, 2):
            now = range(start, min(start + 2, blocks))
            for block, weights in zip(now, block_weights(keys_ref, now)):
                here = slice(block * SLOT_ROWS, (block + 1) * SLOT_ROWS)
                part = jnp.dot(ext_ref[:, here], weights, preferred_element_type=F32)
                if block == 0:
                    sum_ref[...] = part
                else:
                    sum_ref[...] += part
                if block * SLOT_ROWS < nodes:
                    turned_ref[:, here] = weights.T
                    part = jnp.dot(scaled, turned_ref[:, here], preferred_element_type=F32)
                    grad_ref[:, here] += part[:layers] + part[layers:]
            until = min(groups, -(-groups * now[-1] // (nodes // SLOT_ROWS - 1)))
            for group in range(done, until):
                write(group * 16)
            done = until
        rhs_ref[:, cols] = (
            thermal_ref[:, cols] * keep_ref[:, cols]
            + (sum_ref[:layers, :] + sum_ref[layers:, :]) * node_scale_ref[:, cols]
        )

    write = key_writer(node_cols(2 * first), tables, even_ref)
    for group in range(SLOT_ROWS // 16):
        write(group * 16)

    def pair(step, carry):
        use(2 * step, even_ref, odd_ref, even_sum_ref, even_turned_ref)
        use(2 * step + 1, odd_ref, even_ref, odd_sum_ref, odd_turned_ref)
        return carry

    lax.fori_loop(first, end, pair, 0)


def exchange_kernel(
    mix_hbm,
    sens_hbm,
    thermal_hbm,
    adj_hbm,
    coef_hbm,
    sent_hbm,
    atm_hbm,
    scaled_ref,
    grad_ref,
    rhs_ref,
    surface_ref,
    gain_ref,
    scale_ref,
    carry_ref,
    merged_ref,
    rank_ref,
    low_ref,
    high_ref,
    node_scale_ref,
    ext_ref,
    back_ref,
    other_ref,
    keep_ref,
    adj_out_ref,
    column_ref,
    mix3_ref,
    x_ref,
    depart_buf,
    received_buf,
    hgrad_buf,
    back_buf,
    right_buf,
    left_buf,
    from_left_buf,
    from_right_buf,
    send_sem,
    recv_sem,
    gsend_sem,
    grecv_sem,
    rim_sem,
    mix_ref,
    sens_ref,
    thermal_ref,
    adj_ref,
    coef_ref,
    sent_ref,
    atm_ref,
    load_sem,
    even_ref,
    odd_ref,
    even_sum_ref,
    odd_sum_ref,
    even_turned_ref,
    odd_turned_ref,
):
    load = {}
    sources = (
        ("adj", adj_hbm, adj_ref),
        ("coef", coef_hbm, coef_ref),
        ("mix", mix_hbm, mix_ref),
        ("sens", sens_hbm, sens_ref),
        ("atm", atm_hbm, atm_ref),
        ("sent", sent_hbm, sent_ref),
        ("thermal", thermal_hbm, thermal_ref),
    )
    for index, (name, source, target) in enumerate(sources):
        load[name] = pltpu.make_async_copy(source, target, load_sem.at[index])
        load[name].start()
    layers, nodes = mix_ref.shape
    slots = adj_ref.shape[0]
    parts, each = sent_ref.shape
    halo = parts * each
    fields, tile_rows, tile_cols = atm_ref.shape
    mid = tile_rows // 2
    me = lax.axis_index("lon")
    ahead = lax.rem(me + 1, parts)
    behind = lax.rem(me + parts - 1, parts)

    barrier = pltpu.get_barrier_semaphore()
    for off in range(1, parts):
        pl.semaphore_signal(
            barrier, inc=1, device_id={"lon": lax.rem(me + off, parts)}, device_id_type=MESH
        )

    load["adj"].wait()
    load["coef"].wait()
    merge_slots(adj_ref, coef_ref, merged_ref)

    def fit(step, carry):
        cols = pl.ds(pl.multiple_of(step * NODE_TILE, NODE_TILE), NODE_TILE)
        merged = [merged_ref[k : k + 1, cols] for k in range(slots)]
        scale = best_scale(merged, 32)
        node_scale_ref[:, cols] = scale
        merged_ref[:, cols] = merged_ref[:, cols] / scale
        return carry

    lax.fori_loop(0, nodes // NODE_TILE, fit, 0)

    zero = jnp.zeros(x_ref.shape[1:], F32)
    load["mix"].wait()
    load["sens"].wait()
    spread_levels(mix_ref, mix3_ref)
    spread_levels(sens_ref, x_ref)

    def down(level, state):
        mix_prev, gain_prev, d_prev = state
        mix = mix3_ref[level]
        scale = 1.0 / (1.0 + mix + mix_prev * (1.0 - gain_prev))
        gain = mix * scale
        carry = mix_prev * scale
        d_next = x_ref[level] * scale + carry * d_prev
        gain_ref[level] = gain
        scale_ref[level] = scale
        carry_ref[level] = carry
        x_ref[level] = d_next
        return mix, gain, d_next

    lax.fori_loop(0, layers, down, (zero, zero, zero), unroll=4)
    sweep_up(x_ref, gain_ref, zero)
    keep = 1.0 - jnp.sum(coef_ref[...], axis=0, keepdims=True)
    keep_ref[...] = keep
    for level in range(0, layers, 16):
        flat = x_ref[level : level + 16].reshape(16, nodes)
        if level == 0:
            surface_ref[...] = flat[0:1]
        grad_ref[level : level + 16, :] = flat * keep
        high, low = halves(flat * node_scale_ref[...])
        scaled_ref[level : level + 16, :] = high
        scaled_ref[layers + level : layers + level + 16, :] = low

    load["atm"].wait()
    low_lane = lax.broadcasted_iota(jnp.int32, (mid, tile_cols), 1) < tile_cols // 2
    for f in range(fields):
        upper = atm_ref[f, :mid, :].astype(F32)
        lower = pltpu.roll(atm_ref[f, mid:, :].astype(F32), tile_cols // 2, 1)
        right_buf[f] = jnp.where(low_lane, lower, upper).astype(BF16)
        left_buf[f] = jnp.where(low_lane, upper, lower).astype(BF16)

    load["sent"].wait()
    load["thermal"].wait()
    sent_column(sent_ref, column_ref)
    depart = jnp.zeros((halo, 2 * layers), F32)
    tile = 1024

    def pick(step, total):
        cols = pl.ds(pl.multiple_of(step * tile, tile), tile)
        high, low = halves(thermal_ref[:, cols])
        ext = jnp.concatenate([high, low], 0)
        first = (step * tile).astype(F32)
        chosen = jnp.concatenate(
            [chosen_rows(column_ref, first + float(at)) for at in range(0, tile, NODE_TILE)], 1
        )
        return total + lax.dot_general(
            chosen, ext, LANE_CONTRACT, preferred_element_type=F32
        )

    depart = lax.fori_loop(0, nodes // tile, pick, depart)
    depart_buf[...] = depart.astype(BF16)

    pl.semaphore_wait(barrier, parts - 1)

    def rim_copy(source, target, index, to):
        return pltpu.make_async_remote_copy(
            src_ref=source,
            dst_ref=target,
            send_sem=rim_sem.at[index],
            recv_sem=rim_sem.at[2 + index],
            device_id={"lon": to},
            device_id_type=MESH,
        )

    rims = [
        rim_copy(right_buf, from_left_buf, 0, ahead),
        rim_copy(left_buf, from_right_buf, 1, behind),
    ]
    for copy in rims:
        copy.start()

    def rows_of(part):
        return pl.ds(pl.multiple_of(part * each, each), each)

    def halo_copies(source, target, sends, recvs):
        copies = []
        for off in range(1, parts):
            peer = lax.rem(me + off, parts)
            copies.append(
                pltpu.make_async_remote_copy(
                    src_ref=source.at[rows_of(peer)],
                    dst_ref=target.at[rows_of(me)],
                    send_sem=sends.at[off],
                    recv_sem=recvs.at[off],
                    device_id={"lon": peer},
                    device_id_type=MESH,
                )
            )
        return copies

    def own_copy(source, target, sem):
        return pltpu.make_async_copy(source.at[rows_of(me)], target.at[rows_of(me)], sem)

    there = halo_copies(depart_buf, received_buf, send_sem, recv_sem)
    for copy in there:
        copy.start()
    mine = own_copy(depart_buf, received_buf, send_sem.at[0])
    mine.start()

    for block in range(halo // SLOT_ROWS):

        def collect(step, total):
            cols = pl.ds(pl.multiple_of(step * NODE_TILE, NODE_TILE), NODE_TILE)
            weights = slot_weights(adj_ref, merged_ref, cols, nodes + block * SLOT_ROWS)
            return total + lax.dot_general(
                scaled_ref[:, cols], weights, LANE_CONTRACT, preferred_element_type=F32
            )

        total = lax.fori_loop(
            0, nodes // NODE_TILE, collect, jnp.zeros((2 * layers, SLOT_ROWS), F32)
        )
        high, low = halves(total[:layers] + total[layers:])
        both = jnp.concatenate([high.astype(F32), low.astype(F32)], 0)
        hgrad_buf[block * SLOT_ROWS : (block + 1) * SLOT_ROWS, :] = both.T.astype(BF16)

    home = halo_copies(hgrad_buf, back_buf, gsend_sem, grecv_sem)
    for copy in home:
        copy.start()
    mine_back = own_copy(hgrad_buf, back_buf, gsend_sem.at[0])
    mine_back.start()
    rank_slots(adj_ref, rank_ref, low_ref, high_ref)
    adj_out_ref[...] = adj_ref[...]

    high, low = halves(thermal_ref[...])
    ext_ref[:layers, :nodes] = high
    ext_ref[layers:, :nodes] = low
    early = nodes // NODE_TILE // 2 * EARLY_PAIRS // 8
    apply_tiles(
        0,
        early,
        nodes,
        (merged_ref, rank_ref, low_ref, high_ref),
        (ext_ref, scaled_ref, thermal_ref, keep_ref, node_scale_ref, rhs_ref, grad_ref),
        (even_ref, odd_ref, even_sum_ref, odd_sum_ref, even_turned_ref, odd_turned_ref),
    )

    mine.wait()
    for copy in there:
        copy.wait()
    ext_ref[:, nodes:] = received_buf[...].astype(F32).T.astype(BF16)
    for block in range(halo // SLOT_ROWS):
        first = nodes + block * SLOT_ROWS

        def arrive(tile, carry):
            cols = node_cols(tile)
            weights = slot_weights(adj_ref, merged_ref, cols, first, rank_ref)
            part = jnp.dot(
                ext_ref[:, first : first + SLOT_ROWS], weights, preferred_element_type=F32
            )
            rhs_ref[:, cols] += (part[:layers] + part[layers:]) * node_scale_ref[:, cols]
            return carry

        lax.fori_loop(0, 2 * early, arrive, 0)

    for copy in rims:
        copy.wait()
    for f in range(fields):
        right = from_right_buf[f].astype(F32)
        left = from_left_buf[f].astype(F32)
        other_ref[f, :mid, :] = jnp.where(low_lane, right, left).astype(BF16)
        other_ref[f, mid:, :] = pltpu.roll(
            jnp.where(low_lane, left, right), tile_cols // 2, 1
        ).astype(BF16)

    mine_back.wait()
    for copy in home:
        copy.wait()
    back_ref[...] = back_buf[...].astype(F32).T.astype(BF16)


def forcing_kernel(
    start_ref,
    factor_ref,
    atm_ref,
    other_ref,
    row_ref,
    col_ref,
    share_ref,
    surface_ref,
    thermal_ref,
    flux_ref,
    corr_ref,
    own_ref,
    up_ref,
    down_ref,
    window_ref,
    grad_ref,
):
    fields, tile_rows, window_cols = grad_ref.shape
    tile_cols = window_cols // 2
    mid = tile_rows // 2
    tile = row_ref.shape[1]

    @pl.when(pl.program_id(0) == 0)
    def _():
        grad_ref[...] = jnp.zeros_like(grad_ref)
        window_ref[:, :tile_cols] = atm_ref[...].reshape(fields * tile_rows, tile_cols)
        window_ref[:, tile_cols:] = other_ref[...].reshape(fields * tile_rows, tile_cols)

    share = share_ref[...]
    row_low = share[0:1] + share[2:3]
    row_high = share[1:2] + share[3:4]
    col_low = share[0:1] + share[1:2]
    col_high = share[2:3] + share[3:4]
    scale = best_scale([col_low, col_high], 64)
    col_low = col_low / scale
    col_high = col_high / scale
    base_row = row_ref[0:1, :]
    base_col = lax.rem(col_ref[0:1, :] + start_ref[0], window_cols)
    next_col = lax.rem(base_col + 1, window_cols)
    row_at = lax.broadcasted_iota(jnp.int32, (tile_rows, tile), 0)
    col_at = lax.broadcasted_iota(jnp.int32, (window_cols, tile), 0)
    rows = jnp.where(
        row_at == base_row, row_low, jnp.where(row_at == base_row + 1, row_high, 0.0)
    )
    cols = jnp.where(
        col_at == base_col, col_low, jnp.where(col_at == next_col, col_high, 0.0)
    )
    cols = cols.astype(BF16)
    rows = rows * scale
    mixed = jnp.dot(window_ref[...], cols, preferred_element_type=F32)
    forced = [
        jnp.sum(mixed[f * tile_rows : (f + 1) * tile_rows] * rows, axis=0, keepdims=True)
        for f in range(fields)
    ]
    wind = jnp.sqrt(forced[0] * forced[0] + forced[1] * forced[1] + 1.0)
    excess = forced[2] - thermal_ref[0:1, :]
    flux = 0.1 * wind * excess
    for f in range(fields):
        flux = flux + factor_ref[f] * forced[f]
    flux_ref[...] = flux
    surface = surface_ref[...]
    corr_ref[...] = -0.1 * surface * wind
    quotient = surface * (0.1 * excess / wind)
    dot = functools.partial(
        lax.dot_general,
        dimension_numbers=LANE_CONTRACT,
        preferred_element_type=F32,
    )
    row_is = row_at.astype(F32).astype(BF16)
    base_is = base_row.astype(F32).astype(BF16)
    at_low = row_is == base_is
    at_high = row_is == base_is + 1.0
    none = jnp.zeros(row_is.shape, BF16)
    ends = [row_low * scale, row_high * scale]
    lefts = []
    for f in range(fields):
        node_grad = surface * factor_ref[f]
        if f < 2:
            node_grad = node_grad + quotient * forced[f]
        if f == 2:
            node_grad = node_grad + 0.1 * surface * wind
        below, above = (halves(node_grad * end) for end in ends)
        lefts.append(
            [
                jnp.where(at_low, low_end, jnp.where(at_high, high_end, none))
                for low_end, high_end in zip(below, above)
            ]
        )
    left_hi = jnp.concatenate([high for high, _ in lefts], 0)
    left_lo = jnp.concatenate([low for _, low in lefts], 0)
    grad = dot(left_hi, cols) + dot(left_lo, cols)
    grad_ref[...] += grad.reshape(fields, tile_rows, window_cols)

    @pl.when(pl.program_id(0) == pl.num_programs(0) - 1)
    def _():
        low_lane = lax.broadcasted_iota(jnp.int32, (mid, tile_cols), 1) < tile_cols // 2
        for f in range(fields):
            own_ref[f] = grad_ref[f, :, :tile_cols]
            upper = grad_ref[f, :mid, tile_cols:]
            lower = pltpu.roll(grad_ref[f, mid:, tile_cols:], tile_cols // 2, 1)
            up_ref[f] = jnp.where(low_lane, upper, lower)
            down_ref[f] = jnp.where(low_lane, lower, upper)


def lateral_kernel(
    adj_ref,
    merged_ref,
    rank_ref,
    low_ref,
    high_ref,
    node_scale_ref,
    keep_ref,
    thermal_ref,
    ext_ref,
    scaled_ref,
    begun_grad_ref,
    begun_rhs_ref,
    back_ref,
    column_ref,
    flux_ref,
    corr_ref,
    gain_ref,
    scale_ref,
    carry_ref,
    warm_ref,
    grad_ref,
    rhs_ref,
    x_ref,
    even_ref,
    odd_ref,
    even_sum_ref,
    odd_sum_ref,
    even_turned_ref,
    odd_turned_ref,
    deep_ref,
):
    slots, nodes = adj_ref.shape
    layers = rhs_ref.shape[0]
    tiles = nodes // NODE_TILE
    tables = merged_ref, rank_ref, low_ref, high_ref

    def deep_block(tile, bound):
        cols = node_cols(tile)
        high = (adj_ref[:, cols] >> (SLOT_ROWS.bit_length() - 1)).astype(F32)
        deep = jnp.logical_and(rank_ref[:slots, cols] > 1.0, high < bound)
        return jnp.max(jnp.where(deep, high, -1.0)).astype(jnp.int32)

    for tile in range(tiles):
        deep_ref[tile] = deep_block(tile, float(ext_ref.shape[1]))
    start_pair = tiles // 2 * EARLY_PAIRS // 8
    begun = start_pair * 2 * NODE_TILE
    rhs_ref[:, :begun] = begun_rhs_ref[:, :begun]
    grad_ref[...] = begun_grad_ref[...]
    fields_of_tile = (
        ext_ref, scaled_ref, thermal_ref, keep_ref, node_scale_ref, rhs_ref, grad_ref
    )
    scratch = even_ref, odd_ref, even_sum_ref, odd_sum_ref, even_turned_ref, odd_turned_ref

    def mend(tile):
        def one_block(block):
            cols = node_cols(tile)
            here = pl.ds(pl.multiple_of(block * SLOT_ROWS, SLOT_ROWS), SLOT_ROWS)
            local = jnp.where(
                rank_ref[:slots, cols] > 1.0, adj_ref[:, cols] - block * SLOT_ROWS, -1
            )
            local = local.astype(F32).astype(BF16)
            share = merged_ref[:slots, cols].astype(BF16)
            row = lax.broadcasted_iota(jnp.int32, (SLOT_ROWS, NODE_TILE), 0)
            row = row.astype(F32).astype(BF16)
            weights = jnp.zeros((SLOT_ROWS, NODE_TILE), BF16)
            for k in range(2, slots):
                weights = jnp.where(row == local[k : k + 1], share[k : k + 1], weights)
            part = jnp.dot(ext_ref[:, here], weights, preferred_element_type=F32)
            rhs_ref[:, cols] += (part[:layers] + part[layers:]) * node_scale_ref[:, cols]

            @pl.when(block * SLOT_ROWS < nodes)
            def _():
                part = lax.dot_general(
                    scaled_ref[:, cols], weights, LANE_CONTRACT, preferred_element_type=F32
                )
                grad_ref[:, here] += part[:layers] + part[layers:]

            return deep_block(tile, block.astype(F32))

        lax.while_loop(lambda block: block >= 0, one_block, deep_ref[tile])

    apply_tiles(start_pair, tiles // 2, ext_ref.shape[1], tables, fields_of_tile, scratch)

    def fix(tile, carry):
        mend(tile)
        return carry

    lax.fori_loop(0, tiles, fix, 0)

    width = 4 * NODE_TILE

    def give_back(step, carry):
        cols = pl.ds(pl.multiple_of(step * width, width), width)
        first = (step * width).astype(F32)
        chosen = jnp.concatenate(
            [chosen_rows(column_ref, first + float(at)) for at in range(0, width, NODE_TILE)], 1
        )
        part = jnp.dot(back_ref[...], chosen, preferred_element_type=F32)
        grad_ref[:, cols] += part[:layers] + part[layers:]
        return carry

    lax.fori_loop(0, nodes // width, give_back, 0)
    grad_ref[0:1, :] += corr_ref[...]

    rhs_ref[0:1, :] += flux_ref[...]
    zero = jnp.zeros(x_ref.shape[1:], F32)
    spread_levels(rhs_ref, x_ref)

    def down(level, d_prev):
        d_next = x_ref[level] * scale_ref[level] + carry_ref[level] * d_prev
        x_ref[level] = d_next
        return d_next

    lax.fori_loop(0, layers, down, zero, unroll=8)
    sweep_up(x_ref, gain_ref, zero)
    for level in range(0, layers, 8):
        warm_ref[level : level + 8, :] = x_ref[level : level + 8].reshape(8, nodes)


def join_kernel(own_ref, below_ref, above_ref, out_ref):
    fields, tile_rows, tile_cols = own_ref.shape
    mid = tile_rows // 2
    low_lane = lax.broadcasted_iota(jnp.int32, (mid, tile_cols), 1) < tile_cols // 2
    for f in range(fields):
        below, above = below_ref[f], above_ref[f]
        out_ref[f, :mid, :] = own_ref[f, :mid, :] + jnp.where(low_lane, below, above)
        out_ref[f, mid:, :] = own_ref[f, mid:, :] + pltpu.roll(
            jnp.where(low_lane, above, below), tile_cols // 2, 1
        )


def cost(flops, moved):
    return pl.CostEstimate(flops=flops, bytes_accessed=moved, transcendentals=0)


def per_device(
    atmosphere_inputs,
    thermal_anomaly,
    mixing_rates,
    adjacency_table,
    lateral_spread_factor,
    sent_vertices,
    corner_parallel,
    corner_longitude,
    corner_share,
    exchange_factor,
    sensitivity_vector,
):
    layers, nodes = thermal_anomaly.shape
    fields, tile_rows, tile_cols = atmosphere_inputs.shape
    columns, each = sent_vertices.shape
    halo = columns * each
    slots = adjacency_table.shape[0]
    window_cols = 2 * tile_cols
    extended = nodes + halo
    upward = [(i, (i + 1) % columns) for i in range(columns)]
    downward = [((i + 1) % columns, i) for i in range(columns)]
    position = lax.axis_index("lon")
    start = ((columns - position) * tile_cols).astype(jnp.int32).reshape(1)

    dense = (layers, nodes // LANES, LANES)
    block = jax.ShapeDtypeStruct(dense, F32)
    rim = (fields, tile_rows // 2, tile_cols)
    (
        scaled,
        begun_grad,
        begun_rhs,
        surface,
        gain,
        scale,
        carry,
        merged,
        rank,
        low,
        high,
        node_scale,
        ext,
        back,
        other,
        keep,
        adjacency,
        column,
    ) = pl.pallas_call(
        exchange_kernel,
        out_shape=(
            jax.ShapeDtypeStruct((2 * layers, nodes), BF16),
            jax.ShapeDtypeStruct((layers, nodes), F32),
            jax.ShapeDtypeStruct((layers, nodes), F32),
            jax.ShapeDtypeStruct((1, nodes), F32),
            block,
            block,
            block,
            jax.ShapeDtypeStruct((8, nodes), F32),
            jax.ShapeDtypeStruct((8, nodes), F32),
            jax.ShapeDtypeStruct((8 + slots // 2, nodes), F32),
            jax.ShapeDtypeStruct((8 + slots // 2, nodes), F32),
            jax.ShapeDtypeStruct((1, nodes), F32),
            jax.ShapeDtypeStruct((2 * layers, extended), BF16),
            jax.ShapeDtypeStruct((2 * layers, halo), BF16),
            jax.ShapeDtypeStruct(atmosphere_inputs.shape, BF16),
            jax.ShapeDtypeStruct((1, nodes), F32),
            jax.ShapeDtypeStruct((slots, nodes), jnp.int32),
            jax.ShapeDtypeStruct((halo, LANES), F32),
        ),
        in_specs=[pl.BlockSpec(memory_space=pltpu.HBM)] * 7,
        out_specs=tuple(whole(18)),
        scratch_shapes=[
            pltpu.VMEM(dense, F32),
            pltpu.VMEM(dense, F32),
            pltpu.VMEM((halo, 2 * layers), BF16),
            pltpu.VMEM((halo, 2 * layers), BF16),
            pltpu.VMEM((halo, 2 * layers), BF16),
            pltpu.VMEM((halo, 2 * layers), BF16),
            pltpu.VMEM(rim, BF16),
            pltpu.VMEM(rim, BF16),
            pltpu.VMEM(rim, BF16),
            pltpu.VMEM(rim, BF16),
            pltpu.SemaphoreType.DMA((columns,)),
            pltpu.SemaphoreType.DMA((columns,)),
            pltpu.SemaphoreType.DMA((columns,)),
            pltpu.SemaphoreType.DMA((columns,)),
            pltpu.SemaphoreType.DMA((4,)),
            pltpu.VMEM((layers, nodes), F32),
            pltpu.VMEM((layers, nodes), F32),
            pltpu.VMEM((layers, nodes), F32),
            pltpu.VMEM((slots, nodes), jnp.int32),
            pltpu.VMEM((slots, nodes), F32),
            pltpu.VMEM(sent_vertices.shape, jnp.int32),
            pltpu.VMEM(atmosphere_inputs.shape, BF16),
            pltpu.SemaphoreType.DMA((7,)),
            pltpu.VMEM((4, SLOT_ROWS, NODE_TILE), BF16),
            pltpu.VMEM((4, SLOT_ROWS, NODE_TILE), BF16),
            pltpu.VMEM((2 * layers, NODE_TILE), F32),
            pltpu.VMEM((2 * layers, NODE_TILE), F32),
            pltpu.VMEM((NODE_TILE, nodes), BF16),
            pltpu.VMEM((NODE_TILE, nodes), BF16),
        ],
        compiler_params=pltpu.CompilerParams(
            vmem_limit_bytes=47 * MEBI, collective_id=0, has_side_effects=True
        ),
        cost_estimate=cost(layers * nodes * 20, layers * nodes * 24),
        name="exchange",
    )(
        mixing_rates,
        sensitivity_vector,
        thermal_anomaly,
        adjacency_table,
        lateral_spread_factor,
        sent_vertices,
        atmosphere_inputs,
    )

    line = pl.BlockSpec((1, FORCE_TILE), lambda i: (0, i))
    four = pl.BlockSpec((4, FORCE_TILE), lambda i: (0, i))

    def all_of(*shape):
        return pl.BlockSpec(shape, lambda i: (0,) * len(shape))

    flux, corr, own_forcing, up_rim, down_rim = pl.pallas_call(
        forcing_kernel,
        grid=(nodes // FORCE_TILE,),
        out_shape=(
            jax.ShapeDtypeStruct((1, nodes), F32),
            jax.ShapeDtypeStruct((1, nodes), F32),
            jax.ShapeDtypeStruct((fields, tile_rows, tile_cols), F32),
            jax.ShapeDtypeStruct(rim, F32),
            jax.ShapeDtypeStruct(rim, F32),
        ),
        in_specs=[
            pl.BlockSpec(memory_space=pltpu.SMEM),
            pl.BlockSpec(memory_space=pltpu.SMEM),
            all_of(fields, tile_rows, tile_cols),
            all_of(fields, tile_rows, tile_cols),
            four,
            four,
            four,
            line,
            pl.BlockSpec((8, FORCE_TILE), lambda i: (0, i)),
        ],
        out_specs=(
            line,
            line,
            all_of(fields, tile_rows, tile_cols),
            all_of(*rim),
            all_of(*rim),
        ),
        scratch_shapes=[
            pltpu.VMEM((fields * tile_rows, window_cols), BF16),
            pltpu.VMEM((fields, tile_rows, window_cols), F32),
        ],
        compiler_params=pltpu.CompilerParams(vmem_limit_bytes=20 * MEBI),
        cost_estimate=cost(8 * fields * tile_rows * window_cols * nodes, 4000000),
        name="forcing",
    )(
        start,
        exchange_factor,
        atmosphere_inputs,
        other,
        corner_parallel,
        corner_longitude,
        corner_share,
        surface,
        thermal_anomaly,
    )
    below = lax.ppermute(up_rim, "lon", upward)
    above = lax.ppermute(down_rim, "lon", downward)

    updated_warmth, temp_grad = pl.pallas_call(
        lateral_kernel,
        out_shape=(
            jax.ShapeDtypeStruct((layers, nodes), F32),
            jax.ShapeDtypeStruct((layers, nodes), F32),
        ),
        in_specs=whole(19),
        out_specs=tuple(whole(2)),
        scratch_shapes=[
            pltpu.VMEM((layers, nodes), F32),
            pltpu.VMEM(dense, F32),
            pltpu.VMEM((4, SLOT_ROWS, NODE_TILE), BF16),
            pltpu.VMEM((4, SLOT_ROWS, NODE_TILE), BF16),
            pltpu.VMEM((2 * layers, NODE_TILE), F32),
            pltpu.VMEM((2 * layers, NODE_TILE), F32),
            pltpu.VMEM((NODE_TILE, nodes), BF16),
            pltpu.VMEM((NODE_TILE, nodes), BF16),
            pltpu.SMEM((nodes // NODE_TILE,), jnp.int32),
        ],
        compiler_params=pltpu.CompilerParams(vmem_limit_bytes=32 * MEBI),
        cost_estimate=cost(8 * layers * nodes * extended, 8000000),
        name="lateral",
    )(
        adjacency,
        merged,
        rank,
        low,
        high,
        node_scale,
        keep,
        thermal_anomaly,
        ext,
        scaled,
        begun_grad,
        begun_rhs,
        back,
        column,
        flux,
        corr,
        gain,
        scale,
        carry,
    )

    forcing_grad = pl.pallas_call(
        join_kernel,
        out_shape=jax.ShapeDtypeStruct((fields, tile_rows, tile_cols), F32),
        in_specs=whole(3),
        out_specs=pl.BlockSpec(memory_space=pltpu.VMEM),
        compiler_params=pltpu.CompilerParams(vmem_limit_bytes=8 * MEBI),
        cost_estimate=cost(fields * tile_rows * tile_cols, 2000000),
        name="join",
    )(own_forcing, below, above)
    return (updated_warmth, temp_grad, forcing_grad)


def solution(mesh):
    nodes = P(None, ("lat", "lon"))
    placed = (
        P(None, "lat", "lon"),
        nodes,
        nodes,
        nodes,
        nodes,
        P(("lat", "lon"), None),
        nodes,
        nodes,
        nodes,
        P(),
        nodes,
    )
    return jax.shard_map(
        per_device,
        mesh=mesh,
        in_specs=placed,
        out_specs=(nodes, nodes, P(None, "lat", "lon")),
        check_vma=False,
    )
```

```python
import functools

import jax
import jax.numpy as jnp
from jax import lax
from jax.experimental import pallas as pl
from jax.experimental.pallas import tpu as pltpu
from jax.sharding import PartitionSpec as P

F32 = jnp.float32
BF16 = jnp.bfloat16
MEBI = 1024 * 1024
LANES = 128
SLOT_ROWS = 256
NODE_TILE = 256
FORCE_TILE = 512
EARLY_PAIRS = 3
LANE_CONTRACT = (((1,), (1,)), ((), ()))
MESH = pl.DeviceIdType.MESH


def whole(count):
    return [pl.BlockSpec(memory_space=pltpu.VMEM)] * count


def halves(value):
    high = value.astype(BF16)
    return high, (value - high.astype(F32)).astype(BF16)


def spread_levels(source_ref, dense_ref):
    layers = dense_ref.shape[0]
    for level in range(0, layers, 8):
        dense_ref[level : level + 8] = source_ref[level : level + 8, :].reshape(
            (8,) + dense_ref.shape[1:]
        )


def sweep_up(x_ref, mix_ref, scale_ref, zero):
    layers = x_ref.shape[0]

    def up(step, x_next):
        level = layers - 1 - step
        x_here = x_ref[level] + (mix_ref[level] * scale_ref[level]) * x_next
        x_ref[level] = x_here
        return x_here

    lax.fori_loop(0, layers, up, zero, unroll=8)


def best_scale(values, count):
    trial = lax.broadcasted_iota(jnp.int32, (count, values[0].shape[1]), 0).astype(F32)
    trial = 1.0 + trial * (1.0 / count)
    inverse = 1.0 / trial
    miss = jnp.zeros_like(trial)
    for value in values:
        gap = (value * inverse).astype(BF16).astype(F32) * trial - value
        miss = miss + gap * gap
    least = jnp.min(miss, axis=0, keepdims=True)
    return jnp.max(jnp.where(miss == least, trial, 1.0), axis=0, keepdims=True)


def slot_weights(adj_ref, merged_ref, cols, first_row, rank_ref=None):
    row = lax.broadcasted_iota(jnp.int32, (SLOT_ROWS, NODE_TILE), 0).astype(F32).astype(BF16)
    local = adj_ref[:, cols] - first_row
    if rank_ref is not None:
        rank = rank_ref[: adj_ref.shape[0], cols]
        local = jnp.where(jnp.logical_and(rank >= 0.0, rank <= 1.0), local, -1)
    local = local.astype(F32).astype(BF16)
    share = merged_ref[:, cols].astype(BF16)
    weights = jnp.zeros((SLOT_ROWS, NODE_TILE), BF16)
    for k in range(adj_ref.shape[0]):
        weights = jnp.where(row == local[k : k + 1, :], share[k : k + 1, :], weights)
    return weights


def slot_ids(adj_ref):
    slots, nodes = adj_ref.shape
    at = lax.broadcasted_iota(jnp.int32, (8, nodes), 0)
    spare = lax.broadcasted_iota(jnp.int32, (8 - slots, nodes), 0) - (8 - slots)
    return jnp.concatenate([adj_ref[...], spare], 0), at


def merge_slots(adj_ref, coef_ref, merged_ref):
    slots, nodes = adj_ref.shape
    ids, _ = slot_ids(adj_ref)
    coef = jnp.concatenate([coef_ref[...], jnp.zeros((8 - slots, nodes), F32)], 0)
    merged = coef
    for shift in range(1, 8):
        equal = ids == pltpu.roll(ids, shift, 0)
        merged = merged + jnp.where(equal, pltpu.roll(coef, shift, 0), 0.0)
    merged_ref[...] = merged


def rank_slots(adj_ref, rank_ref, low_ref, high_ref):
    slots, nodes = adj_ref.shape
    ids, at = slot_ids(adj_ref)
    low = (ids & (SLOT_ROWS - 1)).astype(F32)
    high = (ids >> (SLOT_ROWS.bit_length() - 1)).astype(F32)
    repeat = jnp.zeros((8, nodes), F32)
    for shift in range(1, slots):
        equal = ids == pltpu.roll(ids, shift, 0)
        repeat = jnp.where(jnp.logical_and(equal, at >= shift), 1.0, repeat)
    rank = jnp.zeros((8, nodes), F32)
    for shift in range(1, slots):
        met = jnp.logical_and(low == pltpu.roll(low, shift, 0), at >= shift)
        rank = rank + jnp.where(met, 1.0 - pltpu.roll(repeat, shift, 0), 0.0)
    rank = jnp.where(jnp.logical_or(repeat > 0.0, at >= slots), -1.0, rank)
    place = jnp.zeros((8, nodes), F32)
    for shift in range(1, slots):
        second = jnp.logical_and(pltpu.roll(rank, shift, 0) == 1.0, at >= shift)
        place = place + jnp.where(second, 1.0, 0.0)
    rank_ref[...] = rank
    low_ref[:8, :] = jnp.where(rank == 0.0, low, -1.0)
    high_ref[:8, :] = high
    for j in range(slots // 2):
        here = jnp.logical_and(rank == 1.0, place == float(j))
        low_ref[8 + j : 9 + j, :] = jnp.max(jnp.where(here, low, -1.0), axis=0, keepdims=True)
        high_ref[8 + j : 9 + j, :] = jnp.max(jnp.where(here, high, -1.0), axis=0, keepdims=True)


def sent_column(sent_ref, column_ref):
    parts, each = sent_ref.shape
    padded = jnp.concatenate(
        [sent_ref[...].astype(F32), jnp.zeros((parts, LANES - each), F32)], 1
    ).T
    for part in range(parts):
        column_ref[part * each : (part + 1) * each, :] = jnp.broadcast_to(
            padded[:each, part : part + 1], (each, LANES)
        )


def chosen_rows(column_ref, first_node):
    local = (column_ref[...] - first_node).astype(BF16)
    lane = lax.broadcasted_iota(jnp.int32, local.shape, 1).astype(F32)
    zero = jnp.zeros(local.shape, BF16)
    one = jnp.ones(local.shape, BF16)
    pieces = [
        jnp.where(local == (lane + float(start)).astype(BF16), one, zero)
        for start in range(0, NODE_TILE, LANES)
    ]
    return jnp.concatenate(pieces, 1)


def key_writer(cols, tables, keys_ref):
    merged_ref, rank_ref, low_ref, high_ref = tables
    rank = rank_ref[:, cols]
    merged = merged_ref[:, cols]
    low = low_ref[:, cols].astype(BF16)
    high = high_ref[:, cols].astype(BF16)
    share = merged.astype(BF16)
    pairs = low.shape[0] - 8
    place = jnp.zeros((1, NODE_TILE), F32)
    seconds = [jnp.zeros((1, NODE_TILE), F32)] * pairs
    for k in range(1, 2 * pairs):
        here = rank[k : k + 1] == 1.0
        for j in range(pairs):
            mine = jnp.logical_and(here, place == float(j))
            seconds[j] = jnp.where(mine, merged[k : k + 1], seconds[j])
        place = place + jnp.where(here, 1.0, 0.0)
    seconds = [second.astype(BF16) for second in seconds]

    def write(first):
        row = lax.broadcasted_iota(jnp.int32, (16, NODE_TILE), 0).astype(F32).astype(BF16)
        row = row + float(first)
        none = jnp.full((16, NODE_TILE), -1.0, BF16)
        zero = jnp.zeros((16, NODE_TILE), BF16)
        key, val = none, zero
        for k in range(2 * pairs):
            mine = row == low[k : k + 1]
            key = jnp.where(mine, high[k : k + 1], key)
            val = jnp.where(mine, share[k : k + 1], val)
        keys_ref[0, first : first + 16, :] = key
        keys_ref[1, first : first + 16, :] = val
        key, val = none, zero
        for j in range(pairs):
            mine = row == low[8 + j : 9 + j]
            key = jnp.where(mine, high[8 + j : 9 + j], key)
            val = jnp.where(mine, seconds[j], val)
        keys_ref[2, first : first + 16, :] = key
        keys_ref[3, first : first + 16, :] = val

    return write


def block_weights(keys_ref, blocks):
    key0, val0, key1, val1 = (keys_ref[i] for i in range(4))
    found = []
    for block in blocks:
        weights = jnp.where(key0 == float(block), val0, jnp.zeros_like(val0))
        found.append(jnp.where(key1 == float(block), val1, weights))
    return found


def node_cols(tile):
    start = tile * NODE_TILE
    if not isinstance(start, int):
        start = pl.multiple_of(start, NODE_TILE)
    return pl.ds(start, NODE_TILE)


def apply_tiles(first, end, rows, tables, fields, scratch):
    ext_ref, scaled_ref, thermal_ref, keep_ref, node_scale_ref, rhs_ref, grad_ref = fields
    even_ref, odd_ref, even_sum_ref, odd_sum_ref, even_turned_ref, odd_turned_ref = scratch
    layers, nodes = thermal_ref.shape
    tiles = nodes // NODE_TILE

    def use(tile, keys_ref, next_keys_ref, sum_ref, turned_ref):
        cols = node_cols(tile)
        scaled = scaled_ref[:, cols]
        groups = SLOT_ROWS // 16
        done = 0
        blocks = rows // SLOT_ROWS
        for start in range(0, blocks, 2):
            now = range(start, min(start + 2, blocks))
            for block, weights in zip(now, block_weights(keys_ref, now)):
                here = slice(block * SLOT_ROWS, (block + 1) * SLOT_ROWS)
                part = jnp.dot(ext_ref[:, here], weights, preferred_element_type=F32)
                if block == 0:
                    sum_ref[...] = part
                else:
                    sum_ref[...] += part
                if block * SLOT_ROWS < nodes:
                    turned_ref[:, here] = weights.T
                    part = jnp.dot(scaled, turned_ref[:, here], preferred_element_type=F32)
                    grad_ref[:, here] += part[:layers] + part[layers:]
            if start == 0:
                write = key_writer(node_cols(jnp.minimum(tile + 1, tiles - 1)), tables, next_keys_ref)
            until = min(groups, -(-groups * now[-1] // (nodes // SLOT_ROWS - 1)))
            for group in range(done, until):
                write(group * 16)
            done = until
        rhs_ref[:, cols] = (
            thermal_ref[:, cols] * keep_ref[:, cols]
            + (sum_ref[:layers, :] + sum_ref[layers:, :]) * node_scale_ref[:, cols]
        )

    write = key_writer(node_cols(2 * first), tables, even_ref)
    for group in range(SLOT_ROWS // 16):
        write(group * 16)

    def pair(step, carry):
        use(2 * step, even_ref, odd_ref, even_sum_ref, even_turned_ref)
        use(2 * step + 1, odd_ref, even_ref, odd_sum_ref, odd_turned_ref)
        return carry

    lax.fori_loop(first, end, pair, 0)


def exchange_kernel(
    mix_hbm,
    sens_hbm,
    thermal_hbm,
    adj_hbm,
    coef_hbm,
    sent_hbm,
    atm_hbm,
    scaled_ref,
    grad_ref,
    rhs_ref,
    surface_ref,
    mix3_ref,
    scale_ref,
    merged_ref,
    rank_ref,
    low_ref,
    high_ref,
    node_scale_ref,
    ext_ref,
    back_ref,
    other_ref,
    keep_ref,
    adj_out_ref,
    column_ref,
    x_ref,
    depart_buf,
    received_buf,
    hgrad_buf,
    back_buf,
    right_buf,
    left_buf,
    from_left_buf,
    from_right_buf,
    send_sem,
    recv_sem,
    gsend_sem,
    grecv_sem,
    rim_sem,
    mix_ref,
    sens_ref,
    thermal_ref,
    adj_ref,
    coef_ref,
    sent_ref,
    atm_ref,
    load_sem,
    even_ref,
    odd_ref,
    even_sum_ref,
    odd_sum_ref,
    even_turned_ref,
    odd_turned_ref,
):
    load = {}
    sources = (
        ("adj", adj_hbm, adj_ref),
        ("coef", coef_hbm, coef_ref),
        ("mix", mix_hbm, mix_ref),
        ("sens", sens_hbm, sens_ref),
        ("atm", atm_hbm, atm_ref),
        ("sent", sent_hbm, sent_ref),
        ("thermal", thermal_hbm, thermal_ref),
    )
    for index, (name, source, target) in enumerate(sources):
        load[name] = pltpu.make_async_copy(source, target, load_sem.at[index])
        load[name].start()
    layers, nodes = mix_ref.shape
    slots = adj_ref.shape[0]
    parts, each = sent_ref.shape
    halo = parts * each
    fields, tile_rows, tile_cols = atm_ref.shape
    mid = tile_rows // 2
    me = lax.axis_index("lon")
    ahead = lax.rem(me + 1, parts)
    behind = lax.rem(me + parts - 1, parts)

    barrier = pltpu.get_barrier_semaphore()
    for off in range(1, parts):
        pl.semaphore_signal(
            barrier, inc=1, device_id={"lon": lax.rem(me + off, parts)}, device_id_type=MESH
        )

    load["adj"].wait()
    load["coef"].wait()
    merge_slots(adj_ref, coef_ref, merged_ref)

    def fit(step, carry):
        cols = pl.ds(pl.multiple_of(step * NODE_TILE, NODE_TILE), NODE_TILE)
        merged = [merged_ref[k : k + 1, cols] for k in range(slots)]
        scale = best_scale(merged, 32)
        node_scale_ref[:, cols] = scale
        merged_ref[:, cols] = merged_ref[:, cols] / scale
        return carry

    lax.fori_loop(0, nodes // NODE_TILE, fit, 0)

    zero = jnp.zeros(x_ref.shape[1:], F32)
    load["mix"].wait()
    load["sens"].wait()
    spread_levels(mix_ref, mix3_ref)
    spread_levels(sens_ref, x_ref)

    def down(level, state):
        mix_prev, gain_prev, d_prev = state
        mix = mix3_ref[level]
        scale = 1.0 / (1.0 + mix + mix_prev * (1.0 - gain_prev))
        gain = mix * scale
        carry = mix_prev * scale
        d_next = x_ref[level] * scale + carry * d_prev
        scale_ref[level] = scale
        x_ref[level] = d_next
        return mix, gain, d_next

    lax.fori_loop(0, layers, down, (zero, zero, zero), unroll=4)
    sweep_up(x_ref, mix3_ref, scale_ref, zero)
    keep = 1.0 - jnp.sum(coef_ref[...], axis=0, keepdims=True)
    keep_ref[...] = keep
    for level in range(0, layers, 16):
        flat = x_ref[level : level + 16].reshape(16, nodes)
        if level == 0:
            surface_ref[...] = flat[0:1]
        grad_ref[level : level + 16, :] = flat * keep
        high, low = halves(flat * node_scale_ref[...])
        scaled_ref[level : level + 16, :] = high
        scaled_ref[layers + level : layers + level + 16, :] = low

    load["atm"].wait()
    low_lane = lax.broadcasted_iota(jnp.int32, (mid, tile_cols), 1) < tile_cols // 2
    for f in range(fields):
        upper = atm_ref[f, :mid, :].astype(F32)
        lower = pltpu.roll(atm_ref[f, mid:, :].astype(F32), tile_cols // 2, 1)
        right_buf[f] = jnp.where(low_lane, lower, upper).astype(BF16)
        left_buf[f] = jnp.where(low_lane, upper, lower).astype(BF16)

    load["sent"].wait()
    load["thermal"].wait()
    sent_column(sent_ref, column_ref)
    depart = jnp.zeros((halo, 2 * layers), F32)
    tile = 1024

    def pick(step, total):
        cols = pl.ds(pl.multiple_of(step * tile, tile), tile)
        high, low = halves(thermal_ref[:, cols])
        ext = jnp.concatenate([high, low], 0)
        first = (step * tile).astype(F32)
        chosen = jnp.concatenate(
            [chosen_rows(column_ref, first + float(at)) for at in range(0, tile, NODE_TILE)], 1
        )
        return total + lax.dot_general(
            chosen, ext, LANE_CONTRACT, preferred_element_type=F32
        )

    depart = lax.fori_loop(0, nodes // tile, pick, depart)
    depart_buf[...] = depart.astype(BF16)

    pl.semaphore_wait(barrier, parts - 1)

    def rim_copy(source, target, index, to):
        return pltpu.make_async_remote_copy(
            src_ref=source,
            dst_ref=target,
            send_sem=rim_sem.at[index],
            recv_sem=rim_sem.at[2 + index],
            device_id={"lon": to},
            device_id_type=MESH,
        )

    rims = [
        rim_copy(right_buf, from_left_buf, 0, ahead),
        rim_copy(left_buf, from_right_buf, 1, behind),
    ]
    for copy in rims:
        copy.start()

    def rows_of(part):
        return pl.ds(pl.multiple_of(part * each, each), each)

    def halo_copies(source, target, sends, recvs):
        copies = []
        for off in range(1, parts):
            peer = lax.rem(me + off, parts)
            copies.append(
                pltpu.make_async_remote_copy(
                    src_ref=source.at[rows_of(peer)],
                    dst_ref=target.at[rows_of(me)],
                    send_sem=sends.at[off],
                    recv_sem=recvs.at[off],
                    device_id={"lon": peer},
                    device_id_type=MESH,
                )
            )
        return copies

    def own_copy(source, target, sem):
        return pltpu.make_async_copy(source.at[rows_of(me)], target.at[rows_of(me)], sem)

    there = halo_copies(depart_buf, received_buf, send_sem, recv_sem)
    for copy in there:
        copy.start()
    mine = own_copy(depart_buf, received_buf, send_sem.at[0])
    mine.start()

    for block in range(halo // SLOT_ROWS):

        def collect(step, total):
            cols = pl.ds(pl.multiple_of(step * NODE_TILE, NODE_TILE), NODE_TILE)
            weights = slot_weights(adj_ref, merged_ref, cols, nodes + block * SLOT_ROWS)
            return total + lax.dot_general(
                scaled_ref[:, cols], weights, LANE_CONTRACT, preferred_element_type=F32
            )

        total = lax.fori_loop(
            0, nodes // NODE_TILE, collect, jnp.zeros((2 * layers, SLOT_ROWS), F32)
        )
        high, low = halves(total[:layers] + total[layers:])
        both = jnp.concatenate([high.astype(F32), low.astype(F32)], 0)
        hgrad_buf[block * SLOT_ROWS : (block + 1) * SLOT_ROWS, :] = both.T.astype(BF16)

    home = halo_copies(hgrad_buf, back_buf, gsend_sem, grecv_sem)
    for copy in home:
        copy.start()
    mine_back = own_copy(hgrad_buf, back_buf, gsend_sem.at[0])
    mine_back.start()
    rank_slots(adj_ref, rank_ref, low_ref, high_ref)
    adj_out_ref[...] = adj_ref[...]

    high, low = halves(thermal_ref[...])
    ext_ref[:layers, :nodes] = high
    ext_ref[layers:, :nodes] = low
    early = nodes // NODE_TILE // 2 * EARLY_PAIRS // 8
    apply_tiles(
        0,
        early,
        nodes,
        (merged_ref, rank_ref, low_ref, high_ref),
        (ext_ref, scaled_ref, thermal_ref, keep_ref, node_scale_ref, rhs_ref, grad_ref),
        (even_ref, odd_ref, even_sum_ref, odd_sum_ref, even_turned_ref, odd_turned_ref),
    )

    mine.wait()
    for copy in there:
        copy.wait()
    ext_ref[:, nodes:] = received_buf[...].astype(F32).T.astype(BF16)
    for block in range(halo // SLOT_ROWS):
        first = nodes + block * SLOT_ROWS

        def arrive(tile, carry):
            cols = node_cols(tile)
            weights = slot_weights(adj_ref, merged_ref, cols, first, rank_ref)
            part = jnp.dot(
                ext_ref[:, first : first + SLOT_ROWS], weights, preferred_element_type=F32
            )
            rhs_ref[:, cols] += (part[:layers] + part[layers:]) * node_scale_ref[:, cols]
            return carry

        lax.fori_loop(0, 2 * early, arrive, 0)

    for copy in rims:
        copy.wait()
    for f in range(fields):
        right = from_right_buf[f].astype(F32)
        left = from_left_buf[f].astype(F32)
        other_ref[f, :mid, :] = jnp.where(low_lane, right, left).astype(BF16)
        other_ref[f, mid:, :] = pltpu.roll(
            jnp.where(low_lane, left, right), tile_cols // 2, 1
        ).astype(BF16)

    mine_back.wait()
    for copy in home:
        copy.wait()
    back_ref[...] = back_buf[...].astype(F32).T.astype(BF16)


def forcing_kernel(
    start_ref,
    factor_ref,
    atm_ref,
    other_ref,
    row_ref,
    col_ref,
    share_ref,
    surface_ref,
    thermal_ref,
    flux_ref,
    corr_ref,
    own_ref,
    up_ref,
    down_ref,
    window_ref,
    grad_ref,
):
    fields, tile_rows, window_cols = grad_ref.shape
    tile_cols = window_cols // 2
    mid = tile_rows // 2
    tile = row_ref.shape[1]

    @pl.when(pl.program_id(0) == 0)
    def _():
        grad_ref[...] = jnp.zeros_like(grad_ref)
        window_ref[:, :tile_cols] = atm_ref[...].reshape(fields * tile_rows, tile_cols)
        window_ref[:, tile_cols:] = other_ref[...].reshape(fields * tile_rows, tile_cols)

    share = share_ref[...]
    row_low = share[0:1] + share[2:3]
    row_high = share[1:2] + share[3:4]
    col_low = share[0:1] + share[1:2]
    col_high = share[2:3] + share[3:4]
    scale = best_scale([col_low, col_high], 64)
    col_low = col_low / scale
    col_high = col_high / scale
    base_row = row_ref[0:1, :]
    base_col = lax.rem(col_ref[0:1, :] + start_ref[0], window_cols)
    next_col = lax.rem(base_col + 1, window_cols)
    row_at = lax.broadcasted_iota(jnp.int32, (tile_rows, tile), 0)
    col_at = lax.broadcasted_iota(jnp.int32, (window_cols, tile), 0)
    rows = jnp.where(
        row_at == base_row, row_low, jnp.where(row_at == base_row + 1, row_high, 0.0)
    )
    col_is = col_at.astype(F32).astype(BF16)
    first_col, second_col = (value.astype(F32).astype(BF16) for value in (base_col, next_col))
    cols = jnp.where(
        col_is == first_col,
        col_low.astype(BF16),
        jnp.where(col_is == second_col, col_high.astype(BF16), jnp.zeros(col_is.shape, BF16)),
    )
    rows = rows * scale
    mixed = jnp.dot(window_ref[...], cols, preferred_element_type=F32)
    forced = [
        jnp.sum(mixed[f * tile_rows : (f + 1) * tile_rows] * rows, axis=0, keepdims=True)
        for f in range(fields)
    ]
    wind = jnp.sqrt(forced[0] * forced[0] + forced[1] * forced[1] + 1.0)
    excess = forced[2] - thermal_ref[0:1, :]
    flux = 0.1 * wind * excess
    for f in range(fields):
        flux = flux + factor_ref[f] * forced[f]
    flux_ref[...] = flux
    surface = surface_ref[...]
    corr_ref[...] = -0.1 * surface * wind
    quotient = surface * (0.1 * excess / wind)
    dot = functools.partial(
        lax.dot_general,
        dimension_numbers=LANE_CONTRACT,
        preferred_element_type=F32,
    )
    row_is = row_at.astype(F32).astype(BF16)
    base_is = base_row.astype(F32).astype(BF16)
    at_low = row_is == base_is
    at_high = row_is == base_is + 1.0
    none = jnp.zeros(row_is.shape, BF16)
    ends = [row_low * scale, row_high * scale]
    lefts = []
    for f in range(fields):
        node_grad = surface * factor_ref[f]
        if f < 2:
            node_grad = node_grad + quotient * forced[f]
        if f == 2:
            node_grad = node_grad + 0.1 * surface * wind
        below, above = (halves(node_grad * end) for end in ends)
        lefts.append(
            [
                jnp.where(at_low, low_end, jnp.where(at_high, high_end, none))
                for low_end, high_end in zip(below, above)
            ]
        )
    left_hi = jnp.concatenate([high for high, _ in lefts], 0)
    left_lo = jnp.concatenate([low for _, low in lefts], 0)
    grad = dot(left_hi, cols) + dot(left_lo, cols)
    grad_ref[...] += grad.reshape(fields, tile_rows, window_cols)

    @pl.when(pl.program_id(0) == pl.num_programs(0) - 1)
    def _():
        low_lane = lax.broadcasted_iota(jnp.int32, (mid, tile_cols), 1) < tile_cols // 2
        for f in range(fields):
            own_ref[f] = grad_ref[f, :, :tile_cols]
            upper = grad_ref[f, :mid, tile_cols:]
            lower = pltpu.roll(grad_ref[f, mid:, tile_cols:], tile_cols // 2, 1)
            up_ref[f] = jnp.where(low_lane, upper, lower)
            down_ref[f] = jnp.where(low_lane, lower, upper)


def lateral_kernel(
    adj_ref,
    merged_ref,
    rank_ref,
    low_ref,
    high_ref,
    node_scale_ref,
    keep_ref,
    thermal_ref,
    ext_ref,
    scaled_ref,
    begun_grad_ref,
    begun_rhs_ref,
    back_ref,
    column_ref,
    flux_ref,
    corr_ref,
    mix3_ref,
    scale_ref,
    warm_ref,
    grad_ref,
    rhs_ref,
    x_ref,
    even_ref,
    odd_ref,
    even_sum_ref,
    odd_sum_ref,
    even_turned_ref,
    odd_turned_ref,
    deep_ref,
):
    slots, nodes = adj_ref.shape
    layers = rhs_ref.shape[0]
    tiles = nodes // NODE_TILE
    tables = merged_ref, rank_ref, low_ref, high_ref

    def deep_block(tile, bound):
        cols = node_cols(tile)
        high = (adj_ref[:, cols] >> (SLOT_ROWS.bit_length() - 1)).astype(F32)
        deep = jnp.logical_and(rank_ref[:slots, cols] > 1.0, high < bound)
        return jnp.max(jnp.where(deep, high, -1.0)).astype(jnp.int32)

    for tile in range(tiles):
        deep_ref[tile] = deep_block(tile, float(ext_ref.shape[1]))
    start_pair = tiles // 2 * EARLY_PAIRS // 8
    begun = start_pair * 2 * NODE_TILE
    rhs_ref[:, :begun] = begun_rhs_ref[:, :begun]
    grad_ref[...] = begun_grad_ref[...]
    fields_of_tile = (
        ext_ref, scaled_ref, thermal_ref, keep_ref, node_scale_ref, rhs_ref, grad_ref
    )
    scratch = even_ref, odd_ref, even_sum_ref, odd_sum_ref, even_turned_ref, odd_turned_ref

    def mend(tile):
        def one_block(block):
            cols = node_cols(tile)
            here = pl.ds(pl.multiple_of(block * SLOT_ROWS, SLOT_ROWS), SLOT_ROWS)
            local = jnp.where(
                rank_ref[:slots, cols] > 1.0, adj_ref[:, cols] - block * SLOT_ROWS, -1
            )
            local = local.astype(F32).astype(BF16)
            share = merged_ref[:slots, cols].astype(BF16)
            row = lax.broadcasted_iota(jnp.int32, (SLOT_ROWS, NODE_TILE), 0)
            row = row.astype(F32).astype(BF16)
            weights = jnp.zeros((SLOT_ROWS, NODE_TILE), BF16)
            for k in range(2, slots):
                weights = jnp.where(row == local[k : k + 1], share[k : k + 1], weights)
            part = jnp.dot(ext_ref[:, here], weights, preferred_element_type=F32)
            rhs_ref[:, cols] += (part[:layers] + part[layers:]) * node_scale_ref[:, cols]

            @pl.when(block * SLOT_ROWS < nodes)
            def _():
                part = lax.dot_general(
                    scaled_ref[:, cols], weights, LANE_CONTRACT, preferred_element_type=F32
                )
                grad_ref[:, here] += part[:layers] + part[layers:]

            return deep_block(tile, block.astype(F32))

        lax.while_loop(lambda block: block >= 0, one_block, deep_ref[tile])

    apply_tiles(start_pair, tiles // 2, ext_ref.shape[1], tables, fields_of_tile, scratch)

    def fix(tile, carry):
        mend(tile)
        return carry

    lax.fori_loop(0, tiles, fix, 0)

    width = 4 * NODE_TILE

    def give_back(step, carry):
        cols = pl.ds(pl.multiple_of(step * width, width), width)
        first = (step * width).astype(F32)
        chosen = jnp.concatenate(
            [chosen_rows(column_ref, first + float(at)) for at in range(0, width, NODE_TILE)], 1
        )
        part = jnp.dot(back_ref[...], chosen, preferred_element_type=F32)
        grad_ref[:, cols] += part[:layers] + part[layers:]
        return carry

    lax.fori_loop(0, nodes // width, give_back, 0)
    grad_ref[0:1, :] += corr_ref[...]

    rhs_ref[0:1, :] += flux_ref[...]
    zero = jnp.zeros(x_ref.shape[1:], F32)
    spread_levels(rhs_ref, x_ref)

    def down(level, state):
        mix_prev, d_prev = state
        scale = scale_ref[level]
        d_next = x_ref[level] * scale + (mix_prev * scale) * d_prev
        x_ref[level] = d_next
        return mix3_ref[level], d_next

    lax.fori_loop(0, layers, down, (zero, zero), unroll=8)
    sweep_up(x_ref, mix3_ref, scale_ref, zero)
    for level in range(0, layers, 8):
        warm_ref[level : level + 8, :] = x_ref[level : level + 8].reshape(8, nodes)


def join_kernel(own_ref, below_ref, above_ref, out_ref):
    fields, tile_rows, tile_cols = own_ref.shape
    mid = tile_rows // 2
    low_lane = lax.broadcasted_iota(jnp.int32, (mid, tile_cols), 1) < tile_cols // 2
    for f in range(fields):
        below, above = below_ref[f], above_ref[f]
        out_ref[f, :mid, :] = own_ref[f, :mid, :] + jnp.where(low_lane, below, above)
        out_ref[f, mid:, :] = own_ref[f, mid:, :] + pltpu.roll(
            jnp.where(low_lane, above, below), tile_cols // 2, 1
        )


def cost(flops, moved):
    return pl.CostEstimate(flops=flops, bytes_accessed=moved, transcendentals=0)


def per_device(
    atmosphere_inputs,
    thermal_anomaly,
    mixing_rates,
    adjacency_table,
    lateral_spread_factor,
    sent_vertices,
    corner_parallel,
    corner_longitude,
    corner_share,
    exchange_factor,
    sensitivity_vector,
):
    layers, nodes = thermal_anomaly.shape
    fields, tile_rows, tile_cols = atmosphere_inputs.shape
    columns, each = sent_vertices.shape
    halo = columns * each
    slots = adjacency_table.shape[0]
    window_cols = 2 * tile_cols
    extended = nodes + halo
    upward = [(i, (i + 1) % columns) for i in range(columns)]
    downward = [((i + 1) % columns, i) for i in range(columns)]
    position = lax.axis_index("lon")
    start = ((columns - position) * tile_cols).astype(jnp.int32).reshape(1)

    dense = (layers, nodes // LANES, LANES)
    block = jax.ShapeDtypeStruct(dense, F32)
    rim = (fields, tile_rows // 2, tile_cols)
    (
        scaled,
        begun_grad,
        begun_rhs,
        surface,
        mix3,
        scale,
        merged,
        rank,
        low,
        high,
        node_scale,
        ext,
        back,
        other,
        keep,
        adjacency,
        column,
    ) = pl.pallas_call(
        exchange_kernel,
        out_shape=(
            jax.ShapeDtypeStruct((2 * layers, nodes), BF16),
            jax.ShapeDtypeStruct((layers, nodes), F32),
            jax.ShapeDtypeStruct((layers, nodes), F32),
            jax.ShapeDtypeStruct((1, nodes), F32),
            block,
            block,
            jax.ShapeDtypeStruct((8, nodes), F32),
            jax.ShapeDtypeStruct((8, nodes), F32),
            jax.ShapeDtypeStruct((8 + slots // 2, nodes), F32),
            jax.ShapeDtypeStruct((8 + slots // 2, nodes), F32),
            jax.ShapeDtypeStruct((1, nodes), F32),
            jax.ShapeDtypeStruct((2 * layers, extended), BF16),
            jax.ShapeDtypeStruct((2 * layers, halo), BF16),
            jax.ShapeDtypeStruct(atmosphere_inputs.shape, BF16),
            jax.ShapeDtypeStruct((1, nodes), F32),
            jax.ShapeDtypeStruct((slots, nodes), jnp.int32),
            jax.ShapeDtypeStruct((halo, LANES), F32),
        ),
        in_specs=[pl.BlockSpec(memory_space=pltpu.HBM)] * 7,
        out_specs=tuple(whole(17)),
        scratch_shapes=[
            pltpu.VMEM(dense, F32),
            pltpu.VMEM((halo, 2 * layers), BF16),
            pltpu.VMEM((halo, 2 * layers), BF16),
            pltpu.VMEM((halo, 2 * layers), BF16),
            pltpu.VMEM((halo, 2 * layers), BF16),
            pltpu.VMEM(rim, BF16),
            pltpu.VMEM(rim, BF16),
            pltpu.VMEM(rim, BF16),
            pltpu.VMEM(rim, BF16),
            pltpu.SemaphoreType.DMA((columns,)),
            pltpu.SemaphoreType.DMA((columns,)),
            pltpu.SemaphoreType.DMA((columns,)),
            pltpu.SemaphoreType.DMA((columns,)),
            pltpu.SemaphoreType.DMA((4,)),
            pltpu.VMEM((layers, nodes), F32),
            pltpu.VMEM((layers, nodes), F32),
            pltpu.VMEM((layers, nodes), F32),
            pltpu.VMEM((slots, nodes), jnp.int32),
            pltpu.VMEM((slots, nodes), F32),
            pltpu.VMEM(sent_vertices.shape, jnp.int32),
            pltpu.VMEM(atmosphere_inputs.shape, BF16),
            pltpu.SemaphoreType.DMA((7,)),
            pltpu.VMEM((4, SLOT_ROWS, NODE_TILE), BF16),
            pltpu.VMEM((4, SLOT_ROWS, NODE_TILE), BF16),
            pltpu.VMEM((2 * layers, NODE_TILE), F32),
            pltpu.VMEM((2 * layers, NODE_TILE), F32),
            pltpu.VMEM((NODE_TILE, nodes), BF16),
            pltpu.VMEM((NODE_TILE, nodes), BF16),
        ],
        compiler_params=pltpu.CompilerParams(
            vmem_limit_bytes=47 * MEBI, collective_id=0, has_side_effects=True
        ),
        cost_estimate=cost(layers * nodes * 20, layers * nodes * 24),
        name="exchange",
    )(
        mixing_rates,
        sensitivity_vector,
        thermal_anomaly,
        adjacency_table,
        lateral_spread_factor,
        sent_vertices,
        atmosphere_inputs,
    )

    line = pl.BlockSpec((1, FORCE_TILE), lambda i: (0, i))
    four = pl.BlockSpec((4, FORCE_TILE), lambda i: (0, i))

    def all_of(*shape):
        return pl.BlockSpec(shape, lambda i: (0,) * len(shape))

    flux, corr, own_forcing, up_rim, down_rim = pl.pallas_call(
        forcing_kernel,
        grid=(nodes // FORCE_TILE,),
        out_shape=(
            jax.ShapeDtypeStruct((1, nodes), F32),
            jax.ShapeDtypeStruct((1, nodes), F32),
            jax.ShapeDtypeStruct((fields, tile_rows, tile_cols), F32),
            jax.ShapeDtypeStruct(rim, F32),
            jax.ShapeDtypeStruct(rim, F32),
        ),
        in_specs=[
            pl.BlockSpec(memory_space=pltpu.SMEM),
            pl.BlockSpec(memory_space=pltpu.SMEM),
            all_of(fields, tile_rows, tile_cols),
            all_of(fields, tile_rows, tile_cols),
            four,
            four,
            four,
            line,
            pl.BlockSpec((8, FORCE_TILE), lambda i: (0, i)),
        ],
        out_specs=(
            line,
            line,
            all_of(fields, tile_rows, tile_cols),
            all_of(*rim),
            all_of(*rim),
        ),
        scratch_shapes=[
            pltpu.VMEM((fields * tile_rows, window_cols), BF16),
            pltpu.VMEM((fields, tile_rows, window_cols), F32),
        ],
        compiler_params=pltpu.CompilerParams(vmem_limit_bytes=20 * MEBI),
        cost_estimate=cost(8 * fields * tile_rows * window_cols * nodes, 4000000),
        name="forcing",
    )(
        start,
        exchange_factor,
        atmosphere_inputs,
        other,
        corner_parallel,
        corner_longitude,
        corner_share,
        surface,
        thermal_anomaly,
    )
    below = lax.ppermute(up_rim, "lon", upward)
    above = lax.ppermute(down_rim, "lon", downward)

    updated_warmth, temp_grad = pl.pallas_call(
        lateral_kernel,
        out_shape=(
            jax.ShapeDtypeStruct((layers, nodes), F32),
            jax.ShapeDtypeStruct((layers, nodes), F32),
        ),
        in_specs=whole(18),
        out_specs=tuple(whole(2)),
        scratch_shapes=[
            pltpu.VMEM((layers, nodes), F32),
            pltpu.VMEM(dense, F32),
            pltpu.VMEM((4, SLOT_ROWS, NODE_TILE), BF16),
            pltpu.VMEM((4, SLOT_ROWS, NODE_TILE), BF16),
            pltpu.VMEM((2 * layers, NODE_TILE), F32),
            pltpu.VMEM((2 * layers, NODE_TILE), F32),
            pltpu.VMEM((NODE_TILE, nodes), BF16),
            pltpu.VMEM((NODE_TILE, nodes), BF16),
            pltpu.SMEM((nodes // NODE_TILE,), jnp.int32),
        ],
        compiler_params=pltpu.CompilerParams(vmem_limit_bytes=32 * MEBI),
        cost_estimate=cost(8 * layers * nodes * extended, 8000000),
        name="lateral",
    )(
        adjacency,
        merged,
        rank,
        low,
        high,
        node_scale,
        keep,
        thermal_anomaly,
        ext,
        scaled,
        begun_grad,
        begun_rhs,
        back,
        column,
        flux,
        corr,
        mix3,
        scale,
    )

    forcing_grad = pl.pallas_call(
        join_kernel,
        out_shape=jax.ShapeDtypeStruct((fields, tile_rows, tile_cols), F32),
        in_specs=whole(3),
        out_specs=pl.BlockSpec(memory_space=pltpu.VMEM),
        compiler_params=pltpu.CompilerParams(vmem_limit_bytes=8 * MEBI),
        cost_estimate=cost(fields * tile_rows * tile_cols, 2000000),
        name="join",
    )(own_forcing, below, above)
    return (updated_warmth, temp_grad, forcing_grad)


def solution(mesh):
    nodes = P(None, ("lat", "lon"))
    placed = (
        P(None, "lat", "lon"),
        nodes,
        nodes,
        nodes,
        nodes,
        P(("lat", "lon"), None),
        nodes,
        nodes,
        nodes,
        P(),
        nodes,
    )
    return jax.shard_map(
        per_device,
        mesh=mesh,
        in_specs=placed,
        out_specs=(nodes, nodes, P(None, "lat", "lon")),
        check_vma=False,
    )
```

```python
import functools

import jax
import jax.numpy as jnp
from jax import lax
from jax.experimental import pallas as pl
from jax.experimental.pallas import tpu as pltpu
from jax.sharding import PartitionSpec as P

F32 = jnp.float32
BF16 = jnp.bfloat16
MEBI = 1024 * 1024
LANES = 128
SLOT_ROWS = 256
NODE_TILE = 256
FORCE_TILE = 512
EARLY_PAIRS = 3
LANE_CONTRACT = (((1,), (1,)), ((), ()))
MESH = pl.DeviceIdType.MESH


def whole(count):
    return [pl.BlockSpec(memory_space=pltpu.VMEM)] * count


def halves(value):
    high = value.astype(BF16)
    return high, (value - high.astype(F32)).astype(BF16)


def spread_levels(source_ref, dense_ref):
    layers = dense_ref.shape[0]
    for level in range(0, layers, 8):
        dense_ref[level : level + 8] = source_ref[level : level + 8, :].reshape(
            (8,) + dense_ref.shape[1:]
        )


def sweep_up(x_ref, mix_ref, scale_ref, zero):
    layers = x_ref.shape[0]

    def up(step, x_next):
        level = layers - 1 - step
        x_here = x_ref[level] + (mix_ref[level] * scale_ref[level]) * x_next
        x_ref[level] = x_here
        return x_here

    lax.fori_loop(0, layers, up, zero, unroll=8)


def best_scale(values, count):
    trial = lax.broadcasted_iota(jnp.int32, (count, values[0].shape[1]), 0).astype(F32)
    trial = 1.0 + trial * (1.0 / count)
    inverse = 1.0 / trial
    miss = jnp.zeros_like(trial)
    for value in values:
        gap = (value * inverse).astype(BF16).astype(F32) * trial - value
        miss = miss + gap * gap
    least = jnp.min(miss, axis=0, keepdims=True)
    return jnp.max(jnp.where(miss == least, trial, 1.0), axis=0, keepdims=True)


def slot_weights(adj_ref, merged_ref, cols, first_row, rank_ref=None):
    row = lax.broadcasted_iota(jnp.int32, (SLOT_ROWS, NODE_TILE), 0).astype(F32).astype(BF16)
    local = adj_ref[:, cols] - first_row
    if rank_ref is not None:
        rank = rank_ref[: adj_ref.shape[0], cols]
        local = jnp.where(jnp.logical_and(rank >= 0.0, rank <= 1.0), local, -1)
    local = local.astype(F32).astype(BF16)
    share = merged_ref[:, cols].astype(BF16)
    weights = jnp.zeros((SLOT_ROWS, NODE_TILE), BF16)
    for k in range(adj_ref.shape[0]):
        weights = jnp.where(row == local[k : k + 1, :], share[k : k + 1, :], weights)
    return weights


def slot_ids(adj_ref):
    slots, nodes = adj_ref.shape
    at = lax.broadcasted_iota(jnp.int32, (8, nodes), 0)
    spare = lax.broadcasted_iota(jnp.int32, (8 - slots, nodes), 0) - (8 - slots)
    return jnp.concatenate([adj_ref[...], spare], 0), at


def merge_slots(adj_ref, coef_ref, merged_ref):
    slots, nodes = adj_ref.shape
    ids, _ = slot_ids(adj_ref)
    coef = jnp.concatenate([coef_ref[...], jnp.zeros((8 - slots, nodes), F32)], 0)
    merged = coef
    for shift in range(1, 8):
        equal = ids == pltpu.roll(ids, shift, 0)
        merged = merged + jnp.where(equal, pltpu.roll(coef, shift, 0), 0.0)
    merged_ref[...] = merged


def rank_slots(adj_ref, rank_ref, low_ref, high_ref):
    slots, nodes = adj_ref.shape
    ids, at = slot_ids(adj_ref)
    low = (ids & (SLOT_ROWS - 1)).astype(F32)
    high = (ids >> (SLOT_ROWS.bit_length() - 1)).astype(F32)
    repeat = jnp.zeros((8, nodes), F32)
    for shift in range(1, slots):
        equal = ids == pltpu.roll(ids, shift, 0)
        repeat = jnp.where(jnp.logical_and(equal, at >= shift), 1.0, repeat)
    rank = jnp.zeros((8, nodes), F32)
    for shift in range(1, slots):
        met = jnp.logical_and(low == pltpu.roll(low, shift, 0), at >= shift)
        rank = rank + jnp.where(met, 1.0 - pltpu.roll(repeat, shift, 0), 0.0)
    rank = jnp.where(jnp.logical_or(repeat > 0.0, at >= slots), -1.0, rank)
    place = jnp.zeros((8, nodes), F32)
    for shift in range(1, slots):
        second = jnp.logical_and(pltpu.roll(rank, shift, 0) == 1.0, at >= shift)
        place = place + jnp.where(second, 1.0, 0.0)
    rank_ref[...] = rank
    low_ref[:8, :] = jnp.where(rank == 0.0, low, -1.0)
    high_ref[:8, :] = high
    for j in range(slots // 2):
        here = jnp.logical_and(rank == 1.0, place == float(j))
        low_ref[8 + j : 9 + j, :] = jnp.max(jnp.where(here, low, -1.0), axis=0, keepdims=True)
        high_ref[8 + j : 9 + j, :] = jnp.max(jnp.where(here, high, -1.0), axis=0, keepdims=True)


def sent_column(sent_ref, column_ref):
    parts, each = sent_ref.shape
    padded = jnp.concatenate(
        [sent_ref[...].astype(F32), jnp.zeros((parts, LANES - each), F32)], 1
    ).T
    for part in range(parts):
        column_ref[part * each : (part + 1) * each, :] = jnp.broadcast_to(
            padded[:each, part : part + 1], (each, LANES)
        )


def chosen_rows(column_ref, first_node):
    local = (column_ref[...] - first_node).astype(BF16)
    lane = lax.broadcasted_iota(jnp.int32, local.shape, 1).astype(F32)
    zero = jnp.zeros(local.shape, BF16)
    one = jnp.ones(local.shape, BF16)
    pieces = [
        jnp.where(local == (lane + float(start)).astype(BF16), one, zero)
        for start in range(0, NODE_TILE, LANES)
    ]
    return jnp.concatenate(pieces, 1)


def key_writer(cols, tables, keys_ref):
    merged_ref, rank_ref, low_ref, high_ref = tables
    rank = rank_ref[:, cols]
    merged = merged_ref[:, cols]
    low = low_ref[:, cols].astype(BF16)
    high = high_ref[:, cols].astype(BF16)
    share = merged.astype(BF16)
    pairs = low.shape[0] - 8
    place = jnp.zeros((1, NODE_TILE), F32)
    seconds = [jnp.zeros((1, NODE_TILE), F32)] * pairs
    for k in range(1, 2 * pairs):
        here = rank[k : k + 1] == 1.0
        for j in range(pairs):
            mine = jnp.logical_and(here, place == float(j))
            seconds[j] = jnp.where(mine, merged[k : k + 1], seconds[j])
        place = place + jnp.where(here, 1.0, 0.0)
    seconds = [second.astype(BF16) for second in seconds]

    def write(first):
        row = lax.broadcasted_iota(jnp.int32, (16, NODE_TILE), 0).astype(F32).astype(BF16)
        row = row + float(first)
        none = jnp.full((16, NODE_TILE), -1.0, BF16)
        zero = jnp.zeros((16, NODE_TILE), BF16)
        key, val = none, zero
        for k in range(2 * pairs):
            mine = row == low[k : k + 1]
            key = jnp.where(mine, high[k : k + 1], key)
            val = jnp.where(mine, share[k : k + 1], val)
        keys_ref[0, first : first + 16, :] = key
        keys_ref[1, first : first + 16, :] = val
        key, val = none, zero
        for j in range(pairs):
            mine = row == low[8 + j : 9 + j]
            key = jnp.where(mine, high[8 + j : 9 + j], key)
            val = jnp.where(mine, seconds[j], val)
        keys_ref[2, first : first + 16, :] = key
        keys_ref[3, first : first + 16, :] = val

    return write


def block_weights(keys_ref, blocks):
    key0, val0, key1, val1 = (keys_ref[i] for i in range(4))
    found = []
    for block in blocks:
        weights = jnp.where(key0 == float(block), val0, jnp.zeros_like(val0))
        found.append(jnp.where(key1 == float(block), val1, weights))
    return found


def node_cols(tile):
    start = tile * NODE_TILE
    if not isinstance(start, int):
        start = pl.multiple_of(start, NODE_TILE)
    return pl.ds(start, NODE_TILE)


def apply_tiles(first, end, rows, tables, fields, scratch):
    ext_ref, scaled_ref, thermal_ref, keep_ref, node_scale_ref, rhs_ref, grad_ref = fields
    even_ref, odd_ref, even_sum_ref, odd_sum_ref, even_turned_ref, odd_turned_ref = scratch
    layers, nodes = thermal_ref.shape
    tiles = nodes // NODE_TILE

    def use(tile, keys_ref, next_keys_ref, sum_ref, turned_ref):
        cols = node_cols(tile)
        scaled = scaled_ref[:, cols]
        groups = SLOT_ROWS // 16
        done = 0
        blocks = rows // SLOT_ROWS
        for start in range(0, blocks, 2):
            now = range(start, min(start + 2, blocks))
            for block, weights in zip(now, block_weights(keys_ref, now)):
                here = slice(block * SLOT_ROWS, (block + 1) * SLOT_ROWS)
                part = jnp.dot(ext_ref[:, here], weights, preferred_element_type=F32)
                if block == 0:
                    sum_ref[...] = part
                else:
                    sum_ref[...] += part
                if block * SLOT_ROWS < nodes:
                    turned_ref[:, here] = weights.T
                    part = jnp.dot(scaled, turned_ref[:, here], preferred_element_type=F32)
                    grad_ref[:, here] += part[:layers] + part[layers:]
            if start == 0:
                write = key_writer(node_cols(jnp.minimum(tile + 1, tiles - 1)), tables, next_keys_ref)
            until = min(groups, -(-groups * now[-1] // (nodes // SLOT_ROWS - 1)))
            for group in range(done, until):
                write(group * 16)
            done = until
        rhs_ref[:, cols] = (
            thermal_ref[:, cols] * keep_ref[:, cols]
            + (sum_ref[:layers, :] + sum_ref[layers:, :]) * node_scale_ref[:, cols]
        )

    write = key_writer(node_cols(2 * first), tables, even_ref)
    for group in range(SLOT_ROWS // 16):
        write(group * 16)

    def pair(step, carry):
        use(2 * step, even_ref, odd_ref, even_sum_ref, even_turned_ref)
        use(2 * step + 1, odd_ref, even_ref, odd_sum_ref, odd_turned_ref)
        return carry

    lax.fori_loop(first, end, pair, 0)


def exchange_kernel(
    mix_hbm,
    sens_hbm,
    thermal_hbm,
    adj_hbm,
    coef_hbm,
    sent_hbm,
    atm_hbm,
    scaled_ref,
    grad_ref,
    rhs_ref,
    surface_ref,
    mix3_ref,
    scale_ref,
    merged_ref,
    rank_ref,
    low_ref,
    high_ref,
    node_scale_ref,
    ext_ref,
    back_ref,
    other_ref,
    keep_ref,
    adj_out_ref,
    column_ref,
    x_ref,
    depart_buf,
    received_buf,
    hgrad_buf,
    back_buf,
    right_buf,
    left_buf,
    from_left_buf,
    from_right_buf,
    send_sem,
    recv_sem,
    gsend_sem,
    grecv_sem,
    rim_sem,
    mix_ref,
    sens_ref,
    thermal_ref,
    adj_ref,
    coef_ref,
    sent_ref,
    atm_ref,
    load_sem,
    even_ref,
    odd_ref,
    even_sum_ref,
    odd_sum_ref,
    even_turned_ref,
    odd_turned_ref,
):
    load = {}
    sources = (
        ("adj", adj_hbm, adj_ref),
        ("coef", coef_hbm, coef_ref),
        ("mix", mix_hbm, mix_ref),
        ("sens", sens_hbm, sens_ref),
        ("atm", atm_hbm, atm_ref),
        ("sent", sent_hbm, sent_ref),
        ("thermal", thermal_hbm, thermal_ref),
    )
    for index, (name, source, target) in enumerate(sources):
        load[name] = pltpu.make_async_copy(source, target, load_sem.at[index])
        load[name].start()
    layers, nodes = mix_ref.shape
    slots = adj_ref.shape[0]
    parts, each = sent_ref.shape
    halo = parts * each
    fields, tile_rows, tile_cols = atm_ref.shape
    mid = tile_rows // 2
    me = lax.axis_index("lon")
    ahead = lax.rem(me + 1, parts)
    behind = lax.rem(me + parts - 1, parts)

    barrier = pltpu.get_barrier_semaphore()
    for off in range(1, parts):
        pl.semaphore_signal(
            barrier, inc=1, device_id={"lon": lax.rem(me + off, parts)}, device_id_type=MESH
        )

    load["adj"].wait()
    load["coef"].wait()
    merge_slots(adj_ref, coef_ref, merged_ref)

    def fit(step, carry):
        cols = pl.ds(pl.multiple_of(step * NODE_TILE, NODE_TILE), NODE_TILE)
        merged = [merged_ref[k : k + 1, cols] for k in range(slots)]
        scale = best_scale(merged, 32)
        node_scale_ref[:, cols] = scale
        merged_ref[:, cols] = merged_ref[:, cols] / scale
        return carry

    lax.fori_loop(0, nodes // NODE_TILE, fit, 0)

    zero = jnp.zeros(x_ref.shape[1:], F32)
    load["mix"].wait()
    load["sens"].wait()
    spread_levels(mix_ref, mix3_ref)
    spread_levels(sens_ref, x_ref)

    def down(level, state):
        mix_prev, gain_prev, d_prev = state
        mix = mix3_ref[level]
        scale = 1.0 / (1.0 + mix + mix_prev * (1.0 - gain_prev))
        gain = mix * scale
        carry = mix_prev * scale
        d_next = x_ref[level] * scale + carry * d_prev
        scale_ref[level] = scale
        x_ref[level] = d_next
        return mix, gain, d_next

    lax.fori_loop(0, layers, down, (zero, zero, zero), unroll=4)
    sweep_up(x_ref, mix3_ref, scale_ref, zero)
    keep = 1.0 - jnp.sum(coef_ref[...], axis=0, keepdims=True)
    keep_ref[...] = keep
    for level in range(0, layers, 16):
        flat = x_ref[level : level + 16].reshape(16, nodes)
        if level == 0:
            surface_ref[...] = flat[0:1]
        grad_ref[level : level + 16, :] = flat * keep
        high, low = halves(flat * node_scale_ref[...])
        scaled_ref[level : level + 16, :] = high
        scaled_ref[layers + level : layers + level + 16, :] = low

    load["atm"].wait()
    low_lane = lax.broadcasted_iota(jnp.int32, (mid, tile_cols), 1) < tile_cols // 2
    for f in range(fields):
        upper = atm_ref[f, :mid, :].astype(F32)
        lower = pltpu.roll(atm_ref[f, mid:, :].astype(F32), tile_cols // 2, 1)
        right_buf[f] = jnp.where(low_lane, lower, upper).astype(BF16)
        left_buf[f] = jnp.where(low_lane, upper, lower).astype(BF16)

    load["sent"].wait()
    load["thermal"].wait()
    sent_column(sent_ref, column_ref)
    depart = jnp.zeros((halo, 2 * layers), F32)
    tile = 1024

    def pick(step, total):
        cols = pl.ds(pl.multiple_of(step * tile, tile), tile)
        high, low = halves(thermal_ref[:, cols])
        ext = jnp.concatenate([high, low], 0)
        first = (step * tile).astype(F32)
        chosen = jnp.concatenate(
            [chosen_rows(column_ref, first + float(at)) for at in range(0, tile, NODE_TILE)], 1
        )
        return total + lax.dot_general(
            chosen, ext, LANE_CONTRACT, preferred_element_type=F32
        )

    depart = lax.fori_loop(0, nodes // tile, pick, depart)
    depart_buf[...] = depart.astype(BF16)

    pl.semaphore_wait(barrier, parts - 1)

    def rim_copy(source, target, index, to):
        return pltpu.make_async_remote_copy(
            src_ref=source,
            dst_ref=target,
            send_sem=rim_sem.at[index],
            recv_sem=rim_sem.at[2 + index],
            device_id={"lon": to},
            device_id_type=MESH,
        )

    rims = [
        rim_copy(right_buf, from_left_buf, 0, ahead),
        rim_copy(left_buf, from_right_buf, 1, behind),
    ]
    for copy in rims:
        copy.start()

    def rows_of(part):
        return pl.ds(pl.multiple_of(part * each, each), each)

    def halo_copies(source, target, sends, recvs):
        copies = []
        for off in range(1, parts):
            peer = lax.rem(me + off, parts)
            copies.append(
                pltpu.make_async_remote_copy(
                    src_ref=source.at[rows_of(peer)],
                    dst_ref=target.at[rows_of(me)],
                    send_sem=sends.at[off],
                    recv_sem=recvs.at[off],
                    device_id={"lon": peer},
                    device_id_type=MESH,
                )
            )
        return copies

    def own_copy(source, target, sem):
        return pltpu.make_async_copy(source.at[rows_of(me)], target.at[rows_of(me)], sem)

    there = halo_copies(depart_buf, received_buf, send_sem, recv_sem)
    for copy in there:
        copy.start()
    mine = own_copy(depart_buf, received_buf, send_sem.at[0])
    mine.start()

    for block in range(halo // SLOT_ROWS):

        def collect(step, total):
            cols = pl.ds(pl.multiple_of(step * NODE_TILE, NODE_TILE), NODE_TILE)
            weights = slot_weights(adj_ref, merged_ref, cols, nodes + block * SLOT_ROWS)
            return total + lax.dot_general(
                scaled_ref[:, cols], weights, LANE_CONTRACT, preferred_element_type=F32
            )

        total = lax.fori_loop(
            0, nodes // NODE_TILE, collect, jnp.zeros((2 * layers, SLOT_ROWS), F32)
        )
        high, low = halves(total[:layers] + total[layers:])
        both = jnp.concatenate([high.astype(F32), low.astype(F32)], 0)
        hgrad_buf[block * SLOT_ROWS : (block + 1) * SLOT_ROWS, :] = both.T.astype(BF16)

    home = halo_copies(hgrad_buf, back_buf, gsend_sem, grecv_sem)
    for copy in home:
        copy.start()
    mine_back = own_copy(hgrad_buf, back_buf, gsend_sem.at[0])
    mine_back.start()
    rank_slots(adj_ref, rank_ref, low_ref, high_ref)
    adj_out_ref[...] = adj_ref[...]

    high, low = halves(thermal_ref[...])
    ext_ref[:layers, :nodes] = high
    ext_ref[layers:, :nodes] = low
    early = nodes // NODE_TILE // 2 * EARLY_PAIRS // 8
    apply_tiles(
        0,
        early,
        nodes,
        (merged_ref, rank_ref, low_ref, high_ref),
        (ext_ref, scaled_ref, thermal_ref, keep_ref, node_scale_ref, rhs_ref, grad_ref),
        (even_ref, odd_ref, even_sum_ref, odd_sum_ref, even_turned_ref, odd_turned_ref),
    )

    mine.wait()
    for copy in there:
        copy.wait()
    ext_ref[:, nodes:] = received_buf[...].astype(F32).T.astype(BF16)
    for block in range(halo // SLOT_ROWS):
        first = nodes + block * SLOT_ROWS

        def arrive(tile, carry):
            cols = node_cols(tile)
            weights = slot_weights(adj_ref, merged_ref, cols, first, rank_ref)
            part = jnp.dot(
                ext_ref[:, first : first + SLOT_ROWS], weights, preferred_element_type=F32
            )
            rhs_ref[:, cols] += (part[:layers] + part[layers:]) * node_scale_ref[:, cols]
            return carry

        lax.fori_loop(0, 2 * early, arrive, 0)

    for copy in rims:
        copy.wait()
    for f in range(fields):
        right = from_right_buf[f].astype(F32)
        left = from_left_buf[f].astype(F32)
        other_ref[f, :mid, :] = jnp.where(low_lane, right, left).astype(BF16)
        other_ref[f, mid:, :] = pltpu.roll(
            jnp.where(low_lane, left, right), tile_cols // 2, 1
        ).astype(BF16)

    mine_back.wait()
    for copy in home:
        copy.wait()
    back_ref[...] = back_buf[...].astype(F32).T.astype(BF16)


def forcing_kernel(
    start_ref,
    factor_ref,
    atm_ref,
    other_ref,
    row_ref,
    col_ref,
    share_ref,
    surface_ref,
    thermal_ref,
    flux_ref,
    corr_ref,
    own_ref,
    up_ref,
    down_ref,
    window_ref,
    grad_ref,
):
    fields, tile_rows, window_cols = grad_ref.shape
    tile_cols = window_cols // 2
    mid = tile_rows // 2
    tile = row_ref.shape[1]

    @pl.when(pl.program_id(0) == 0)
    def _():
        grad_ref[...] = jnp.zeros_like(grad_ref)
        window_ref[:, :tile_cols] = atm_ref[...].reshape(fields * tile_rows, tile_cols)
        window_ref[:, tile_cols:] = other_ref[...].reshape(fields * tile_rows, tile_cols)

    share = share_ref[...]
    row_low = share[0:1] + share[2:3]
    row_high = share[1:2] + share[3:4]
    col_low = share[0:1] + share[1:2]
    col_high = share[2:3] + share[3:4]
    scale = best_scale([col_low, col_high], 64)
    col_low = col_low / scale
    col_high = col_high / scale
    base_row = row_ref[0:1, :]
    base_col = lax.rem(col_ref[0:1, :] + start_ref[0], window_cols)
    next_col = lax.rem(base_col + 1, window_cols)
    row_at = lax.broadcasted_iota(jnp.int32, (tile_rows, tile), 0)
    col_at = lax.broadcasted_iota(jnp.int32, (window_cols, tile), 0)
    rows = jnp.where(
        row_at == base_row, row_low, jnp.where(row_at == base_row + 1, row_high, 0.0)
    )
    col_is = col_at.astype(F32).astype(BF16)
    first_col, second_col = (value.astype(F32).astype(BF16) for value in (base_col, next_col))
    cols = jnp.where(
        col_is == first_col,
        col_low.astype(BF16),
        jnp.where(col_is == second_col, col_high.astype(BF16), jnp.zeros(col_is.shape, BF16)),
    )
    rows = rows * scale
    mixed = jnp.dot(window_ref[...], cols, preferred_element_type=F32)
    forced = [
        jnp.sum(mixed[f * tile_rows : (f + 1) * tile_rows] * rows, axis=0, keepdims=True)
        for f in range(fields)
    ]
    wind = jnp.sqrt(forced[0] * forced[0] + forced[1] * forced[1] + 1.0)
    excess = forced[2] - thermal_ref[0:1, :]
    flux = 0.1 * wind * excess
    for f in range(fields):
        flux = flux + factor_ref[f] * forced[f]
    flux_ref[...] = flux
    surface = surface_ref[...]
    corr_ref[...] = -0.1 * surface * wind
    quotient = surface * (0.1 * excess / wind)
    dot = functools.partial(
        lax.dot_general,
        dimension_numbers=LANE_CONTRACT,
        preferred_element_type=F32,
    )
    row_is = row_at.astype(F32).astype(BF16)
    base_is = base_row.astype(F32).astype(BF16)
    at_low = row_is == base_is
    at_high = row_is == base_is + 1.0
    none = jnp.zeros(row_is.shape, BF16)
    ends = [row_low * scale, row_high * scale]
    lefts = []
    for f in range(fields):
        node_grad = surface * factor_ref[f]
        if f < 2:
            node_grad = node_grad + quotient * forced[f]
        if f == 2:
            node_grad = node_grad + 0.1 * surface * wind
        below, above = (halves(node_grad * end) for end in ends)
        lefts.append(
            [
                jnp.where(at_low, low_end, jnp.where(at_high, high_end, none))
                for low_end, high_end in zip(below, above)
            ]
        )
    left_hi = jnp.concatenate([high for high, _ in lefts], 0)
    left_lo = jnp.concatenate([low for _, low in lefts], 0)
    grad = dot(left_hi, cols) + dot(left_lo, cols)
    grad_ref[...] += grad.reshape(fields, tile_rows, window_cols)

    @pl.when(pl.program_id(0) == pl.num_programs(0) - 1)
    def _():
        low_lane = lax.broadcasted_iota(jnp.int32, (mid, tile_cols), 1) < tile_cols // 2
        for f in range(fields):
            own_ref[f] = grad_ref[f, :, :tile_cols]
            upper = grad_ref[f, :mid, tile_cols:]
            lower = pltpu.roll(grad_ref[f, mid:, tile_cols:], tile_cols // 2, 1)
            up_ref[f] = jnp.where(low_lane, upper, lower)
            down_ref[f] = jnp.where(low_lane, lower, upper)


def lateral_kernel(
    adj_ref,
    merged_ref,
    rank_ref,
    low_ref,
    high_ref,
    node_scale_ref,
    keep_ref,
    thermal_ref,
    ext_ref,
    scaled_ref,
    begun_grad_ref,
    begun_rhs_ref,
    back_ref,
    column_ref,
    flux_ref,
    corr_ref,
    mix3_ref,
    scale_ref,
    warm_out_ref,
    grad_out_ref,
    rhs_ref,
    x_ref,
    even_ref,
    odd_ref,
    even_sum_ref,
    odd_sum_ref,
    even_turned_ref,
    odd_turned_ref,
    deep_ref,
    warm_ref,
    grad_ref,
    out_sem,
):
    slots, nodes = adj_ref.shape
    layers = rhs_ref.shape[0]
    tiles = nodes // NODE_TILE
    tables = merged_ref, rank_ref, low_ref, high_ref

    def deep_block(tile, bound):
        cols = node_cols(tile)
        high = (adj_ref[:, cols] >> (SLOT_ROWS.bit_length() - 1)).astype(F32)
        deep = jnp.logical_and(rank_ref[:slots, cols] > 1.0, high < bound)
        return jnp.max(jnp.where(deep, high, -1.0)).astype(jnp.int32)

    for tile in range(tiles):
        deep_ref[tile] = deep_block(tile, float(ext_ref.shape[1]))
    start_pair = tiles // 2 * EARLY_PAIRS // 8
    begun = start_pair * 2 * NODE_TILE
    rhs_ref[:, :begun] = begun_rhs_ref[:, :begun]
    grad_ref[...] = begun_grad_ref[...]
    fields_of_tile = (
        ext_ref, scaled_ref, thermal_ref, keep_ref, node_scale_ref, rhs_ref, grad_ref
    )
    scratch = even_ref, odd_ref, even_sum_ref, odd_sum_ref, even_turned_ref, odd_turned_ref

    def mend(tile):
        def one_block(block):
            cols = node_cols(tile)
            here = pl.ds(pl.multiple_of(block * SLOT_ROWS, SLOT_ROWS), SLOT_ROWS)
            local = jnp.where(
                rank_ref[:slots, cols] > 1.0, adj_ref[:, cols] - block * SLOT_ROWS, -1
            )
            local = local.astype(F32).astype(BF16)
            share = merged_ref[:slots, cols].astype(BF16)
            row = lax.broadcasted_iota(jnp.int32, (SLOT_ROWS, NODE_TILE), 0)
            row = row.astype(F32).astype(BF16)
            weights = jnp.zeros((SLOT_ROWS, NODE_TILE), BF16)
            for k in range(2, slots):
                weights = jnp.where(row == local[k : k + 1], share[k : k + 1], weights)
            part = jnp.dot(ext_ref[:, here], weights, preferred_element_type=F32)
            rhs_ref[:, cols] += (part[:layers] + part[layers:]) * node_scale_ref[:, cols]

            @pl.when(block * SLOT_ROWS < nodes)
            def _():
                part = lax.dot_general(
                    scaled_ref[:, cols], weights, LANE_CONTRACT, preferred_element_type=F32
                )
                grad_ref[:, here] += part[:layers] + part[layers:]

            return deep_block(tile, block.astype(F32))

        lax.while_loop(lambda block: block >= 0, one_block, deep_ref[tile])

    apply_tiles(start_pair, tiles // 2, ext_ref.shape[1], tables, fields_of_tile, scratch)

    def fix(tile, carry):
        mend(tile)
        return carry

    lax.fori_loop(0, tiles, fix, 0)

    width = 4 * NODE_TILE

    def give_back(step, carry):
        cols = pl.ds(pl.multiple_of(step * width, width), width)
        first = (step * width).astype(F32)
        chosen = jnp.concatenate(
            [chosen_rows(column_ref, first + float(at)) for at in range(0, width, NODE_TILE)], 1
        )
        part = jnp.dot(back_ref[...], chosen, preferred_element_type=F32)
        grad_ref[:, cols] += part[:layers] + part[layers:]
        return carry

    lax.fori_loop(0, nodes // width, give_back, 0)
    grad_ref[0:1, :] += corr_ref[...]
    copies = [pltpu.make_async_copy(grad_ref, grad_out_ref, out_sem.at[0])]
    copies[0].start()

    rhs_ref[0:1, :] += flux_ref[...]
    zero = jnp.zeros(x_ref.shape[1:], F32)
    spread_levels(rhs_ref, x_ref)

    def down(level, state):
        mix_prev, d_prev = state
        scale = scale_ref[level]
        d_next = x_ref[level] * scale + (mix_prev * scale) * d_prev
        x_ref[level] = d_next
        return mix3_ref[level], d_next

    lax.fori_loop(0, layers, down, (zero, zero), unroll=8)
    sweep_up(x_ref, mix3_ref, scale_ref, zero)
    for level in range(0, layers, 8):
        rows = slice(level, level + 8)
        warm_ref[rows, :] = x_ref[rows].reshape(8, nodes)
        copies.append(
            pltpu.make_async_copy(
                warm_ref.at[rows, :], warm_out_ref.at[rows, :], out_sem.at[1 + level // 8]
            )
        )
        copies[-1].start()
    for copy in copies:
        copy.wait()


def join_kernel(own_ref, below_ref, above_ref, out_ref):
    fields, tile_rows, tile_cols = own_ref.shape
    mid = tile_rows // 2
    low_lane = lax.broadcasted_iota(jnp.int32, (mid, tile_cols), 1) < tile_cols // 2
    for f in range(fields):
        below, above = below_ref[f], above_ref[f]
        out_ref[f, :mid, :] = own_ref[f, :mid, :] + jnp.where(low_lane, below, above)
        out_ref[f, mid:, :] = own_ref[f, mid:, :] + pltpu.roll(
            jnp.where(low_lane, above, below), tile_cols // 2, 1
        )


def cost(flops, moved):
    return pl.CostEstimate(flops=flops, bytes_accessed=moved, transcendentals=0)


def per_device(
    atmosphere_inputs,
    thermal_anomaly,
    mixing_rates,
    adjacency_table,
    lateral_spread_factor,
    sent_vertices,
    corner_parallel,
    corner_longitude,
    corner_share,
    exchange_factor,
    sensitivity_vector,
):
    layers, nodes = thermal_anomaly.shape
    fields, tile_rows, tile_cols = atmosphere_inputs.shape
    columns, each = sent_vertices.shape
    halo = columns * each
    slots = adjacency_table.shape[0]
    window_cols = 2 * tile_cols
    extended = nodes + halo
    upward = [(i, (i + 1) % columns) for i in range(columns)]
    downward = [((i + 1) % columns, i) for i in range(columns)]
    position = lax.axis_index("lon")
    start = ((columns - position) * tile_cols).astype(jnp.int32).reshape(1)

    dense = (layers, nodes // LANES, LANES)
    block = jax.ShapeDtypeStruct(dense, F32)
    rim = (fields, tile_rows // 2, tile_cols)
    (
        scaled,
        begun_grad,
        begun_rhs,
        surface,
        mix3,
        scale,
        merged,
        rank,
        low,
        high,
        node_scale,
        ext,
        back,
        other,
        keep,
        adjacency,
        column,
    ) = pl.pallas_call(
        exchange_kernel,
        out_shape=(
            jax.ShapeDtypeStruct((2 * layers, nodes), BF16),
            jax.ShapeDtypeStruct((layers, nodes), F32),
            jax.ShapeDtypeStruct((layers, nodes), F32),
            jax.ShapeDtypeStruct((1, nodes), F32),
            block,
            block,
            jax.ShapeDtypeStruct((8, nodes), F32),
            jax.ShapeDtypeStruct((8, nodes), F32),
            jax.ShapeDtypeStruct((8 + slots // 2, nodes), F32),
            jax.ShapeDtypeStruct((8 + slots // 2, nodes), F32),
            jax.ShapeDtypeStruct((1, nodes), F32),
            jax.ShapeDtypeStruct((2 * layers, extended), BF16),
            jax.ShapeDtypeStruct((2 * layers, halo), BF16),
            jax.ShapeDtypeStruct(atmosphere_inputs.shape, BF16),
            jax.ShapeDtypeStruct((1, nodes), F32),
            jax.ShapeDtypeStruct((slots, nodes), jnp.int32),
            jax.ShapeDtypeStruct((halo, LANES), F32),
        ),
        in_specs=[pl.BlockSpec(memory_space=pltpu.HBM)] * 7,
        out_specs=tuple(whole(17)),
        scratch_shapes=[
            pltpu.VMEM(dense, F32),
            pltpu.VMEM((halo, 2 * layers), BF16),
            pltpu.VMEM((halo, 2 * layers), BF16),
            pltpu.VMEM((halo, 2 * layers), BF16),
            pltpu.VMEM((halo, 2 * layers), BF16),
            pltpu.VMEM(rim, BF16),
            pltpu.VMEM(rim, BF16),
            pltpu.VMEM(rim, BF16),
            pltpu.VMEM(rim, BF16),
            pltpu.SemaphoreType.DMA((columns,)),
            pltpu.SemaphoreType.DMA((columns,)),
            pltpu.SemaphoreType.DMA((columns,)),
            pltpu.SemaphoreType.DMA((columns,)),
            pltpu.SemaphoreType.DMA((4,)),
            pltpu.VMEM((layers, nodes), F32),
            pltpu.VMEM((layers, nodes), F32),
            pltpu.VMEM((layers, nodes), F32),
            pltpu.VMEM((slots, nodes), jnp.int32),
            pltpu.VMEM((slots, nodes), F32),
            pltpu.VMEM(sent_vertices.shape, jnp.int32),
            pltpu.VMEM(atmosphere_inputs.shape, BF16),
            pltpu.SemaphoreType.DMA((7,)),
            pltpu.VMEM((4, SLOT_ROWS, NODE_TILE), BF16),
            pltpu.VMEM((4, SLOT_ROWS, NODE_TILE), BF16),
            pltpu.VMEM((2 * layers, NODE_TILE), F32),
            pltpu.VMEM((2 * layers, NODE_TILE), F32),
            pltpu.VMEM((NODE_TILE, nodes), BF16),
            pltpu.VMEM((NODE_TILE, nodes), BF16),
        ],
        compiler_params=pltpu.CompilerParams(
            vmem_limit_bytes=47 * MEBI, collective_id=0, has_side_effects=True
        ),
        cost_estimate=cost(layers * nodes * 20, layers * nodes * 24),
        name="exchange",
    )(
        mixing_rates,
        sensitivity_vector,
        thermal_anomaly,
        adjacency_table,
        lateral_spread_factor,
        sent_vertices,
        atmosphere_inputs,
    )

    line = pl.BlockSpec((1, FORCE_TILE), lambda i: (0, i))
    four = pl.BlockSpec((4, FORCE_TILE), lambda i: (0, i))

    def all_of(*shape):
        return pl.BlockSpec(shape, lambda i: (0,) * len(shape))

    flux, corr, own_forcing, up_rim, down_rim = pl.pallas_call(
        forcing_kernel,
        grid=(nodes // FORCE_TILE,),
        out_shape=(
            jax.ShapeDtypeStruct((1, nodes), F32),
            jax.ShapeDtypeStruct((1, nodes), F32),
            jax.ShapeDtypeStruct((fields, tile_rows, tile_cols), F32),
            jax.ShapeDtypeStruct(rim, F32),
            jax.ShapeDtypeStruct(rim, F32),
        ),
        in_specs=[
            pl.BlockSpec(memory_space=pltpu.SMEM),
            pl.BlockSpec(memory_space=pltpu.SMEM),
            all_of(fields, tile_rows, tile_cols),
            all_of(fields, tile_rows, tile_cols),
            four,
            four,
            four,
            line,
            pl.BlockSpec((8, FORCE_TILE), lambda i: (0, i)),
        ],
        out_specs=(
            line,
            line,
            all_of(fields, tile_rows, tile_cols),
            all_of(*rim),
            all_of(*rim),
        ),
        scratch_shapes=[
            pltpu.VMEM((fields * tile_rows, window_cols), BF16),
            pltpu.VMEM((fields, tile_rows, window_cols), F32),
        ],
        compiler_params=pltpu.CompilerParams(vmem_limit_bytes=20 * MEBI),
        cost_estimate=cost(8 * fields * tile_rows * window_cols * nodes, 4000000),
        name="forcing",
    )(
        start,
        exchange_factor,
        atmosphere_inputs,
        other,
        corner_parallel,
        corner_longitude,
        corner_share,
        surface,
        thermal_anomaly,
    )
    below = lax.ppermute(up_rim, "lon", upward)
    above = lax.ppermute(down_rim, "lon", downward)

    updated_warmth, temp_grad = pl.pallas_call(
        lateral_kernel,
        out_shape=(
            jax.ShapeDtypeStruct((layers, nodes), F32),
            jax.ShapeDtypeStruct((layers, nodes), F32),
        ),
        in_specs=whole(18),
        out_specs=(pl.BlockSpec(memory_space=pl.ANY),) * 2,
        scratch_shapes=[
            pltpu.VMEM((layers, nodes), F32),
            pltpu.VMEM(dense, F32),
            pltpu.VMEM((4, SLOT_ROWS, NODE_TILE), BF16),
            pltpu.VMEM((4, SLOT_ROWS, NODE_TILE), BF16),
            pltpu.VMEM((2 * layers, NODE_TILE), F32),
            pltpu.VMEM((2 * layers, NODE_TILE), F32),
            pltpu.VMEM((NODE_TILE, nodes), BF16),
            pltpu.VMEM((NODE_TILE, nodes), BF16),
            pltpu.SMEM((nodes // NODE_TILE,), jnp.int32),
            pltpu.VMEM((layers, nodes), F32),
            pltpu.VMEM((layers, nodes), F32),
            pltpu.SemaphoreType.DMA((1 + layers // 8,)),
        ],
        compiler_params=pltpu.CompilerParams(vmem_limit_bytes=32 * MEBI),
        cost_estimate=cost(8 * layers * nodes * extended, 8000000),
        name="lateral",
    )(
        adjacency,
        merged,
        rank,
        low,
        high,
        node_scale,
        keep,
        thermal_anomaly,
        ext,
        scaled,
        begun_grad,
        begun_rhs,
        back,
        column,
        flux,
        corr,
        mix3,
        scale,
    )

    forcing_grad = pl.pallas_call(
        join_kernel,
        out_shape=jax.ShapeDtypeStruct((fields, tile_rows, tile_cols), F32),
        in_specs=whole(3),
        out_specs=pl.BlockSpec(memory_space=pltpu.VMEM),
        compiler_params=pltpu.CompilerParams(vmem_limit_bytes=8 * MEBI),
        cost_estimate=cost(fields * tile_rows * tile_cols, 2000000),
        name="join",
    )(own_forcing, below, above)
    return (updated_warmth, temp_grad, forcing_grad)


def solution(mesh):
    nodes = P(None, ("lat", "lon"))
    placed = (
        P(None, "lat", "lon"),
        nodes,
        nodes,
        nodes,
        nodes,
        P(("lat", "lon"), None),
        nodes,
        nodes,
        nodes,
        P(),
        nodes,
    )
    return jax.shard_map(
        per_device,
        mesh=mesh,
        in_specs=placed,
        out_specs=(nodes, nodes, P(None, "lat", "lon")),
        check_vma=False,
    )
```

```python
import functools

import jax
import jax.numpy as jnp
from jax import lax
from jax.experimental import pallas as pl
from jax.experimental.pallas import tpu as pltpu
from jax.sharding import PartitionSpec as P

F32 = jnp.float32
BF16 = jnp.bfloat16
MEBI = 1024 * 1024
LANES = 128
SLOT_ROWS = 256
NODE_TILE = 256
FORCE_TILE = 512
EARLY_PAIRS = 4
LANE_CONTRACT = (((1,), (1,)), ((), ()))
MESH = pl.DeviceIdType.MESH


def whole(count):
    return [pl.BlockSpec(memory_space=pltpu.VMEM)] * count


def halves(value):
    high = value.astype(BF16)
    return high, (value - high.astype(F32)).astype(BF16)


def spread_levels(source_ref, dense_ref):
    layers = dense_ref.shape[0]
    for level in range(0, layers, 8):
        dense_ref[level : level + 8] = source_ref[level : level + 8, :].reshape(
            (8,) + dense_ref.shape[1:]
        )


def sweep_up(x_ref, mix_ref, scale_ref, zero):
    layers = x_ref.shape[0]

    def up(step, x_next):
        level = layers - 1 - step
        x_here = x_ref[level] + (mix_ref[level] * scale_ref[level]) * x_next
        x_ref[level] = x_here
        return x_here

    lax.fori_loop(0, layers, up, zero, unroll=8)


def best_scale(values, count):
    trial = lax.broadcasted_iota(jnp.int32, (count, values[0].shape[1]), 0).astype(F32)
    trial = 1.0 + trial * (1.0 / count)
    inverse = 1.0 / trial
    miss = jnp.zeros_like(trial)
    for value in values:
        gap = (value * inverse).astype(BF16).astype(F32) * trial - value
        miss = miss + gap * gap
    least = jnp.min(miss, axis=0, keepdims=True)
    return jnp.max(jnp.where(miss == least, trial, 1.0), axis=0, keepdims=True)


def slot_weights(adj_ref, merged_ref, cols, first_row, rank_ref=None):
    row = lax.broadcasted_iota(jnp.int32, (SLOT_ROWS, NODE_TILE), 0).astype(F32).astype(BF16)
    local = adj_ref[:, cols] - first_row
    if rank_ref is not None:
        rank = rank_ref[: adj_ref.shape[0], cols]
        local = jnp.where(jnp.logical_and(rank >= 0.0, rank <= 1.0), local, -1)
    local = local.astype(F32).astype(BF16)
    share = merged_ref[:, cols].astype(BF16)
    weights = jnp.zeros((SLOT_ROWS, NODE_TILE), BF16)
    for k in range(adj_ref.shape[0]):
        weights = jnp.where(row == local[k : k + 1, :], share[k : k + 1, :], weights)
    return weights


def slot_ids(adj_ref):
    slots, nodes = adj_ref.shape
    at = lax.broadcasted_iota(jnp.int32, (8, nodes), 0)
    spare = lax.broadcasted_iota(jnp.int32, (8 - slots, nodes), 0) - (8 - slots)
    return jnp.concatenate([adj_ref[...], spare], 0), at


def merge_slots(adj_ref, coef_ref, merged_ref):
    slots, nodes = adj_ref.shape
    ids, _ = slot_ids(adj_ref)
    coef = jnp.concatenate([coef_ref[...], jnp.zeros((8 - slots, nodes), F32)], 0)
    merged = coef
    for shift in range(1, 8):
        equal = ids == pltpu.roll(ids, shift, 0)
        merged = merged + jnp.where(equal, pltpu.roll(coef, shift, 0), 0.0)
    merged_ref[...] = merged


def rank_slots(adj_ref, rank_ref, low_ref, high_ref):
    slots, nodes = adj_ref.shape
    ids, at = slot_ids(adj_ref)
    low = (ids & (SLOT_ROWS - 1)).astype(F32)
    high = (ids >> (SLOT_ROWS.bit_length() - 1)).astype(F32)
    repeat = jnp.zeros((8, nodes), F32)
    for shift in range(1, slots):
        equal = ids == pltpu.roll(ids, shift, 0)
        repeat = jnp.where(jnp.logical_and(equal, at >= shift), 1.0, repeat)
    rank = jnp.zeros((8, nodes), F32)
    for shift in range(1, slots):
        met = jnp.logical_and(low == pltpu.roll(low, shift, 0), at >= shift)
        rank = rank + jnp.where(met, 1.0 - pltpu.roll(repeat, shift, 0), 0.0)
    rank = jnp.where(jnp.logical_or(repeat > 0.0, at >= slots), -1.0, rank)
    place = jnp.zeros((8, nodes), F32)
    for shift in range(1, slots):
        second = jnp.logical_and(pltpu.roll(rank, shift, 0) == 1.0, at >= shift)
        place = place + jnp.where(second, 1.0, 0.0)
    rank_ref[...] = rank
    low_ref[:8, :] = jnp.where(rank == 0.0, low, -1.0)
    high_ref[:8, :] = high
    for j in range(slots // 2):
        here = jnp.logical_and(rank == 1.0, place == float(j))
        low_ref[8 + j : 9 + j, :] = jnp.max(jnp.where(here, low, -1.0), axis=0, keepdims=True)
        high_ref[8 + j : 9 + j, :] = jnp.max(jnp.where(here, high, -1.0), axis=0, keepdims=True)


def sent_column(sent_ref, column_ref):
    parts, each = sent_ref.shape
    padded = jnp.concatenate(
        [sent_ref[...].astype(F32), jnp.zeros((parts, LANES - each), F32)], 1
    ).T
    for part in range(parts):
        column_ref[part * each : (part + 1) * each, :] = jnp.broadcast_to(
            padded[:each, part : part + 1], (each, LANES)
        )


def chosen_rows(column_ref, first_node):
    local = (column_ref[...] - first_node).astype(BF16)
    lane = lax.broadcasted_iota(jnp.int32, local.shape, 1).astype(F32)
    zero = jnp.zeros(local.shape, BF16)
    one = jnp.ones(local.shape, BF16)
    pieces = [
        jnp.where(local == (lane + float(start)).astype(BF16), one, zero)
        for start in range(0, NODE_TILE, LANES)
    ]
    return jnp.concatenate(pieces, 1)


def key_writer(cols, tables, keys_ref):
    merged_ref, rank_ref, low_ref, high_ref = tables
    rank = rank_ref[:, cols]
    merged = merged_ref[:, cols]
    low = low_ref[:, cols].astype(BF16)
    high = high_ref[:, cols].astype(BF16)
    share = merged.astype(BF16)
    pairs = low.shape[0] - 8
    place = jnp.zeros((1, NODE_TILE), F32)
    seconds = [jnp.zeros((1, NODE_TILE), F32)] * pairs
    for k in range(1, 2 * pairs):
        here = rank[k : k + 1] == 1.0
        for j in range(pairs):
            mine = jnp.logical_and(here, place == float(j))
            seconds[j] = jnp.where(mine, merged[k : k + 1], seconds[j])
        place = place + jnp.where(here, 1.0, 0.0)
    seconds = [second.astype(BF16) for second in seconds]

    def write(first):
        row = lax.broadcasted_iota(jnp.int32, (16, NODE_TILE), 0).astype(F32).astype(BF16)
        row = row + float(first)
        none = jnp.full((16, NODE_TILE), -1.0, BF16)
        zero = jnp.zeros((16, NODE_TILE), BF16)
        key, val = none, zero
        for k in range(2 * pairs):
            mine = row == low[k : k + 1]
            key = jnp.where(mine, high[k : k + 1], key)
            val = jnp.where(mine, share[k : k + 1], val)
        keys_ref[0, first : first + 16, :] = key
        keys_ref[1, first : first + 16, :] = val
        key, val = none, zero
        for j in range(pairs):
            mine = row == low[8 + j : 9 + j]
            key = jnp.where(mine, high[8 + j : 9 + j], key)
            val = jnp.where(mine, seconds[j], val)
        keys_ref[2, first : first + 16, :] = key
        keys_ref[3, first : first + 16, :] = val

    return write


def block_weights(keys_ref, blocks):
    key0, val0, key1, val1 = (keys_ref[i] for i in range(4))
    found = []
    for block in blocks:
        weights = jnp.where(key0 == float(block), val0, jnp.zeros_like(val0))
        found.append(jnp.where(key1 == float(block), val1, weights))
    return found


def node_cols(tile):
    start = tile * NODE_TILE
    if not isinstance(start, int):
        start = pl.multiple_of(start, NODE_TILE)
    return pl.ds(start, NODE_TILE)


def apply_tiles(first, end, rows, tables, fields, scratch):
    ext_ref, scaled_ref, thermal_ref, keep_ref, node_scale_ref, rhs_ref, grad_ref = fields
    even_ref, odd_ref, even_sum_ref, odd_sum_ref, even_turned_ref, odd_turned_ref = scratch
    layers, nodes = thermal_ref.shape
    tiles = nodes // NODE_TILE

    def use(tile, keys_ref, next_keys_ref, sum_ref, turned_ref):
        cols = node_cols(tile)
        scaled = scaled_ref[:, cols]
        groups = SLOT_ROWS // 16
        done = 0
        blocks = rows // SLOT_ROWS
        for start in range(0, blocks, 2):
            now = range(start, min(start + 2, blocks))
            for block, weights in zip(now, block_weights(keys_ref, now)):
                here = slice(block * SLOT_ROWS, (block + 1) * SLOT_ROWS)
                part = jnp.dot(ext_ref[:, here], weights, preferred_element_type=F32)
                if block == 0:
                    sum_ref[...] = part
                else:
                    sum_ref[...] += part
                if block * SLOT_ROWS < nodes:
                    turned_ref[:, here] = weights.T
                    part = jnp.dot(scaled, turned_ref[:, here], preferred_element_type=F32)
                    grad_ref[:, here] += part[:layers] + part[layers:]
            if start == 0:
                write = key_writer(node_cols(jnp.minimum(tile + 1, tiles - 1)), tables, next_keys_ref)
            until = min(groups, -(-groups * now[-1] // (nodes // SLOT_ROWS - 1)))
            for group in range(done, until):
                write(group * 16)
            done = until
        rhs_ref[:, cols] = (
            thermal_ref[:, cols] * keep_ref[:, cols]
            + (sum_ref[:layers, :] + sum_ref[layers:, :]) * node_scale_ref[:, cols]
        )

    write = key_writer(node_cols(2 * first), tables, even_ref)
    for group in range(SLOT_ROWS // 16):
        write(group * 16)

    def pair(step, carry):
        use(2 * step, even_ref, odd_ref, even_sum_ref, even_turned_ref)
        use(2 * step + 1, odd_ref, even_ref, odd_sum_ref, odd_turned_ref)
        return carry

    lax.fori_loop(first, end, pair, 0)


def exchange_kernel(
    mix_hbm,
    sens_hbm,
    thermal_hbm,
    adj_hbm,
    coef_hbm,
    sent_hbm,
    atm_hbm,
    scaled_ref,
    grad_ref,
    rhs_ref,
    surface_ref,
    mix3_ref,
    scale_ref,
    merged_ref,
    rank_ref,
    low_ref,
    high_ref,
    node_scale_ref,
    ext_ref,
    back_ref,
    other_ref,
    keep_ref,
    adj_out_ref,
    column_ref,
    x_ref,
    depart_buf,
    received_buf,
    hgrad_buf,
    back_buf,
    right_buf,
    left_buf,
    from_left_buf,
    from_right_buf,
    send_sem,
    recv_sem,
    gsend_sem,
    grecv_sem,
    rim_sem,
    mix_ref,
    sens_ref,
    thermal_ref,
    adj_ref,
    coef_ref,
    sent_ref,
    atm_ref,
    load_sem,
    even_ref,
    odd_ref,
    even_sum_ref,
    odd_sum_ref,
    even_turned_ref,
    odd_turned_ref,
):
    load = {}
    sources = (
        ("adj", adj_hbm, adj_ref),
        ("coef", coef_hbm, coef_ref),
        ("mix", mix_hbm, mix_ref),
        ("sens", sens_hbm, sens_ref),
        ("atm", atm_hbm, atm_ref),
        ("sent", sent_hbm, sent_ref),
        ("thermal", thermal_hbm, thermal_ref),
    )
    for index, (name, source, target) in enumerate(sources):
        load[name] = pltpu.make_async_copy(source, target, load_sem.at[index])
        load[name].start()
    layers, nodes = mix_ref.shape
    slots = adj_ref.shape[0]
    parts, each = sent_ref.shape
    halo = parts * each
    fields, tile_rows, tile_cols = atm_ref.shape
    mid = tile_rows // 2
    me = lax.axis_index("lon")
    ahead = lax.rem(me + 1, parts)
    behind = lax.rem(me + parts - 1, parts)

    barrier = pltpu.get_barrier_semaphore()
    for off in range(1, parts):
        pl.semaphore_signal(
            barrier, inc=1, device_id={"lon": lax.rem(me + off, parts)}, device_id_type=MESH
        )

    load["adj"].wait()
    load["coef"].wait()
    merge_slots(adj_ref, coef_ref, merged_ref)

    def fit(step, carry):
        cols = pl.ds(pl.multiple_of(step * NODE_TILE, NODE_TILE), NODE_TILE)
        merged = [merged_ref[k : k + 1, cols] for k in range(slots)]
        scale = best_scale(merged, 32)
        node_scale_ref[:, cols] = scale
        merged_ref[:, cols] = merged_ref[:, cols] / scale
        return carry

    lax.fori_loop(0, nodes // NODE_TILE, fit, 0)

    zero = jnp.zeros(x_ref.shape[1:], F32)
    load["mix"].wait()
    load["sens"].wait()
    spread_levels(mix_ref, mix3_ref)
    spread_levels(sens_ref, x_ref)

    def down(level, state):
        mix_prev, gain_prev, d_prev = state
        mix = mix3_ref[level]
        scale = 1.0 / (1.0 + mix + mix_prev * (1.0 - gain_prev))
        gain = mix * scale
        carry = mix_prev * scale
        d_next = x_ref[level] * scale + carry * d_prev
        scale_ref[level] = scale
        x_ref[level] = d_next
        return mix, gain, d_next

    lax.fori_loop(0, layers, down, (zero, zero, zero), unroll=4)
    sweep_up(x_ref, mix3_ref, scale_ref, zero)
    keep = 1.0 - jnp.sum(coef_ref[...], axis=0, keepdims=True)
    keep_ref[...] = keep
    for level in range(0, layers, 16):
        flat = x_ref[level : level + 16].reshape(16, nodes)
        if level == 0:
            surface_ref[...] = flat[0:1]
        grad_ref[level : level + 16, :] = flat * keep
        high, low = halves(flat * node_scale_ref[...])
        scaled_ref[level : level + 16, :] = high
        scaled_ref[layers + level : layers + level + 16, :] = low

    load["atm"].wait()
    low_lane = lax.broadcasted_iota(jnp.int32, (mid, tile_cols), 1) < tile_cols // 2
    for f in range(fields):
        upper = atm_ref[f, :mid, :].astype(F32)
        lower = pltpu.roll(atm_ref[f, mid:, :].astype(F32), tile_cols // 2, 1)
        right_buf[f] = jnp.where(low_lane, lower, upper).astype(BF16)
        left_buf[f] = jnp.where(low_lane, upper, lower).astype(BF16)

    load["sent"].wait()
    load["thermal"].wait()
    sent_column(sent_ref, column_ref)
    depart = jnp.zeros((halo, 2 * layers), F32)
    tile = 1024

    def pick(step, total):
        cols = pl.ds(pl.multiple_of(step * tile, tile), tile)
        high, low = halves(thermal_ref[:, cols])
        ext = jnp.concatenate([high, low], 0)
        first = (step * tile).astype(F32)
        chosen = jnp.concatenate(
            [chosen_rows(column_ref, first + float(at)) for at in range(0, tile, NODE_TILE)], 1
        )
        return total + lax.dot_general(
            chosen, ext, LANE_CONTRACT, preferred_element_type=F32
        )

    depart = lax.fori_loop(0, nodes // tile, pick, depart)
    depart_buf[...] = depart.astype(BF16)

    pl.semaphore_wait(barrier, parts - 1)

    def rim_copy(source, target, index, to):
        return pltpu.make_async_remote_copy(
            src_ref=source,
            dst_ref=target,
            send_sem=rim_sem.at[index],
            recv_sem=rim_sem.at[2 + index],
            device_id={"lon": to},
            device_id_type=MESH,
        )

    rims = [
        rim_copy(right_buf, from_left_buf, 0, ahead),
        rim_copy(left_buf, from_right_buf, 1, behind),
    ]
    for copy in rims:
        copy.start()

    def rows_of(part):
        return pl.ds(pl.multiple_of(part * each, each), each)

    def halo_copies(source, target, sends, recvs):
        copies = []
        for off in range(1, parts):
            peer = lax.rem(me + off, parts)
            copies.append(
                pltpu.make_async_remote_copy(
                    src_ref=source.at[rows_of(peer)],
                    dst_ref=target.at[rows_of(me)],
                    send_sem=sends.at[off],
                    recv_sem=recvs.at[off],
                    device_id={"lon": peer},
                    device_id_type=MESH,
                )
            )
        return copies

    def own_copy(source, target, sem):
        return pltpu.make_async_copy(source.at[rows_of(me)], target.at[rows_of(me)], sem)

    there = halo_copies(depart_buf, received_buf, send_sem, recv_sem)
    for copy in there:
        copy.start()
    mine = own_copy(depart_buf, received_buf, send_sem.at[0])
    mine.start()

    for block in range(halo // SLOT_ROWS):

        def collect(step, total):
            cols = pl.ds(pl.multiple_of(step * NODE_TILE, NODE_TILE), NODE_TILE)
            weights = slot_weights(adj_ref, merged_ref, cols, nodes + block * SLOT_ROWS)
            return total + lax.dot_general(
                scaled_ref[:, cols], weights, LANE_CONTRACT, preferred_element_type=F32
            )

        total = lax.fori_loop(
            0, nodes // NODE_TILE, collect, jnp.zeros((2 * layers, SLOT_ROWS), F32)
        )
        high, low = halves(total[:layers] + total[layers:])
        both = jnp.concatenate([high.astype(F32), low.astype(F32)], 0)
        hgrad_buf[block * SLOT_ROWS : (block + 1) * SLOT_ROWS, :] = both.T.astype(BF16)

    home = halo_copies(hgrad_buf, back_buf, gsend_sem, grecv_sem)
    for copy in home:
        copy.start()
    mine_back = own_copy(hgrad_buf, back_buf, gsend_sem.at[0])
    mine_back.start()
    rank_slots(adj_ref, rank_ref, low_ref, high_ref)
    adj_out_ref[...] = adj_ref[...]

    high, low = halves(thermal_ref[...])
    ext_ref[:layers, :nodes] = high
    ext_ref[layers:, :nodes] = low
    early = nodes // NODE_TILE // 2 * EARLY_PAIRS // 8
    apply_tiles(
        0,
        early,
        nodes,
        (merged_ref, rank_ref, low_ref, high_ref),
        (ext_ref, scaled_ref, thermal_ref, keep_ref, node_scale_ref, rhs_ref, grad_ref),
        (even_ref, odd_ref, even_sum_ref, odd_sum_ref, even_turned_ref, odd_turned_ref),
    )

    mine.wait()
    for copy in there:
        copy.wait()
    ext_ref[:, nodes:] = received_buf[...].astype(F32).T.astype(BF16)
    for block in range(halo // SLOT_ROWS):
        first = nodes + block * SLOT_ROWS

        def arrive(tile, carry):
            cols = node_cols(tile)
            weights = slot_weights(adj_ref, merged_ref, cols, first, rank_ref)
            part = jnp.dot(
                ext_ref[:, first : first + SLOT_ROWS], weights, preferred_element_type=F32
            )
            rhs_ref[:, cols] += (part[:layers] + part[layers:]) * node_scale_ref[:, cols]
            return carry

        lax.fori_loop(0, 2 * early, arrive, 0)

    for copy in rims:
        copy.wait()
    for f in range(fields):
        right = from_right_buf[f].astype(F32)
        left = from_left_buf[f].astype(F32)
        other_ref[f, :mid, :] = jnp.where(low_lane, right, left).astype(BF16)
        other_ref[f, mid:, :] = pltpu.roll(
            jnp.where(low_lane, left, right), tile_cols // 2, 1
        ).astype(BF16)

    mine_back.wait()
    for copy in home:
        copy.wait()
    back_ref[...] = back_buf[...].astype(F32).T.astype(BF16)


def forcing_kernel(
    start_ref,
    factor_ref,
    atm_ref,
    other_ref,
    row_ref,
    col_ref,
    share_ref,
    surface_ref,
    thermal_ref,
    flux_ref,
    corr_ref,
    own_ref,
    up_ref,
    down_ref,
    window_ref,
    grad_ref,
):
    fields, tile_rows, window_cols = grad_ref.shape
    tile_cols = window_cols // 2
    mid = tile_rows // 2
    tile = row_ref.shape[1]

    @pl.when(pl.program_id(0) == 0)
    def _():
        grad_ref[...] = jnp.zeros_like(grad_ref)
        window_ref[:, :tile_cols] = atm_ref[...].reshape(fields * tile_rows, tile_cols)
        window_ref[:, tile_cols:] = other_ref[...].reshape(fields * tile_rows, tile_cols)

    share = share_ref[...]
    row_low = share[0:1] + share[2:3]
    row_high = share[1:2] + share[3:4]
    col_low = share[0:1] + share[1:2]
    col_high = share[2:3] + share[3:4]
    scale = best_scale([col_low, col_high], 64)
    col_low = col_low / scale
    col_high = col_high / scale
    base_row = row_ref[0:1, :]
    base_col = lax.rem(col_ref[0:1, :] + start_ref[0], window_cols)
    next_col = lax.rem(base_col + 1, window_cols)
    row_at = lax.broadcasted_iota(jnp.int32, (tile_rows, tile), 0)
    col_at = lax.broadcasted_iota(jnp.int32, (window_cols, tile), 0)
    rows = jnp.where(
        row_at == base_row, row_low, jnp.where(row_at == base_row + 1, row_high, 0.0)
    )
    col_is = col_at.astype(F32).astype(BF16)
    first_col, second_col = (value.astype(F32).astype(BF16) for value in (base_col, next_col))
    cols = jnp.where(
        col_is == first_col,
        col_low.astype(BF16),
        jnp.where(col_is == second_col, col_high.astype(BF16), jnp.zeros(col_is.shape, BF16)),
    )
    rows = rows * scale
    mixed = jnp.dot(window_ref[...], cols, preferred_element_type=F32)
    forced = [
        jnp.sum(mixed[f * tile_rows : (f + 1) * tile_rows] * rows, axis=0, keepdims=True)
        for f in range(fields)
    ]
    wind = jnp.sqrt(forced[0] * forced[0] + forced[1] * forced[1] + 1.0)
    excess = forced[2] - thermal_ref[0:1, :]
    flux = 0.1 * wind * excess
    for f in range(fields):
        flux = flux + factor_ref[f] * forced[f]
    flux_ref[...] = flux
    surface = surface_ref[...]
    corr_ref[...] = -0.1 * surface * wind
    quotient = surface * (0.1 * excess / wind)
    dot = functools.partial(
        lax.dot_general,
        dimension_numbers=LANE_CONTRACT,
        preferred_element_type=F32,
    )
    row_is = row_at.astype(F32).astype(BF16)
    base_is = base_row.astype(F32).astype(BF16)
    at_low = row_is == base_is
    at_high = row_is == base_is + 1.0
    none = jnp.zeros(row_is.shape, BF16)
    ends = [row_low * scale, row_high * scale]
    lefts = []
    for f in range(fields):
        node_grad = surface * factor_ref[f]
        if f < 2:
            node_grad = node_grad + quotient * forced[f]
        if f == 2:
            node_grad = node_grad + 0.1 * surface * wind
        below, above = (halves(node_grad * end) for end in ends)
        lefts.append(
            [
                jnp.where(at_low, low_end, jnp.where(at_high, high_end, none))
                for low_end, high_end in zip(below, above)
            ]
        )
    left_hi = jnp.concatenate([high for high, _ in lefts], 0)
    left_lo = jnp.concatenate([low for _, low in lefts], 0)
    grad = dot(left_hi, cols) + dot(left_lo, cols)
    grad_ref[...] += grad.reshape(fields, tile_rows, window_cols)

    @pl.when(pl.program_id(0) == pl.num_programs(0) - 1)
    def _():
        low_lane = lax.broadcasted_iota(jnp.int32, (mid, tile_cols), 1) < tile_cols // 2
        for f in range(fields):
            own_ref[f] = grad_ref[f, :, :tile_cols]
            upper = grad_ref[f, :mid, tile_cols:]
            lower = pltpu.roll(grad_ref[f, mid:, tile_cols:], tile_cols // 2, 1)
            up_ref[f] = jnp.where(low_lane, upper, lower)
            down_ref[f] = jnp.where(low_lane, lower, upper)


def lateral_kernel(
    adj_ref,
    merged_ref,
    rank_ref,
    low_ref,
    high_ref,
    node_scale_ref,
    keep_ref,
    thermal_ref,
    ext_ref,
    scaled_ref,
    begun_grad_ref,
    begun_rhs_ref,
    back_ref,
    column_ref,
    flux_ref,
    corr_ref,
    mix3_ref,
    scale_ref,
    warm_out_ref,
    grad_out_ref,
    rhs_ref,
    x_ref,
    even_ref,
    odd_ref,
    even_sum_ref,
    odd_sum_ref,
    even_turned_ref,
    odd_turned_ref,
    deep_ref,
    warm_ref,
    grad_ref,
    out_sem,
):
    slots, nodes = adj_ref.shape
    layers = rhs_ref.shape[0]
    tiles = nodes // NODE_TILE
    tables = merged_ref, rank_ref, low_ref, high_ref

    def deep_block(tile, bound):
        cols = node_cols(tile)
        high = (adj_ref[:, cols] >> (SLOT_ROWS.bit_length() - 1)).astype(F32)
        deep = jnp.logical_and(rank_ref[:slots, cols] > 1.0, high < bound)
        return jnp.max(jnp.where(deep, high, -1.0)).astype(jnp.int32)

    for tile in range(tiles):
        deep_ref[tile] = deep_block(tile, float(ext_ref.shape[1]))
    start_pair = tiles // 2 * EARLY_PAIRS // 8
    begun = start_pair * 2 * NODE_TILE
    rhs_ref[:, :begun] = begun_rhs_ref[:, :begun]
    grad_ref[...] = begun_grad_ref[...]
    fields_of_tile = (
        ext_ref, scaled_ref, thermal_ref, keep_ref, node_scale_ref, rhs_ref, grad_ref
    )
    scratch = even_ref, odd_ref, even_sum_ref, odd_sum_ref, even_turned_ref, odd_turned_ref

    def mend(tile):
        def one_block(block):
            cols = node_cols(tile)
            here = pl.ds(pl.multiple_of(block * SLOT_ROWS, SLOT_ROWS), SLOT_ROWS)
            local = jnp.where(
                rank_ref[:slots, cols] > 1.0, adj_ref[:, cols] - block * SLOT_ROWS, -1
            )
            local = local.astype(F32).astype(BF16)
            share = merged_ref[:slots, cols].astype(BF16)
            row = lax.broadcasted_iota(jnp.int32, (SLOT_ROWS, NODE_TILE), 0)
            row = row.astype(F32).astype(BF16)
            weights = jnp.zeros((SLOT_ROWS, NODE_TILE), BF16)
            for k in range(2, slots):
                weights = jnp.where(row == local[k : k + 1], share[k : k + 1], weights)
            part = jnp.dot(ext_ref[:, here], weights, preferred_element_type=F32)
            rhs_ref[:, cols] += (part[:layers] + part[layers:]) * node_scale_ref[:, cols]

            @pl.when(block * SLOT_ROWS < nodes)
            def _():
                part = lax.dot_general(
                    scaled_ref[:, cols], weights, LANE_CONTRACT, preferred_element_type=F32
                )
                grad_ref[:, here] += part[:layers] + part[layers:]

            return deep_block(tile, block.astype(F32))

        lax.while_loop(lambda block: block >= 0, one_block, deep_ref[tile])

    apply_tiles(start_pair, tiles // 2, ext_ref.shape[1], tables, fields_of_tile, scratch)

    def fix(tile, carry):
        mend(tile)
        return carry

    lax.fori_loop(0, tiles, fix, 0)

    width = 4 * NODE_TILE

    def give_back(step, carry):
        cols = pl.ds(pl.multiple_of(step * width, width), width)
        first = (step * width).astype(F32)
        chosen = jnp.concatenate(
            [chosen_rows(column_ref, first + float(at)) for at in range(0, width, NODE_TILE)], 1
        )
        part = jnp.dot(back_ref[...], chosen, preferred_element_type=F32)
        grad_ref[:, cols] += part[:layers] + part[layers:]
        return carry

    lax.fori_loop(0, nodes // width, give_back, 0)
    grad_ref[0:1, :] += corr_ref[...]
    copies = [pltpu.make_async_copy(grad_ref, grad_out_ref, out_sem.at[0])]
    copies[0].start()

    rhs_ref[0:1, :] += flux_ref[...]
    zero = jnp.zeros(x_ref.shape[1:], F32)
    spread_levels(rhs_ref, x_ref)

    def down(level, state):
        mix_prev, d_prev = state
        scale = scale_ref[level]
        d_next = x_ref[level] * scale + (mix_prev * scale) * d_prev
        x_ref[level] = d_next
        return mix3_ref[level], d_next

    lax.fori_loop(0, layers, down, (zero, zero), unroll=8)
    sweep_up(x_ref, mix3_ref, scale_ref, zero)
    for level in range(0, layers, 8):
        rows = slice(level, level + 8)
        warm_ref[rows, :] = x_ref[rows].reshape(8, nodes)
        copies.append(
            pltpu.make_async_copy(
                warm_ref.at[rows, :], warm_out_ref.at[rows, :], out_sem.at[1 + level // 8]
            )
        )
        copies[-1].start()
    for copy in copies:
        copy.wait()


def join_kernel(own_ref, below_ref, above_ref, out_ref):
    fields, tile_rows, tile_cols = own_ref.shape
    mid = tile_rows // 2
    low_lane = lax.broadcasted_iota(jnp.int32, (mid, tile_cols), 1) < tile_cols // 2
    for f in range(fields):
        below, above = below_ref[f], above_ref[f]
        out_ref[f, :mid, :] = own_ref[f, :mid, :] + jnp.where(low_lane, below, above)
        out_ref[f, mid:, :] = own_ref[f, mid:, :] + pltpu.roll(
            jnp.where(low_lane, above, below), tile_cols // 2, 1
        )


def cost(flops, moved):
    return pl.CostEstimate(flops=flops, bytes_accessed=moved, transcendentals=0)


def per_device(
    atmosphere_inputs,
    thermal_anomaly,
    mixing_rates,
    adjacency_table,
    lateral_spread_factor,
    sent_vertices,
    corner_parallel,
    corner_longitude,
    corner_share,
    exchange_factor,
    sensitivity_vector,
):
    layers, nodes = thermal_anomaly.shape
    fields, tile_rows, tile_cols = atmosphere_inputs.shape
    columns, each = sent_vertices.shape
    halo = columns * each
    slots = adjacency_table.shape[0]
    window_cols = 2 * tile_cols
    extended = nodes + halo
    upward = [(i, (i + 1) % columns) for i in range(columns)]
    downward = [((i + 1) % columns, i) for i in range(columns)]
    position = lax.axis_index("lon")
    start = ((columns - position) * tile_cols).astype(jnp.int32).reshape(1)

    dense = (layers, nodes // LANES, LANES)
    block = jax.ShapeDtypeStruct(dense, F32)
    rim = (fields, tile_rows // 2, tile_cols)
    (
        scaled,
        begun_grad,
        begun_rhs,
        surface,
        mix3,
        scale,
        merged,
        rank,
        low,
        high,
        node_scale,
        ext,
        back,
        other,
        keep,
        adjacency,
        column,
    ) = pl.pallas_call(
        exchange_kernel,
        out_shape=(
            jax.ShapeDtypeStruct((2 * layers, nodes), BF16),
            jax.ShapeDtypeStruct((layers, nodes), F32),
            jax.ShapeDtypeStruct((layers, nodes), F32),
            jax.ShapeDtypeStruct((1, nodes), F32),
            block,
            block,
            jax.ShapeDtypeStruct((8, nodes), F32),
            jax.ShapeDtypeStruct((8, nodes), F32),
            jax.ShapeDtypeStruct((8 + slots // 2, nodes), F32),
            jax.ShapeDtypeStruct((8 + slots // 2, nodes), F32),
            jax.ShapeDtypeStruct((1, nodes), F32),
            jax.ShapeDtypeStruct((2 * layers, extended), BF16),
            jax.ShapeDtypeStruct((2 * layers, halo), BF16),
            jax.ShapeDtypeStruct(atmosphere_inputs.shape, BF16),
            jax.ShapeDtypeStruct((1, nodes), F32),
            jax.ShapeDtypeStruct((slots, nodes), jnp.int32),
            jax.ShapeDtypeStruct((halo, LANES), F32),
        ),
        in_specs=[pl.BlockSpec(memory_space=pltpu.HBM)] * 7,
        out_specs=tuple(whole(17)),
        scratch_shapes=[
            pltpu.VMEM(dense, F32),
            pltpu.VMEM((halo, 2 * layers), BF16),
            pltpu.VMEM((halo, 2 * layers), BF16),
            pltpu.VMEM((halo, 2 * layers), BF16),
            pltpu.VMEM((halo, 2 * layers), BF16),
            pltpu.VMEM(rim, BF16),
            pltpu.VMEM(rim, BF16),
            pltpu.VMEM(rim, BF16),
            pltpu.VMEM(rim, BF16),
            pltpu.SemaphoreType.DMA((columns,)),
            pltpu.SemaphoreType.DMA((columns,)),
            pltpu.SemaphoreType.DMA((columns,)),
            pltpu.SemaphoreType.DMA((columns,)),
            pltpu.SemaphoreType.DMA((4,)),
            pltpu.VMEM((layers, nodes), F32),
            pltpu.VMEM((layers, nodes), F32),
            pltpu.VMEM((layers, nodes), F32),
            pltpu.VMEM((slots, nodes), jnp.int32),
            pltpu.VMEM((slots, nodes), F32),
            pltpu.VMEM(sent_vertices.shape, jnp.int32),
            pltpu.VMEM(atmosphere_inputs.shape, BF16),
            pltpu.SemaphoreType.DMA((7,)),
            pltpu.VMEM((4, SLOT_ROWS, NODE_TILE), BF16),
            pltpu.VMEM((4, SLOT_ROWS, NODE_TILE), BF16),
            pltpu.VMEM((2 * layers, NODE_TILE), F32),
            pltpu.VMEM((2 * layers, NODE_TILE), F32),
            pltpu.VMEM((NODE_TILE, nodes), BF16),
            pltpu.VMEM((NODE_TILE, nodes), BF16),
        ],
        compiler_params=pltpu.CompilerParams(
            vmem_limit_bytes=47 * MEBI, collective_id=0, has_side_effects=True
        ),
        cost_estimate=cost(layers * nodes * 20, layers * nodes * 24),
        name="exchange",
    )(
        mixing_rates,
        sensitivity_vector,
        thermal_anomaly,
        adjacency_table,
        lateral_spread_factor,
        sent_vertices,
        atmosphere_inputs,
    )

    line = pl.BlockSpec((1, FORCE_TILE), lambda i: (0, i))
    four = pl.BlockSpec((4, FORCE_TILE), lambda i: (0, i))

    def all_of(*shape):
        return pl.BlockSpec(shape, lambda i: (0,) * len(shape))

    flux, corr, own_forcing, up_rim, down_rim = pl.pallas_call(
        forcing_kernel,
        grid=(nodes // FORCE_TILE,),
        out_shape=(
            jax.ShapeDtypeStruct((1, nodes), F32),
            jax.ShapeDtypeStruct((1, nodes), F32),
            jax.ShapeDtypeStruct((fields, tile_rows, tile_cols), F32),
            jax.ShapeDtypeStruct(rim, F32),
            jax.ShapeDtypeStruct(rim, F32),
        ),
        in_specs=[
            pl.BlockSpec(memory_space=pltpu.SMEM),
            pl.BlockSpec(memory_space=pltpu.SMEM),
            all_of(fields, tile_rows, tile_cols),
            all_of(fields, tile_rows, tile_cols),
            four,
            four,
            four,
            line,
            pl.BlockSpec((8, FORCE_TILE), lambda i: (0, i)),
        ],
        out_specs=(
            line,
            line,
            all_of(fields, tile_rows, tile_cols),
            all_of(*rim),
            all_of(*rim),
        ),
        scratch_shapes=[
            pltpu.VMEM((fields * tile_rows, window_cols), BF16),
            pltpu.VMEM((fields, tile_rows, window_cols), F32),
        ],
        compiler_params=pltpu.CompilerParams(vmem_limit_bytes=20 * MEBI),
        cost_estimate=cost(8 * fields * tile_rows * window_cols * nodes, 4000000),
        name="forcing",
    )(
        start,
        exchange_factor,
        atmosphere_inputs,
        other,
        corner_parallel,
        corner_longitude,
        corner_share,
        surface,
        thermal_anomaly,
    )
    below = lax.ppermute(up_rim, "lon", upward)
    above = lax.ppermute(down_rim, "lon", downward)

    updated_warmth, temp_grad = pl.pallas_call(
        lateral_kernel,
        out_shape=(
            jax.ShapeDtypeStruct((layers, nodes), F32),
            jax.ShapeDtypeStruct((layers, nodes), F32),
        ),
        in_specs=whole(18),
        out_specs=(pl.BlockSpec(memory_space=pl.ANY),) * 2,
        scratch_shapes=[
            pltpu.VMEM((layers, nodes), F32),
            pltpu.VMEM(dense, F32),
            pltpu.VMEM((4, SLOT_ROWS, NODE_TILE), BF16),
            pltpu.VMEM((4, SLOT_ROWS, NODE_TILE), BF16),
            pltpu.VMEM((2 * layers, NODE_TILE), F32),
            pltpu.VMEM((2 * layers, NODE_TILE), F32),
            pltpu.VMEM((NODE_TILE, nodes), BF16),
            pltpu.VMEM((NODE_TILE, nodes), BF16),
            pltpu.SMEM((nodes // NODE_TILE,), jnp.int32),
            pltpu.VMEM((layers, nodes), F32),
            pltpu.VMEM((layers, nodes), F32),
            pltpu.SemaphoreType.DMA((1 + layers // 8,)),
        ],
        compiler_params=pltpu.CompilerParams(vmem_limit_bytes=32 * MEBI),
        cost_estimate=cost(8 * layers * nodes * extended, 8000000),
        name="lateral",
    )(
        adjacency,
        merged,
        rank,
        low,
        high,
        node_scale,
        keep,
        thermal_anomaly,
        ext,
        scaled,
        begun_grad,
        begun_rhs,
        back,
        column,
        flux,
        corr,
        mix3,
        scale,
    )

    forcing_grad = pl.pallas_call(
        join_kernel,
        out_shape=jax.ShapeDtypeStruct((fields, tile_rows, tile_cols), F32),
        in_specs=whole(3),
        out_specs=pl.BlockSpec(memory_space=pltpu.VMEM),
        compiler_params=pltpu.CompilerParams(vmem_limit_bytes=8 * MEBI),
        cost_estimate=cost(fields * tile_rows * tile_cols, 2000000),
        name="join",
    )(own_forcing, below, above)
    return (updated_warmth, temp_grad, forcing_grad)


def solution(mesh):
    nodes = P(None, ("lat", "lon"))
    placed = (
        P(None, "lat", "lon"),
        nodes,
        nodes,
        nodes,
        nodes,
        P(("lat", "lon"), None),
        nodes,
        nodes,
        nodes,
        P(),
        nodes,
    )
    return jax.shard_map(
        per_device,
        mesh=mesh,
        in_specs=placed,
        out_specs=(nodes, nodes, P(None, "lat", "lon")),
        check_vma=False,
    )
```
